32 devices in a mesh: seq: 8 (over z, y), tp: 4 (over x, core).
Axes of the slice: x: 2, y: 2, z: 4, core: 2. Of those that a mesh axis runs over, the one named last changes fastest.
Arguments:
- queries: bfloat16 [1024, 4096], P('seq', 'tp'), may hold values from -128 to 128
- keys: bfloat16 [1024, 4096], P('seq', 'tp'), may hold values from -6 to 6
- values: bfloat16 [1024, 4096], P('seq', 'tp'), may hold values from -18 to 18
- residual_in: bfloat16 [1024, 4096], P('seq', 'tp'), may hold values from -6 to 6
- norm_gain: float32 [4096], replicated, may hold values from 0.1 to 1.9
- routing: int32 [8, 1], replicated, may hold values from 0 to 3; in each aligned block of 8 rows (0 to 7, 8 to 15, ...) at most 4 rows name the same one
- gate_weight: bfloat16 [8, 4096, 512], P('seq', None, 'tp'), may hold values from -0.09375 to 0.09375
- up_weight: bfloat16 [8, 4096, 512], P('seq', None, 'tp'), may hold values from -0.09375 to 0.09375
- down_weight: bfloat16 [8, 512, 4096], P('seq', None, 'tp'), may hold values from -0.1875 to 0.1875
Outputs:
- mixed: bfloat16 [1024, 4096], P('seq', 'tp')
The draws below stay inside these ranges and needn't reach their ends.
Inputs may be any that keep to these rules, and one draw needn't show every extreme that they name: `routing`: every expert is named by some block; no expert by more than 4 blocks, and one by exactly 4.
All inputs are finite; a program needn't handle non-finite values.
Results may differ from the reference program's by a relative error of at most 0.006.
Values may be sent and summed in bfloat16 or wider, within the bound.
A program may use at most 64 MiB of HBM per device.

```python
import math
import jax
import jax.numpy as jnp
import numpy as np
from jax import lax

HEADS = 32
HEAD_DIM = 128
FF = 1024
BLOCK = 128
WINDOW = 512
D = 4096
TOKENS = 1024
NBLOCKS = 8
EXPERTS = 4
MOST = 4


def raw_keys(key):
    return jnp.clip(jax.random.normal(jax.random.fold_in(key, 11), (TOKENS, D), jnp.float32), -6.0, 6.0)


def draw_keys(key, part):
    base_keys = raw_keys(key)
    return base_keys.astype(jnp.bfloat16)


def draw_queries(key, part):
    drawn = jnp.clip(jax.random.normal(jax.random.fold_in(key, 12), (TOKENS, D), jnp.float32), -6.0, 6.0)
    return drawn.astype(jnp.bfloat16)


def shard_levels(own_key, dims, cuts, least, largest):
    level = 1.0
    for axis_at, blocks in cuts:
        heights = jax.random.uniform(jax.random.fold_in(jax.random.fold_in(own_key, 6), axis_at), (blocks,), jnp.float32, least / len(cuts), largest / len(cuts))
        level = level * jnp.repeat(jnp.exp(heights), dims[axis_at] // blocks).reshape((-1,) + (1,) * (len(dims) - 1 - axis_at))
    return level


def assign_block(stream_key, own, number, rows, count, top, bound, slope):
    sequence = jax.random.permutation(stream_key, count)
    packed, common = load_shares(count, rows * top, bound, slope, True), load_shares(count, rows * top, bound, slope, False)
    places = jnp.arange(count)

    def named(tallies, rotation):
        used = int((tallies > 0).sum())
        fixed = max(1, used // 4)
        moved = fixed + (places - fixed + rotation * (used - fixed)) % max(1, count - fixed)
        return jnp.zeros((count,), jnp.int32).at[sequence[jnp.where(places < fixed, places, moved)]].set(jnp.asarray(tallies, jnp.int32))

    tallies = jnp.where(number % 4 == 0, named(packed, number // 4), named(common, number - number // 4 - 1))
    mixed = jax.random.permutation(jax.random.fold_in(own, 3), count)
    source_of, receiver = mixed[0:count // 2 * 2:2], mixed[1:count // 2 * 2:2]
    margin = jnp.minimum(tallies[source_of] - 1, bound - tallies[receiver]) // 2
    margin = jnp.where((source_of == sequence[0]) | (receiver == sequence[0]) | (tallies[receiver] == 0), 0, jnp.maximum(margin, 0))
    moved = jax.random.randint(jax.random.fold_in(own, 4), (count // 2,), 0, 1 << 20) % (margin + 1)
    tallies = tallies.at[source_of].add(-moved).at[receiver].add(moved)
    labels = jnp.searchsorted(jnp.cumsum(tallies), jnp.arange(rows * top), side="right").astype(jnp.int32)
    listing = labels.reshape(top, rows).T
    listing = listing[jax.random.permutation(jax.random.fold_in(own, 1), rows)]
    rotation = jax.random.randint(jax.random.fold_in(own, 2), (rows, 1), 0, top)
    return jnp.take_along_axis(listing, (jnp.arange(top)[None, :] + rotation) % top, axis=1)


def load_shares(number_of, total, limit, lean, full):
    portions = [(1 << 20) // math.isqrt(grade ** lean) + 1 for grade in range(1, number_of + 1)]
    largest = limit if full else min(limit, max(-(-total // number_of), total * portions[0] // sum(portions)))
    least = 1 if total - largest >= number_of - 1 else 0
    holding, spare = [largest] + [least] * (number_of - 1), total - largest - least * (number_of - 1)
    while spare > 0:
        movable = [i for i in range(1, number_of) if holding[i] < largest] or [i for i in range(1, number_of) if holding[i] < limit]
        whole, left = sum([portions[i] for i in movable]), spare
        for i in movable:
            more = min(limit - holding[i], max(1, left * portions[i] // whole), spare)
            holding[i] = holding[i] + more
            spare = spare - more
    return np.array(holding)


def scatter_about(key, shape, deviation, most, shards=(), kind=jnp.bfloat16):
    factor_of = shard_levels(key, shape, shards, -0.22, 0.18) if shards else 1.0
    entries = jax.random.normal(key, shape, jnp.float32) * deviation * factor_of
    return jnp.minimum(jnp.maximum(entries, -most), most).astype(kind)


def setup_inputs(seed: int = 0) -> dict:
    arg_keys = jax.random.split(jax.random.key(seed), 10)
    queries = draw_queries(jax.random.fold_in(arg_keys[9], 71), 0)
    keys = draw_keys(jax.random.fold_in(arg_keys[9], 71), 0)
    values = scatter_about(arg_keys[2], (TOKENS, D), 3.0, 18.0, ((0, 8), (1, 4)))
    residual_in = scatter_about(arg_keys[3], (TOKENS, D), 1.0, 6.0, ((0, 8), (1, 4)))
    norm_gain = jnp.clip(1.0 + 0.18 * jax.random.normal(arg_keys[4], (D,), jnp.float32), 0.1, 1.9)
    routing_keys = jax.random.split(jax.random.fold_in(arg_keys[5], 1), NBLOCKS // NBLOCKS)
    routing_turns = jax.random.permutation(jax.random.fold_in(arg_keys[5], 3), NBLOCKS // NBLOCKS)
    routing = jax.vmap(lambda own, number: assign_block(jax.random.fold_in(arg_keys[5], 2), own, number, NBLOCKS, EXPERTS, 1, MOST, 2))(routing_keys, routing_turns).reshape((NBLOCKS, 1))
    gate_weight = scatter_about(arg_keys[6], (2 * EXPERTS, D, FF // 2), D ** -0.5, 0.09375, ((0, 8), (2, 4)))
    up_weight = scatter_about(arg_keys[7], (2 * EXPERTS, D, FF // 2), D ** -0.5, 0.09375, ((0, 8), (2, 4)))
    down_weight = scatter_about(arg_keys[8], (2 * EXPERTS, FF // 2, D), FF ** -0.5, 0.1875, ((0, 8), (2, 4)))
    return dict(queries=queries, keys=keys, values=values, residual_in=residual_in, norm_gain=norm_gain, routing=routing, gate_weight=gate_weight, up_weight=up_weight, down_weight=down_weight)


epsilon = 1e-05
masked_score = -1e+30

def attend_block(block_index, query_heads, key_padded, value_padded):
    begin_row = block_index * BLOCK
    query_block = lax.dynamic_slice_in_dim(query_heads, begin_row, BLOCK, 0).astype(jnp.float32)
    key_block = lax.dynamic_slice_in_dim(key_padded, begin_row, WINDOW + BLOCK, 0).astype(jnp.float32)
    value_block = lax.dynamic_slice_in_dim(value_padded, begin_row, WINDOW + BLOCK, 0).astype(jnp.float32)
    query_pos = begin_row + jnp.arange(BLOCK, dtype=jnp.int32)
    key_pos = begin_row - WINDOW + jnp.arange(WINDOW + BLOCK, dtype=jnp.int32)
    visible = (key_pos[None, :] >= 0) & (key_pos[None, :] <= query_pos[:, None]) & (key_pos[None, :] > query_pos[:, None] - WINDOW)
    scores = jnp.einsum('qhd,khd->hqk', query_block, key_block) * (1.0 / math.sqrt(HEAD_DIM))
    scores = jnp.where(visible[None], scores, masked_score)
    top_score = lax.optimization_barrier(jnp.max(scores, axis=2, keepdims=True))
    expo = jnp.exp(scores - top_score)
    weights_soft = (expo / lax.optimization_barrier(jnp.sum(expo, axis=2, keepdims=True))).astype(jnp.bfloat16)
    attended = jnp.einsum('hqk,khd->qhd', weights_soft.astype(jnp.float32), value_block)
    return attended.reshape(BLOCK, D)

def expert_block(stream_block, expert, norm_gain, gate_weight, up_weight, down_weight):
    stream_f32 = stream_block.astype(jnp.float32)
    mean_square = lax.optimization_barrier(jnp.mean(stream_f32 * stream_f32, axis=1, keepdims=True))
    normed = (stream_f32 * lax.rsqrt(mean_square + epsilon) * norm_gain).astype(jnp.bfloat16)
    summed = stream_f32
    for half_index in range(2):
        weight_row = (2 * expert + half_index).astype(jnp.int32)
        gate_rows = lax.dynamic_index_in_dim(gate_weight, weight_row, 0, keepdims=False)
        up_rows = lax.dynamic_index_in_dim(up_weight, weight_row, 0, keepdims=False)
        down_rows = lax.dynamic_index_in_dim(down_weight, weight_row, 0, keepdims=False)
        gate_val = jnp.dot(normed, gate_rows, preferred_element_type=jnp.float32)
        up_val = jnp.dot(normed, up_rows, preferred_element_type=jnp.float32)
        hidden = (jax.nn.silu(gate_val) * up_val).astype(jnp.bfloat16)
        branch = jnp.dot(hidden, down_rows, preferred_element_type=jnp.float32).astype(jnp.bfloat16)
        summed = summed + branch.astype(jnp.float32)
    return summed.astype(jnp.bfloat16)

def reference(queries, keys, values, residual_in, norm_gain, routing, gate_weight, up_weight, down_weight):
    query_heads = queries.reshape(TOKENS, HEADS, HEAD_DIM)
    zero_rows = jnp.zeros((WINDOW, D), keys.dtype)
    key_padded = jnp.concatenate([zero_rows, keys], axis=0).reshape(WINDOW + TOKENS, HEADS, HEAD_DIM)
    value_padded = jnp.concatenate([zero_rows, values], axis=0).reshape(WINDOW + TOKENS, HEADS, HEAD_DIM)
    attended = lax.map(lambda index: attend_block(index, query_heads, key_padded, value_padded), jnp.arange(NBLOCKS, dtype=jnp.int32))
    stream = (residual_in.reshape(NBLOCKS, BLOCK, D).astype(jnp.float32) + attended).astype(jnp.bfloat16)
    mixed = lax.map(lambda pair: expert_block(pair[0], pair[1], norm_gain, gate_weight, up_weight, down_weight), (stream, routing[:, 0]))
    return mixed.reshape(TOKENS, D)
```

```python
import contextlib
import math

import jax
import jax.numpy as jnp
from jax import lax
from jax.experimental import pallas as pl
from jax.experimental.pallas import tpu as pltpu
from jax.sharding import PartitionSpec as P

HEAD_DIM = 128
BLOCK = 128
WINDOW = 512


epsilon = 1e-05
masked_score = -1e30


def shifted(block, axis, distance):
    devices = range(lax.axis_size(axis))
    route = [(i - distance, i) for i in devices if i - distance in devices]
    return lax.ppermute(block, axis, route)


def local_general(
    queries, keys, values, residual_in, norm_gain, routing, gate_weight, up_weight, down_weight
):
    seq_count = lax.axis_size("seq")
    seq_place = lax.axis_index("seq")
    tok_rows = queries.shape[0]
    feat_width = queries.shape[1]
    head_count = feat_width // HEAD_DIM
    prior_count = (WINDOW - 1) // tok_rows + 1
    earlier_keys = []
    earlier_values = []
    for distance in range(1, prior_count + 1):
        moved_keys, moved_values = shifted((keys, values), "seq", distance)
        earlier_keys.insert(0, moved_keys)
        earlier_values.insert(0, moved_values)
    key_all = jnp.concatenate(earlier_keys + [keys], axis=0).reshape(-1, head_count, HEAD_DIM)
    value_all = jnp.concatenate(earlier_values + [values], axis=0).reshape(-1, head_count, HEAD_DIM)
    query_heads = queries.reshape(tok_rows, head_count, HEAD_DIM)
    query_pos = seq_place * tok_rows + jnp.arange(tok_rows, dtype=jnp.int32)
    key_pos = (
        seq_place * tok_rows
        - prior_count * tok_rows
        + jnp.arange((prior_count + 1) * tok_rows, dtype=jnp.int32)
    )
    visible = (
        (key_pos[None, :] >= 0)
        & (key_pos[None, :] <= query_pos[:, None])
        & (key_pos[None, :] > query_pos[:, None] - WINDOW)
    )
    scores = jnp.einsum(
        "qhd,khd->hqk", query_heads, key_all, preferred_element_type=jnp.float32
    ) * (1.0 / math.sqrt(HEAD_DIM))
    scores = jnp.where(visible[None], scores, masked_score)
    top_score = jnp.max(scores, axis=2, keepdims=True)
    expo = jnp.exp(scores - top_score)
    weights_soft = (expo / jnp.sum(expo, axis=2, keepdims=True)).astype(jnp.bfloat16)
    attended = jnp.einsum(
        "hqk,khd->qhd", weights_soft, value_all, preferred_element_type=jnp.float32
    ).reshape(tok_rows, feat_width)
    stream = (residual_in.astype(jnp.float32) + attended).astype(jnp.bfloat16)
    send_width = stream.shape[1]
    blocks_dev = tok_rows // BLOCK
    piece_rows = BLOCK // seq_count
    spread_in = stream.reshape(blocks_dev, seq_count, piece_rows, send_width)
    spread_out = lax.all_to_all(spread_in, "seq", split_axis=1, concat_axis=0, tiled=True)
    block_count = blocks_dev * seq_count
    spread_rows = spread_out.reshape(block_count, piece_rows, send_width)
    expert_ids = routing[:, 0]
    expert_count = seq_count // 2
    most_blocks = min(2 * block_count // expert_count, block_count - expert_count + 1)
    order_index = jnp.arange(block_count, dtype=jnp.int32)
    same_expert = expert_ids[None, :] == expert_ids[:, None]
    rank_of = jnp.sum(same_expert & (order_index[None, :] < order_index[:, None]), axis=1)
    expert_range = jnp.arange(expert_count, dtype=jnp.int32)
    slot_range = jnp.arange(most_blocks, dtype=jnp.int32)
    selector = (
        (expert_ids[None, None, :] == expert_range[:, None, None])
        & (rank_of[None, None, :] == slot_range[None, :, None])
    ).astype(jnp.bfloat16)
    picked = jnp.einsum(
        "erb,bqf->erqf", selector, spread_rows, preferred_element_type=jnp.float32
    ).astype(jnp.bfloat16)
    outgoing = jnp.broadcast_to(
        picked[:, None], (expert_count, 2, most_blocks, piece_rows, send_width)
    )
    outgoing = outgoing.reshape(seq_count, most_blocks, piece_rows, send_width)
    features_full = lax.all_gather(
        lax.all_to_all(outgoing, "seq", split_axis=0, concat_axis=0, tiled=True),
        "tp",
        axis=3,
        tiled=True,
    )
    source_count = features_full.shape[0]
    slot_count = features_full.shape[1]
    stream_f32 = features_full.astype(jnp.float32)
    mean_square = jnp.mean(stream_f32 * stream_f32, axis=3, keepdims=True)
    normed = (stream_f32 * lax.rsqrt(mean_square + epsilon) * norm_gain).astype(jnp.bfloat16)
    normed = normed.reshape(-1, normed.shape[3])
    gate_val = jnp.dot(normed, gate_weight[0], preferred_element_type=jnp.float32)
    up_val = jnp.dot(normed, up_weight[0], preferred_element_type=jnp.float32)
    hidden = (jax.nn.silu(gate_val) * up_val).astype(jnp.bfloat16)
    hidden_half = lax.all_gather(hidden, "tp", axis=1, tiled=True)
    partial_value = jnp.dot(hidden_half, down_weight[0], preferred_element_type=jnp.float32).astype(
        jnp.bfloat16
    )
    partial_value = partial_value.reshape(source_count, slot_count, piece_rows, feat_width)
    returned = lax.all_to_all(partial_value, "seq", split_axis=0, concat_axis=0, tiled=True)
    returned = returned.reshape(expert_count, 2, most_blocks, piece_rows * feat_width)
    combined = jnp.einsum("erb,epry->pby", selector, returned, preferred_element_type=jnp.float32)
    residual_rows = spread_rows
    residual_rows = residual_rows.reshape(block_count, piece_rows * feat_width).astype(jnp.float32)
    finished = (residual_rows + combined[0] + combined[1]).astype(jnp.bfloat16)
    finished = finished.reshape(seq_count, blocks_dev, piece_rows, feat_width)
    restored = lax.all_to_all(finished, "seq", split_axis=0, concat_axis=2, tiled=True)
    return restored.reshape(tok_rows, feat_width)


BF16 = jnp.bfloat16
F32 = jnp.float32
PLANES = 4
GROUPS = 2
SPAN = 2 * HEAD_DIM
STAY_HEAD = 3


def mark(name):
    return contextlib.nullcontext()


def remote(src, dst, send_sem, recv_sem, device):
    return pltpu.make_async_remote_copy(
        src_ref=src,
        dst_ref=dst,
        send_sem=send_sem,
        recv_sem=recv_sem,
        device_id=device,
        device_id_type=pl.DeviceIdType.MESH,
    )


def size_of(ref):
    return math.prod(ref.shape) * ref.dtype.itemsize


def layer_kernel(most, arguments, out_ref, scratch):
    routing_ref, q_ref, k_ref, v_ref, r_ref, gain_ref, gate_ref, up_ref, down_ref = arguments
    (
        kv_buf,
        qr_buf,
        away,
        line,
        x_buf,
        x_other,
        w_buf,
        d_buf,
        acc_buf,
        square_buf,
        hid_buf,
        b_out,
        b_in,
        part,
        mix,
        end_in,
        up_out,
        up_in,
        dn_out,
        dn_in,
        fin,
        own_s,
        away_s,
        weight_s,
        swap_r,
        kv_r,
        qr_r,
        line_r,
        feat_r,
        weight_r,
        hid_r,
        branch_r,
        end_r,
        ret_r,
        last_r,
        sent,
        plane_sent,
    ) = scratch
    rows = q_ref.shape[0]
    half = q_ref.shape[1] // 2
    heads = half // HEAD_DIM
    units = gate_ref.shape[2]
    features = gain_ref.shape[1]
    core_rows = rows // 2
    group_rows = core_rows // GROUPS
    me = lax.axis_index("seq")
    t = lax.axis_index("tp")
    z = me // 2
    y = me % 2
    x = t // 2
    c = t % 2
    yo, xo, co = 1 - y, 1 - x, 1 - c
    tc = 2 * x + co
    tx = 2 * xo + c
    txc = 2 * xo + co
    mate = 2 * z + yo
    dev_y, dev_yc = (mate, t), (mate, tc)
    dev_x, dev_xc = (me, tx), (me, txc)
    dev_c = (me, tc)
    dev_up, dev_dn = (me + 2, t), (me - 2, t)
    has_up, has_dn = z < PLANES - 1, z > 0

    limit = size_of(w_buf.at[0])
    all_lots = [0]
    plane_lots = [[0] for _ in range(PLANES)]

    def lot_for(lots, ref):
        if lots[-1] + size_of(ref) > limit:
            lots.append(0)
        lots[-1] += size_of(ref)
        return len(lots) - 1

    def push(src, dst, recv_sem, device):
        lot = lot_for(all_lots, src)
        remote(src, dst, sent.at[lot], recv_sem, device).start()

    def push_plane(plane, src, dst, recv_sem, device):
        lot = lot_for(plane_lots[plane], src)
        remote(src, dst, plane_sent.at[lot], recv_sem, device).start()

    def got(ref, recv_sem):
        remote(ref, ref, sent.at[0], recv_sem, dev_y).wait_recv()

    def wait_for(amount, recv_sem):
        got(w_buf.at[0, pl.ds(0, amount // (2 * units))], recv_sem)

    def loaded(ref, sem):
        pltpu.make_async_copy(ref, ref, sem).wait()

    barrier = pltpu.get_barrier_semaphore()

    def greet(device):
        pl.semaphore_signal(
            barrier, inc=1, device_id=device, device_id_type=pl.DeviceIdType.MESH
        )

    for device in (dev_y, dev_yc, dev_c, dev_x, dev_xc):
        greet(device)
    pl.when(has_up)(lambda: greet(dev_up))
    pl.when(has_dn)(lambda: greet(dev_dn))

    def cols(which, h):
        return pl.ds(pl.multiple_of(which * half + h * HEAD_DIM, HEAD_DIM), HEAD_DIM)

    sources = ((k_ref, v_ref), (q_ref, r_ref))

    def place(kind, h, n, block):
        buf = kv_buf if kind == 0 else qr_buf
        return buf.at[0, h, n, block]

    def load_own(kind, h):
        for n, ref in enumerate(sources[kind]):
            pltpu.make_async_copy(
                ref.at[:, cols(y, h)], place(kind, h, n, y), own_s.at[kind, h]
            ).start()

    def load_away(kind, h):
        for n, ref in enumerate(sources[kind]):
            pltpu.make_async_copy(
                ref.at[:, cols(yo, h)], away.at[kind, h, n], away_s.at[kind, h]
            ).start()

    def swap(kind, h):
        loaded(away.at[kind, h], away_s.at[kind, h])
        buf = kv_buf if kind == 0 else qr_buf
        push(away.at[kind, h], buf.at[0, h, :, y], swap_r.at[kind, h], dev_y)

    def own(kind, h):
        buf = kv_buf if kind == 0 else qr_buf
        loaded(buf.at[0, h, :, y], own_s.at[kind, h])
        got(buf.at[0, h, :, yo], swap_r.at[kind, h])

    for kind in range(2):
        for h in range(heads):
            load_away(kind, h)
    for kind in range(2):
        for h in range(heads):
            load_own(kind, h)

    expert = [routing_ref[b] for b in range(2 * PLANES)]
    slot = []
    for b in range(2 * PLANES):
        count = jnp.int32(0)
        for j in range(b):
            count = count + jnp.where(expert[j] == expert[b], 1, 0)
        slot.append(jnp.minimum(count, most - 1))
    chosen = []
    for r in range(most):
        index = jnp.int32(0)
        for b in range(2 * PLANES):
            index = jnp.where((expert[b] == z) & (slot[b] == r), b, index)
        chosen.append(index)

    with mark("barwait"):
        pl.semaphore_wait(barrier, 5 + jnp.where(has_up, 1, 0) + jnp.where(has_dn, 1, 0))

    low_order = ((0, 3), (0, 0), (1, 3), (1, 0), (0, 1), (0, 2), (1, 1), (1, 2))
    high_order = ((0, 0), (1, 0), (0, 1), (1, 1), (0, 3), (0, 2), (1, 2), (1, 3))

    @pl.when(z < 2)
    def _():
        for kind, h in low_order:
            swap(kind, h)

    all_lots[:] = [0]

    @pl.when(z >= 2)
    def _():
        for kind, h in high_order:
            swap(kind, h)

    weights = (
        (gate_ref.at[0], w_buf.at[c]),
        (up_ref.at[0], w_buf.at[2 + c]),
        (down_ref.at[0], d_buf.at[c]),
    )
    for i, (src, dst) in enumerate(weights):
        pltpu.make_async_copy(src, dst, weight_s.at[i]).start()
        push(src, dst, weight_r.at[i], dev_c)

    row_at = lax.broadcasted_iota(jnp.int32, (rows, rows), 0)
    col_at = lax.broadcasted_iota(jnp.int32, (rows, rows), 1)
    below, above, farther = 1, 2, 3

    def attend(here, plane, h):
        side = 0 if plane == here else 1
        keep = {here: 0, here - 1: below, here + 1: above, here - 2: farther}
        reach = WINDOW // rows
        for n in range(2):
            block = 2 * plane + n
            seen = [
                (back, keep[(block - back) // 2], (block - back) % 2)
                for back in range(reach + 1)
                if block >= back
            ]
            query = qr_buf[side, h, 0, n]
            parts = []
            for back, at, odd in seen:
                score = lax.dot_general(
                    query,
                    kv_buf[at, h, 0, odd],
                    (((1,), (1,)), ((), ())),
                    preferred_element_type=F32,
                )
                if back == 0:
                    score = jnp.where(col_at <= row_at, score, masked_score)
                if back == reach:
                    score = jnp.where(col_at > row_at, score, masked_score)
                parts.append(score)
            top = parts[0]
            for score in parts[1:]:
                top = jnp.maximum(top, score)
            top = jnp.max(top, axis=1, keepdims=True)
            parts = [jnp.exp((score - top) * (1.0 / math.sqrt(HEAD_DIM))) for score in parts]
            total = parts[0]
            for score in parts[1:]:
                total = total + score
            share = 1.0 / jnp.sum(total, axis=1, keepdims=True)
            attended = jnp.dot(
                jnp.concatenate([(score * share).astype(BF16) for score in parts], axis=1),
                jnp.concatenate([kv_buf[at, h, 1, odd] for _, at, odd in seen], axis=0),
                preferred_element_type=F32,
            )
            stream = (qr_buf[side, h, 1, n].astype(F32) + attended).astype(BF16)
            line[h][block] = stream.reshape(2, core_rows, HEAD_DIM)

    def device_at(way):
        return dev_up if way > 0 else dev_dn

    def send_kv(here, way, src, dst, h):
        push_plane(here, kv_buf.at[src, h], kv_buf.at[dst, h], kv_r.at[dst, h], device_at(way))

    def got_kv(at, h):
        got(kv_buf.at[at, h], kv_r.at[at, h])

    def send_qr(here, h):
        push_plane(here, qr_buf.at[0, h], qr_buf.at[1, h], qr_r.at[h], dev_dn)

    def got_qr(h):
        got(qr_buf.at[1, h], qr_r.at[h])

    def send_line(here, way, plane, h):
        ref = line[h].at[pl.ds(2 * plane, 2)]
        push_plane(here, ref, ref, line_r.at[plane, h], device_at(way))

    def got_line(plane, h):
        got(line[h].at[pl.ds(2 * plane, 2)], line_r.at[plane, h])

    taken = [set() for _ in range(PLANES)]

    def made(here, plane, h):
        taken[here].add((plane, h))
        with mark(f"attend{plane}_{h}"):
            attend(here, plane, h)
        if here < PLANES - 1:
            send_line(here, 1, plane, h)
        if here > 0:
            send_line(here, -1, plane, h)

    def pass_on(here, way, plane, h):
        with mark(f"pass{plane}_{h}"):
            taken[here].add((plane, h))
            got_line(plane, h)
            send_line(here, way, plane, h)

    def steps_0(step):
        if step == 0:
            for kind, h in low_order:
                with mark(f"own{kind}_{h}"):
                    own(kind, h)
                if kind == 0:
                    send_kv(0, 1, 0, below, h)
                else:
                    made(0, 0, h)

    def steps_1(step):
        def first(h):
            with mark(f"own0_{h}"):
                own(0, h)
            send_kv(1, 1, 0, below, h)

        def home(h):
            with mark(f"own1_{h}"):
                own(1, h)
                got_kv(below, h)
            if h == STAY_HEAD:
                send_kv(1, 1, below, farther, h)
            made(1, 1, h)

        def lower(h):
            with mark(f"lower{h}"):
                got_kv(above, h)
                got_qr(h)
            made(1, 2, h)

        if step == 0:
            first(3)
            first(0)
            home(3)
            first(1)
            home(0)
            pass_on(1, 1, 0, 3)
            first(2)
            lower(0)
            pass_on(1, 1, 0, 0)
            home(1)
            lower(1)
            pass_on(1, 1, 0, 1)
            home(2)
            pass_on(1, 1, 0, 2)
            lower(2)
            pass_on(1, -1, 3, 0)
        if step == 1:
            pass_on(1, -1, 2, 3)
            pass_on(1, -1, 3, 3)
        if step == 2:
            pass_on(1, -1, 3, 1)
        if step == 3:
            pass_on(1, -1, 3, 2)

    def steps_2(step):
        def first(h):
            with mark(f"own0_{h}"):
                own(0, h)
            if h == STAY_HEAD:
                send_kv(2, 1, 0, below, h)
            else:
                send_kv(2, -1, 0, above, h)

        def second(h):
            with mark(f"own1_{h}"):
                own(1, h)
            if h != STAY_HEAD:
                send_qr(2, h)

        def lower(h):
            with mark(f"lower{h}"):
                got_kv(above, h)
                got_kv(below, h)
                got_qr(h)
            made(2, 3, h)

        if step == 0:
            for kind, h in high_order:
                if (kind, h) == (1, 2):
                    with mark("below3"):
                        got_kv(below, 3)
                    send_kv(2, 1, below, farther, 3)
                (second if kind else first)(h)
            lower(0)
            with mark("farther3"):
                got_kv(farther, 3)
            made(2, 2, 3)
            pass_on(2, 1, 1, 3)
            lower(1)
            pass_on(2, 1, 0, 3)
            pass_on(2, 1, 1, 0)
            lower(2)
            pass_on(2, 1, 0, 0)
            pass_on(2, -1, 3, 3)
            pass_on(2, 1, 2, 0)
        if step == 2:
            pass_on(2, 1, 1, 1)
            pass_on(2, 1, 0, 1)
            pass_on(2, 1, 2, 1)
        if step == 3:
            pass_on(2, 1, 1, 2)
            pass_on(2, 1, 0, 2)
            pass_on(2, 1, 2, 2)

    def steps_3(step):
        if step == 0:
            for kind, h in high_order:
                with mark(f"own{kind}_{h}"):
                    own(kind, h)
                if h != STAY_HEAD:
                    if kind == 0:
                        send_kv(3, -1, 0, above, h)
                    else:
                        send_qr(3, h)
            with mark("below3"):
                got_kv(below, 3)
                got_kv(farther, 3)
            made(3, 3, 3)

    def planes(step):
        for plane, steps in enumerate((steps_0, steps_1, steps_2, steps_3)):

            @pl.when(z == plane)
            def _():
                steps(step)

    def collect(h):
        for plane in range(PLANES):

            @pl.when(z == plane)
            def _():
                for other in range(PLANES):
                    if (other, h) not in taken[plane]:
                        taken[plane].add((other, h))
                        got_line(other, h)

    def groups_of(h):
        return [pl.ds(g, 1) for g in range(GROUPS)] if h == order[-1] else [pl.ds(0, GROUPS)]

    def feature_at(h, g):
        return order.index(h) + g.start

    def feature(n, py, pt, h, g, device, src=None):
        ref = x_buf.at[py, pt, h, g]
        push(ref if src is None else src, ref, feat_r.at[lot_of[n], feature_at(h, g)], device)

    lot_of = (0, 0, 1, 2, 0, 3, 3)
    arrivals = (
        (y, tc),
        (y, tx),
        (y, txc),
        (yo, t),
        (yo, tc),
        (yo, tx),
        (yo, txc),
    )

    def take(n, h, g):
        py, pt = arrivals[n]
        got(x_buf.at[py, pt, h, g], feat_r.at[lot_of[n], feature_at(h, g)])

    def first_stage(h):
        for g in groups_of(h):
            for r in range(most):
                at = pl.ds(r * group_rows, group_rows)
                for ref, side in ((x_buf.at[y, t, h], c), (x_other.at[h], co)):
                    block = line[h][chosen[r], side]
                    for i in range(GROUPS):
                        if g.start <= i < g.start + g.size:
                            ref[i, at] = block[i * group_rows : (i + 1) * group_rows]
            other = x_other.at[h, g]
            feature(3, y, t, h, g, dev_y)
            feature(2, y, t, h, g, dev_xc, other)
            feature(1, y, t, h, g, dev_x)
            feature(4, y, t, h, g, dev_yc, other)
            feature(0, y, t, h, g, dev_c, other)

    def second_stage(h, g):
        take(3, h, g)
        feature(5, yo, t, h, g, dev_x)
        take(2, h, g)
        feature(6, y, txc, h, g, dev_y)

    def near(h, g):
        wait_for(3 * size_of(x_buf.at[y, t, h, g]), feat_r.at[0, feature_at(h, g)])

    def far(h, g):
        wait_for(2 * size_of(x_buf.at[y, t, h, g]), feat_r.at[3, feature_at(h, g)])

    def expert_parts(parts, h, g):
        depth = g.size * most * group_rows
        left, right = [], []
        square = square_buf[g].reshape(depth, 1)
        for py, pt in parts:
            start = pl.multiple_of((2 * pt + py) * half + h * HEAD_DIM, HEAD_DIM)
            value = x_buf[py, pt, h, g].reshape(depth, HEAD_DIM).astype(F32)
            square = square + jnp.sum(value * value, axis=1, keepdims=True)
            left.append((value * gain_ref[:, pl.ds(start, HEAD_DIM)]).astype(BF16))
            right.append(
                jnp.concatenate(
                    [w_buf[i, pl.ds(start, HEAD_DIM), :] for i in range(4)], axis=1
                )
            )
        square_buf[g] = square.reshape(g.size, most * group_rows, 1)
        acc_buf[g] += jnp.dot(
            jnp.concatenate(left, axis=1),
            jnp.concatenate(right, axis=0),
            preferred_element_type=F32,
        ).reshape(g.size, most * group_rows, 4 * units)

    order = (0, 3, 1, 2)
    near_parts = [(y, t)] + list(arrivals[:5])
    far_parts = list(arrivals[5:])
    last = order[-1]

    planes(0)
    with mark("collect0"):
        collect(0)
    first_stage(0)
    planes(1)
    planes(2)
    with mark("collect3"):
        collect(3)
    first_stage(3)
    with mark("second0"):
        second_stage(0, groups_of(0)[0])
    with mark("collect1"):
        collect(1)
    first_stage(1)
    planes(3)
    with mark("second3"):
        second_stage(3, groups_of(3)[0])
    with mark("collect2"):
        collect(2)
    first_stage(2)
    with mark("second1"):
        second_stage(1, groups_of(1)[0])
    acc_buf[...] = jnp.zeros_like(acc_buf)
    square_buf[...] = jnp.zeros_like(square_buf)
    with mark("weights"):
        for i, (_, ref) in enumerate(
            ((gate_ref, w_buf.at[co]), (up_ref, w_buf.at[2 + co]), (down_ref, d_buf.at[co]))
        ):
            loaded(weights[i][1], weight_s.at[i])
            got(ref, weight_r.at[i])
    for h in order[:2]:
        g = groups_of(h)[0]
        with mark(f"feat{h}"):
            near(h, g)
            far(h, g)
        with mark(f"expert{h}"):
            expert_parts(near_parts + far_parts, h, g)
    g0, g1 = groups_of(last)
    with mark("secondL0"):
        second_stage(last, g0)
    g = groups_of(1)[0]
    with mark("feat1"):
        near(1, g)
        far(1, g)
    with mark("secondL1"):
        second_stage(last, g1)
    with mark("expert1"):
        expert_parts(near_parts + far_parts, 1, g)
    for g in (g0, g1):
        with mark(f"nearL{g.start}"):
            near(last, g)
        with mark(f"farL{g.start}"):
            far(last, g)
        with mark(f"expertL{g.start}"):
            expert_parts(near_parts + far_parts, last, g)
            i = g.start
            scale = lax.rsqrt(square_buf[i] * (1.0 / features) + epsilon)
            gate_val = acc_buf[i, :, pl.ds(0, 2 * units)] * scale
            up_val = acc_buf[i, :, pl.ds(2 * units, 2 * units)] * scale
            hid_buf[x, i] = (gate_val / (1.0 + jnp.exp(-gate_val)) * up_val).astype(BF16)
        push(hid_buf.at[x, i], hid_buf.at[x, i], hid_r.at[i], dev_x)

    wide = half // SPAN
    pieces = [(s, j) for s in range(2) for j in range(wide)]
    per = SPAN // HEAD_DIM

    def chunk(i, s, j):
        return (i * 2 + s) * wide + j

    def branch(i, s, which, j):
        hidden = jnp.concatenate([hid_buf[n, i] for n in range(2)], axis=1)
        at = pl.ds(pl.multiple_of(which * half + j * SPAN, SPAN), SPAN)
        weight = d_buf[c if s == 0 else co, :, at]
        return jnp.dot(hidden, weight, preferred_element_type=F32).astype(BF16)

    def down(i):
        with mark(f"hid{i}"):
            got(hid_buf.at[xo, i], hid_r.at[i])
        with mark(f"down{i}"):
            for s, j in pieces:
                k = chunk(i, s, j)
                b_out[k] = branch(i, s, yo, j)
                push(b_out.at[k], b_in.at[k], branch_r.at[k], dev_y)
            for s, j in pieces:
                k = chunk(i, s, j)
                stream = jnp.concatenate(
                    [x_buf[y, t if s == 0 else tc, j * per + m, i] for m in range(per)], axis=1
                )
                part[k] = stream.astype(F32) + branch(i, s, y, j).astype(F32)

    def blend(k):
        with mark(f"blend{k}"):
            got(b_in.at[k], branch_r.at[k])
            total = part[k] + b_in[k].astype(F32)
            mix[k][...] = total.astype(BF16).reshape(most, group_rows, SPAN)
        for plane, device in ((0, dev_up), (PLANES - 1, dev_dn)):

            @pl.when(z == plane)
            def _():
                push_plane(plane, mix[k], end_in[k], end_r.at[k], device)

    def pick(flag, a, b):
        mask = jnp.full(a.shape, flag.astype(jnp.int32), jnp.int32) > 0
        return jnp.where(mask, a.astype(F32), b.astype(F32)).astype(BF16)

    def give(here, way, k, d, other):
        out, arrived = (up_out, up_in) if way == 0 else (dn_out, dn_in)
        for n in range(2):
            b = 2 * d + n
            out[k, d, n] = pick(expert[b] == here, mix[k][slot[b]], other(b, n))
        push_plane(
            here,
            out.at[k, d],
            arrived.at[k, d],
            ret_r.at[d % 2, k],
            dev_up if way == 0 else dev_dn,
        )

    def turn_in(k):
        for here, way, targets in ((1, 0, (3, 2)), (2, 1, (0, 1))):

            @pl.when(z == here)
            def _():
                with mark(f"turn{k}"):
                    got(end_in[k], end_r.at[k])
                for d in targets:
                    give(here, way, k, d, lambda b, n: end_in[k][slot[b]])

    def carry(k):
        for here, way, d, arrived in ((2, 0, 3, up_in), (1, 1, 0, dn_in)):

            @pl.when(z == here)
            def _():
                with mark(f"carry{k}"):
                    got(arrived.at[k, d], ret_r.at[d % 2, k])
                give(here, way, k, d, lambda b, n: arrived[k, d, n])

    def target(side, i, which, j):
        return out_ref.at[
            pl.ds(pl.multiple_of(side * core_rows + i * group_rows, group_rows), group_rows),
            pl.ds(pl.multiple_of(which * half + j * SPAN, SPAN), SPAN),
        ]

    def arrive(i, s, j):
        k = chunk(i, s, j)
        for d in range(PLANES):

            @pl.when(z == d)
            def _():
                with mark(f"arrive{k}"):
                    if d > 1:
                        got(up_in.at[k, d], ret_r.at[d % 2, k])
                    if d < PLANES - 2:
                        got(dn_in.at[k, d], ret_r.at[d % 2, k])
                for n in range(2):
                    b = 2 * d + n
                    value = mix[k][slot[b]]
                    if d > 0:
                        lower = up_in[k, d, n] if d > 1 else end_in[k][slot[b]]
                        value = pick(expert[b] < d, lower, value)
                    if d < PLANES - 1:
                        higher = dn_in[k, d, n] if d < PLANES - 2 else end_in[k][slot[b]]
                        value = pick(expert[b] > d, higher, value)
                    fin[k, n] = value

        mine = target(c, i, y, j)
        push(fin.at[k, yo], mine, last_r.at[0], dev_y if s == 0 else dev_yc)
        if s == 0:
            mine[...] = fin[k, y]
        else:
            push(fin.at[k, y], mine, last_r.at[0], dev_c)

    down(0)
    first_chunks = [chunk(0, s, j) for s, j in pieces]
    second_chunks = [chunk(1, s, j) for s, j in pieces]
    for k in first_chunks:
        blend(k)
    down(1)
    for k in first_chunks[:2]:
        turn_in(k)
    for k in second_chunks:
        blend(k)
    every = [(i, s, j) for i in range(GROUPS) for s, j in pieces]
    for k in first_chunks[2:]:
        turn_in(k)
    for n, (i, s, j) in enumerate(every):
        k = chunk(i, s, j)
        if n + 4 < len(every):
            turn_in(chunk(*every[n + 4]))
        carry(k)
        if n > 0:
            arrive(*every[n - 1])
    arrive(*every[-1])
    with mark("lastwait"):
        wait_for(3 * size_of(out_ref) // 4, last_r.at[0])

    def all_sent(sem, amount):
        if amount:
            ref = w_buf.at[0, pl.ds(0, amount // (2 * units))]
            remote(ref, ref, sem, hid_r.at[0], dev_y).wait_send()

    with mark("drain"):
        for lot, amount in enumerate(all_lots):
            all_sent(sent.at[lot], amount)
        for plane in range(PLANES):

            @pl.when(z == plane)
            def _():
                for lot, amount in enumerate(plane_lots[plane]):
                    all_sent(plane_sent.at[lot], amount)


def local(
    queries, keys, values, residual_in, norm_gain, routing, gate_weight, up_weight, down_weight
):
    seq_count = lax.axis_size("seq")
    tp_count = lax.axis_size("tp")
    rows, width = queries.shape
    units = gate_weight.shape[2]
    planes = seq_count // 2
    fits = (
        tp_count == 4
        and seq_count == 2 * PLANES
        and rows == BLOCK
        and WINDOW == 4 * rows
        and units == 128
        and width == 8 * HEAD_DIM
    )
    if not fits:
        return local_general(
            queries,
            keys,
            values,
            residual_in,
            norm_gain,
            routing,
            gate_weight,
            up_weight,
            down_weight,
        )
    half = width // 2
    heads = half // HEAD_DIM
    most = min(2 * seq_count // planes, seq_count - planes + 1)
    core_rows = rows // 2
    group_rows = core_rows // GROUPS
    wide = half // SPAN
    chunks = GROUPS * 2 * wide
    vmem = pl.BlockSpec(memory_space=pltpu.VMEM)
    anywhere = pl.BlockSpec(memory_space=pltpu.MemorySpace.HBM)
    dma = pltpu.SemaphoreType.DMA

    def room(*shape, kind=BF16):
        return pltpu.VMEM(shape, kind)

    scratch = (
        room(4, heads, 2, 2, rows, HEAD_DIM),
        room(2, heads, 2, 2, rows, HEAD_DIM),
        room(2, heads, 2, rows, HEAD_DIM),
        [room(2 * planes, 2, core_rows, HEAD_DIM) for _ in range(heads)],
        room(2, tp_count, heads, GROUPS, most * group_rows, HEAD_DIM),
        room(heads, GROUPS, most * group_rows, HEAD_DIM),
        room(4, gate_weight.shape[1], units),
        room(2, down_weight.shape[1], width),
        room(GROUPS, most * group_rows, 4 * units, kind=F32),
        room(GROUPS, most * group_rows, 1, kind=F32),
        room(2, GROUPS, most * group_rows, 2 * units),
        room(chunks, most * group_rows, SPAN),
        room(chunks, most * group_rows, SPAN),
        room(chunks, most * group_rows, SPAN, kind=F32),
        [room(most, group_rows, SPAN) for _ in range(chunks)],
        [room(most, group_rows, SPAN) for _ in range(chunks)],
        room(chunks, planes, 2, group_rows, SPAN),
        room(chunks, planes, 2, group_rows, SPAN),
        room(chunks, planes, 2, group_rows, SPAN),
        room(chunks, planes, 2, group_rows, SPAN),
        room(chunks, 2, group_rows, SPAN),
        dma((2, heads)),
        dma((2, heads)),
        dma((3,)),
        dma((2, heads)),
        dma((4, heads)),
        dma((heads,)),
        dma((planes, heads)),
        dma((4, heads + GROUPS - 1)),
        dma((3,)),
        dma((GROUPS,)),
        dma((chunks,)),
        dma((chunks,)),
        dma((2, chunks)),
        dma((1,)),
        dma((8,)),
        dma((4,)),
    )
    flat, tree = jax.tree.flatten(scratch, is_leaf=lambda leaf: not isinstance(leaf, (list, tuple)))

    def kernel(*refs):
        layer_kernel(most, refs[:9], refs[9], jax.tree.unflatten(tree, refs[10:]))

    return pl.pallas_call(
        kernel,
        name="layer",
        out_shape=jax.ShapeDtypeStruct((rows, width), BF16),
        in_specs=[pl.BlockSpec(memory_space=pltpu.SMEM)]
        + [anywhere] * 4
        + [vmem]
        + [anywhere] * 3,
        out_specs=vmem,
        scratch_shapes=flat,
        compiler_params=pltpu.CompilerParams(
            collective_id=0, has_side_effects=True, vmem_limit_bytes=67043328
        ),
    )(
        routing.reshape(-1),
        queries,
        keys,
        values,
        residual_in,
        norm_gain.reshape(1, -1),
        gate_weight,
        up_weight,
        down_weight,
    )


def solution(mesh):
    in_specs = (
        P("seq", "tp"),
        P("seq", "tp"),
        P("seq", "tp"),
        P("seq", "tp"),
        P(),
        P(),
        P("seq", None, "tp"),
        P("seq", None, "tp"),
        P("seq", None, "tp"),
    )
    out_specs = P("seq", "tp")
    return jax.shard_map(local, mesh=mesh, in_specs=in_specs, out_specs=out_specs, check_vma=False)
```

```python
import contextlib
import math

import jax
import jax.numpy as jnp
from jax import lax
from jax.experimental import pallas as pl
from jax.experimental.pallas import tpu as pltpu
from jax.sharding import PartitionSpec as P

HEAD_DIM = 128
BLOCK = 128
WINDOW = 512


epsilon = 1e-05
masked_score = -1e30


def shifted(block, axis, distance):
    devices = range(lax.axis_size(axis))
    route = [(i - distance, i) for i in devices if i - distance in devices]
    return lax.ppermute(block, axis, route)


def local_general(
    queries, keys, values, residual_in, norm_gain, routing, gate_weight, up_weight, down_weight
):
    seq_count = lax.axis_size("seq")
    seq_place = lax.axis_index("seq")
    tok_rows = queries.shape[0]
    feat_width = queries.shape[1]
    head_count = feat_width // HEAD_DIM
    prior_count = (WINDOW - 1) // tok_rows + 1
    earlier_keys = []
    earlier_values = []
    for distance in range(1, prior_count + 1):
        moved_keys, moved_values = shifted((keys, values), "seq", distance)
        earlier_keys.insert(0, moved_keys)
        earlier_values.insert(0, moved_values)
    key_all = jnp.concatenate(earlier_keys + [keys], axis=0).reshape(-1, head_count, HEAD_DIM)
    value_all = jnp.concatenate(earlier_values + [values], axis=0).reshape(-1, head_count, HEAD_DIM)
    query_heads = queries.reshape(tok_rows, head_count, HEAD_DIM)
    query_pos = seq_place * tok_rows + jnp.arange(tok_rows, dtype=jnp.int32)
    key_pos = (
        seq_place * tok_rows
        - prior_count * tok_rows
        + jnp.arange((prior_count + 1) * tok_rows, dtype=jnp.int32)
    )
    visible = (
        (key_pos[None, :] >= 0)
        & (key_pos[None, :] <= query_pos[:, None])
        & (key_pos[None, :] > query_pos[:, None] - WINDOW)
    )
    scores = jnp.einsum(
        "qhd,khd->hqk", query_heads, key_all, preferred_element_type=jnp.float32
    ) * (1.0 / math.sqrt(HEAD_DIM))
    scores = jnp.where(visible[None], scores, masked_score)
    top_score = jnp.max(scores, axis=2, keepdims=True)
    expo = jnp.exp(scores - top_score)
    weights_soft = (expo / jnp.sum(expo, axis=2, keepdims=True)).astype(jnp.bfloat16)
    attended = jnp.einsum(
        "hqk,khd->qhd", weights_soft, value_all, preferred_element_type=jnp.float32
    ).reshape(tok_rows, feat_width)
    stream = (residual_in.astype(jnp.float32) + attended).astype(jnp.bfloat16)
    send_width = stream.shape[1]
    blocks_dev = tok_rows // BLOCK
    piece_rows = BLOCK // seq_count
    spread_in = stream.reshape(blocks_dev, seq_count, piece_rows, send_width)
    spread_out = lax.all_to_all(spread_in, "seq", split_axis=1, concat_axis=0, tiled=True)
    block_count = blocks_dev * seq_count
    spread_rows = spread_out.reshape(block_count, piece_rows, send_width)
    expert_ids = routing[:, 0]
    expert_count = seq_count // 2
    most_blocks = min(2 * block_count // expert_count, block_count - expert_count + 1)
    order_index = jnp.arange(block_count, dtype=jnp.int32)
    same_expert = expert_ids[None, :] == expert_ids[:, None]
    rank_of = jnp.sum(same_expert & (order_index[None, :] < order_index[:, None]), axis=1)
    expert_range = jnp.arange(expert_count, dtype=jnp.int32)
    slot_range = jnp.arange(most_blocks, dtype=jnp.int32)
    selector = (
        (expert_ids[None, None, :] == expert_range[:, None, None])
        & (rank_of[None, None, :] == slot_range[None, :, None])
    ).astype(jnp.bfloat16)
    picked = jnp.einsum(
        "erb,bqf->erqf", selector, spread_rows, preferred_element_type=jnp.float32
    ).astype(jnp.bfloat16)
    outgoing = jnp.broadcast_to(
        picked[:, None], (expert_count, 2, most_blocks, piece_rows, send_width)
    )
    outgoing = outgoing.reshape(seq_count, most_blocks, piece_rows, send_width)
    features_full = lax.all_gather(
        lax.all_to_all(outgoing, "seq", split_axis=0, concat_axis=0, tiled=True),
        "tp",
        axis=3,
        tiled=True,
    )
    source_count = features_full.shape[0]
    slot_count = features_full.shape[1]
    stream_f32 = features_full.astype(jnp.float32)
    mean_square = jnp.mean(stream_f32 * stream_f32, axis=3, keepdims=True)
    normed = (stream_f32 * lax.rsqrt(mean_square + epsilon) * norm_gain).astype(jnp.bfloat16)
    normed = normed.reshape(-1, normed.shape[3])
    gate_val = jnp.dot(normed, gate_weight[0], preferred_element_type=jnp.float32)
    up_val = jnp.dot(normed, up_weight[0], preferred_element_type=jnp.float32)
    hidden = (jax.nn.silu(gate_val) * up_val).astype(jnp.bfloat16)
    hidden_half = lax.all_gather(hidden, "tp", axis=1, tiled=True)
    partial_value = jnp.dot(hidden_half, down_weight[0], preferred_element_type=jnp.float32).astype(
        jnp.bfloat16
    )
    partial_value = partial_value.reshape(source_count, slot_count, piece_rows, feat_width)
    returned = lax.all_to_all(partial_value, "seq", split_axis=0, concat_axis=0, tiled=True)
    returned = returned.reshape(expert_count, 2, most_blocks, piece_rows * feat_width)
    combined = jnp.einsum("erb,epry->pby", selector, returned, preferred_element_type=jnp.float32)
    residual_rows = spread_rows
    residual_rows = residual_rows.reshape(block_count, piece_rows * feat_width).astype(jnp.float32)
    finished = (residual_rows + combined[0] + combined[1]).astype(jnp.bfloat16)
    finished = finished.reshape(seq_count, blocks_dev, piece_rows, feat_width)
    restored = lax.all_to_all(finished, "seq", split_axis=0, concat_axis=2, tiled=True)
    return restored.reshape(tok_rows, feat_width)


BF16 = jnp.bfloat16
F32 = jnp.float32
PLANES = 4
GROUPS = 2
SPAN = HEAD_DIM
STAY_HEAD = 3


def mark(name):
    return contextlib.nullcontext()


def remote(src, dst, send_sem, recv_sem, device):
    return pltpu.make_async_remote_copy(
        src_ref=src,
        dst_ref=dst,
        send_sem=send_sem,
        recv_sem=recv_sem,
        device_id=device,
        device_id_type=pl.DeviceIdType.MESH,
    )


def size_of(ref):
    return math.prod(ref.shape) * ref.dtype.itemsize


def layer_kernel(most, arguments, out_ref, scratch):
    routing_ref, q_ref, k_ref, v_ref, r_ref, gain_ref, gate_ref, up_ref, down_ref = arguments
    (
        kv_buf,
        qr_buf,
        away,
        line,
        x_buf,
        x_other,
        w_buf,
        d_buf,
        acc_buf,
        square_buf,
        hid_buf,
        b_out,
        b_in,
        part,
        mix,
        end_in,
        up_out,
        up_in,
        dn_out,
        dn_in,
        fin,
        own_s,
        away_s,
        weight_s,
        swap_r,
        kv_r,
        line_r,
        feat_r,
        weight_r,
        hid_r,
        branch_r,
        end_r,
        ret_r,
        last_r,
        sent,
        plane_sent,
    ) = scratch
    rows = q_ref.shape[0]
    half = q_ref.shape[1] // 2
    heads = half // HEAD_DIM
    units = gate_ref.shape[2]
    features = gain_ref.shape[1]
    core_rows = rows // 2
    group_rows = core_rows // GROUPS
    me = lax.axis_index("seq")
    t = lax.axis_index("tp")
    z = me // 2
    y = me % 2
    x = t // 2
    c = t % 2
    yo, xo, co = 1 - y, 1 - x, 1 - c
    tc = 2 * x + co
    tx = 2 * xo + c
    txc = 2 * xo + co
    mate = 2 * z + yo
    dev_y, dev_yc = (mate, t), (mate, tc)
    dev_x, dev_xc = (me, tx), (me, txc)
    dev_c = (me, tc)
    dev_up, dev_dn = (me + 2, t), (me - 2, t)
    has_up, has_dn = z < PLANES - 1, z > 0

    limit = size_of(w_buf.at[0])
    all_lots = [0]
    plane_lots = [[0] for _ in range(PLANES)]

    def lot_for(lots, ref):
        if lots[-1] + size_of(ref) > limit:
            lots.append(0)
        lots[-1] += size_of(ref)
        return len(lots) - 1

    def push(src, dst, recv_sem, device):
        lot = lot_for(all_lots, src)
        remote(src, dst, sent.at[lot], recv_sem, device).start()

    def push_plane(plane, src, dst, recv_sem, device):
        lot = lot_for(plane_lots[plane], src)
        remote(src, dst, plane_sent.at[lot], recv_sem, device).start()

    def got(ref, recv_sem):
        remote(ref, ref, sent.at[0], recv_sem, dev_y).wait_recv()

    def wait_for(amount, recv_sem):
        got(w_buf.at[0, pl.ds(0, amount // (2 * units))], recv_sem)

    def loaded(ref, sem):
        pltpu.make_async_copy(ref, ref, sem).wait()

    barrier = pltpu.get_barrier_semaphore()

    def greet(device):
        pl.semaphore_signal(
            barrier, inc=1, device_id=device, device_id_type=pl.DeviceIdType.MESH
        )

    for device in (dev_y, dev_yc, dev_c, dev_x, dev_xc):
        greet(device)
    pl.when(has_up)(lambda: greet(dev_up))
    pl.when(has_dn)(lambda: greet(dev_dn))

    def cols(which, h):
        return pl.ds(pl.multiple_of(which * half + h * HEAD_DIM, HEAD_DIM), HEAD_DIM)

    sources = ((k_ref, v_ref), (q_ref, r_ref))

    def place(kind, h, n, block):
        buf = kv_buf if kind == 0 else qr_buf
        return buf.at[0, h, n, block]

    def load_own(kind, h):
        for n, ref in enumerate(sources[kind]):
            pltpu.make_async_copy(
                ref.at[:, cols(y, h)], place(kind, h, n, y), own_s.at[0]
            ).start()

    def load_away(kind, h):
        for n, ref in enumerate(sources[kind]):
            pltpu.make_async_copy(
                ref.at[:, cols(yo, h)], away.at[kind, h, n], away_s.at[0]
            ).start()

    def swap(kind, h):
        buf = kv_buf if kind == 0 else qr_buf
        push(away.at[kind, h], buf.at[0, h, :, y], swap_r.at[kind, h], dev_y)

    def own(kind, h):
        buf = kv_buf if kind == 0 else qr_buf
        got(buf.at[0, h, :, yo], swap_r.at[kind, h])

    for kind in range(2):
        for h in range(heads):
            load_away(kind, h)
    for kind in range(2):
        for h in range(heads):
            load_own(kind, h)

    expert = [routing_ref[b] for b in range(2 * PLANES)]
    slot = []
    for b in range(2 * PLANES):
        count = jnp.int32(0)
        for j in range(b):
            count = count + jnp.where(expert[j] == expert[b], 1, 0)
        slot.append(jnp.minimum(count, most - 1))
    chosen = []
    for r in range(most):
        index = jnp.int32(0)
        for b in range(2 * PLANES):
            index = jnp.where((expert[b] == z) & (slot[b] == r), b, index)
        chosen.append(index)

    with mark("barwait"):
        pl.semaphore_wait(barrier, 5 + jnp.where(has_up, 1, 0) + jnp.where(has_dn, 1, 0))

    low_order = ((0, 3), (0, 0), (1, 3), (1, 0), (0, 1), (1, 1), (0, 2), (1, 2))
    high_order = ((0, 0), (1, 0), (0, 3), (0, 1), (1, 1), (1, 3), (0, 2), (1, 2))

    with mark("away"):
        loaded(away, away_s.at[0])

    @pl.when(z < 2)
    def _():
        for kind, h in low_order:
            swap(kind, h)

    all_lots[:] = [0]

    @pl.when(z >= 2)
    def _():
        for kind, h in high_order:
            swap(kind, h)

    weights = (
        (gate_ref.at[0], w_buf.at[c]),
        (up_ref.at[0], w_buf.at[2 + c]),
        (down_ref.at[0], d_buf.at[c]),
    )
    for src, dst in weights:
        pltpu.make_async_copy(src, dst, weight_s.at[0]).start()
        push(src, dst, weight_r.at[0], dev_c)

    with mark("ownwait"):
        loaded(away, own_s.at[0])
    row_at = lax.broadcasted_iota(jnp.int32, (rows, rows), 0)
    col_at = lax.broadcasted_iota(jnp.int32, (rows, rows), 1)
    below, above, farther = 1, 2, 3

    def attend(here, plane, h):
        side = 0 if plane == here else 1
        keep = {here: 0, here - 1: below, here + 1: above, here - 2: farther}
        reach = WINDOW // rows
        for n in range(2):
            block = 2 * plane + n
            seen = [
                (back, keep[(block - back) // 2], (block - back) % 2)
                for back in range(reach + 1)
                if block >= back
            ]
            query = qr_buf[side, h, 0, n]
            parts = []
            for back, at, odd in seen:
                score = lax.dot_general(
                    query,
                    kv_buf[at, h, 0, odd],
                    (((1,), (1,)), ((), ())),
                    preferred_element_type=F32,
                )
                if back == 0:
                    score = jnp.where(col_at <= row_at, score, masked_score)
                if back == reach:
                    score = jnp.where(col_at > row_at, score, masked_score)
                parts.append(score)
            top = parts[0]
            for score in parts[1:]:
                top = jnp.maximum(top, score)
            top = jnp.max(top, axis=1, keepdims=True)
            parts = [jnp.exp((score - top) * (1.0 / math.sqrt(HEAD_DIM))) for score in parts]
            total = parts[0]
            for score in parts[1:]:
                total = total + score
            share = 1.0 / jnp.sum(total, axis=1, keepdims=True)
            attended = jnp.dot(
                jnp.concatenate([(score * share).astype(BF16) for score in parts], axis=1),
                jnp.concatenate([kv_buf[at, h, 1, odd] for _, at, odd in seen], axis=0),
                preferred_element_type=F32,
            )
            stream = (qr_buf[side, h, 1, n].astype(F32) + attended).astype(BF16)
            line[h][block] = stream.reshape(2, core_rows, HEAD_DIM)

    def device_at(way):
        return dev_up if way > 0 else dev_dn

    def kv_sem(at, h):
        return kv_r.at[2 * heads if at == farther else (at - 1) * heads + h]

    def send_kv(here, way, src, dst, h):
        push_plane(here, kv_buf.at[src, h], kv_buf.at[dst, h], kv_sem(dst, h), device_at(way))

    def got_kv(at, h):
        got(kv_buf.at[at, h], kv_sem(at, h))

    def send_qr(here, h):
        push_plane(here, qr_buf.at[0, h], qr_buf.at[1, h], kv_sem(above, h), dev_dn)

    def got_above(h):
        wait_for(size_of(kv_buf.at[0, h]) + size_of(qr_buf.at[0, h]), kv_sem(above, h))

    def send_line(here, way, plane, h):
        ref = line[h].at[pl.ds(2 * plane, 2)]
        push_plane(here, ref, ref, line_r.at[plane, h], device_at(way))

    def got_line(plane, h):
        got(line[h].at[pl.ds(2 * plane, 2)], line_r.at[plane, h])

    taken = [set() for _ in range(PLANES)]

    def made(here, plane, h):
        taken[here].add((plane, h))
        with mark(f"attend{plane}_{h}"):
            attend(here, plane, h)
        if here < PLANES - 1:
            send_line(here, 1, plane, h)
        if here > 0:
            send_line(here, -1, plane, h)

    def pass_on(here, way, plane, h):
        with mark(f"pass{plane}_{h}"):
            taken[here].add((plane, h))
            got_line(plane, h)
            send_line(here, way, plane, h)

    def steps_0(step):
        if step == 0:
            for kind, h in low_order:
                with mark(f"own{kind}_{h}"):
                    own(kind, h)
                if kind == 0:
                    send_kv(0, 1, 0, below, h)
                else:
                    made(0, 0, h)

    def steps_1(step):
        def first(h):
            with mark(f"own0_{h}"):
                own(0, h)
            send_kv(1, 1, 0, below, h)

        def home(h):
            with mark(f"own1_{h}"):
                own(1, h)
                got_kv(below, h)
            if h == STAY_HEAD:
                send_kv(1, 1, below, farther, h)
            made(1, 1, h)

        def lower(h):
            with mark(f"lower{h}"):
                got_above(h)
            made(1, 2, h)

        if step == 0:
            first(3)
            first(0)
            home(3)
            first(1)
            home(0)
            pass_on(1, 1, 0, 3)
            lower(0)
            pass_on(1, 1, 0, 0)
            first(2)
            home(1)
            pass_on(1, -1, 3, 0)
            lower(1)
        if step == 1:
            pass_on(1, 1, 0, 1)
            pass_on(1, -1, 2, 3)
            home(2)
            pass_on(1, -1, 3, 1)
        if step == 2:
            pass_on(1, 1, 0, 2)
            pass_on(1, -1, 3, 3)
        if step == 3:
            lower(2)
            pass_on(1, -1, 3, 2)

    def steps_2(step):
        def first(h):
            with mark(f"own0_{h}"):
                own(0, h)
            if h == STAY_HEAD:
                send_kv(2, 1, 0, below, h)
            else:
                send_kv(2, -1, 0, above, h)

        def second(h):
            with mark(f"own1_{h}"):
                own(1, h)
            if h != STAY_HEAD:
                send_qr(2, h)

        def lower(h):
            with mark(f"lower{h}"):
                got_above(h)
                got_kv(below, h)
            made(2, 3, h)

        if step == 0:
            first(0)
            second(0)
            first(3)
            first(1)
            with mark("below3"):
                got_kv(below, 3)
            send_kv(2, 1, below, farther, 3)
            second(1)
            second(3)
            lower(0)
            with mark("farther3"):
                got_kv(farther, 3)
            made(2, 2, 3)
            pass_on(2, 1, 1, 3)
            lower(1)
            pass_on(2, -1, 3, 3)
            first(2)
            second(2)
            pass_on(2, 1, 1, 0)
            pass_on(2, 1, 0, 3)
        if step == 1:
            pass_on(2, 1, 2, 0)
            pass_on(2, 1, 0, 0)
        if step == 2:
            pass_on(2, 1, 1, 1)
            pass_on(2, 1, 2, 1)
            pass_on(2, 1, 0, 1)
        if step == 3:
            lower(2)
            pass_on(2, 1, 1, 2)
            pass_on(2, 1, 0, 2)
            pass_on(2, 1, 2, 2)

    def steps_3(step):
        if step == 0:
            for kind, h in high_order:
                with mark(f"own{kind}_{h}"):
                    own(kind, h)
                if h != STAY_HEAD:
                    if kind == 0:
                        send_kv(3, -1, 0, above, h)
                    else:
                        send_qr(3, h)
                elif kind == 1:
                    with mark("below3"):
                        got_kv(below, 3)
                        got_kv(farther, 3)
                    made(3, 3, 3)

    def planes(step):
        for plane, steps in enumerate((steps_0, steps_1, steps_2, steps_3)):

            @pl.when(z == plane)
            def _():
                steps(step)

    def collect(order, pos):
        h = order[pos]
        for plane in range(PLANES):
            if orders[plane // 2][pos] != h:
                continue

            @pl.when(z == plane)
            def _():
                for other in range(PLANES):
                    if (other, h) not in taken[plane]:
                        taken[plane].add((other, h))
                        got_line(other, h)

    high = jnp.where(z < 2, 0, 1)
    orders = ((0, 1, 3, 2), (3, 0, 1, 2))
    heads_at = [low + high * (up - low) for low, up in zip(*orders)]
    ends = len(heads_at) - 1

    def groups_of(pos):
        return [pl.ds(g, 1) for g in range(GROUPS)] if pos == ends else [pl.ds(0, GROUPS)]

    def feature_at(pos, g):
        return pos + g.start

    def feature(n, py, pt, pos, g, device, src=None):
        ref = x_buf.at[py, pt, heads_at[pos], g]
        push(ref if src is None else src, ref, feat_r.at[lot_of[n], feature_at(pos, g)], device)

    lot_of = (0, 0, 1, 2, 0, 3, 3)
    arrivals = (
        (y, tc),
        (y, tx),
        (y, txc),
        (yo, t),
        (yo, tc),
        (yo, tx),
        (yo, txc),
    )

    def take(n, pos, g):
        py, pt = arrivals[n]
        got(x_buf.at[py, pt, heads_at[pos], g], feat_r.at[lot_of[n], feature_at(pos, g)])

    def choose(h, g):
        for r in range(most):
            at = pl.ds(r * group_rows, group_rows)
            for ref, side in ((x_buf.at[y, t, h], c), (x_other.at[h], co)):
                block = line[h][chosen[r], side]
                for i in range(GROUPS):
                    if g.start <= i < g.start + g.size:
                        ref[i, at] = block[i * group_rows : (i + 1) * group_rows]

    def gather(pos):
        with mark(f"collect{pos}"):
            for order in orders:
                if order is orders[0] or order[pos] != orders[0][pos]:
                    collect(order, pos)

    def first_stage(pos, lots=None):
        for g in lots or groups_of(pos):
            if orders[0][pos] == orders[1][pos]:
                choose(orders[0][pos], g)
            else:
                pl.when(z < 2)(lambda: choose(orders[0][pos], g))
                pl.when(z >= 2)(lambda: choose(orders[1][pos], g))
            other = x_other.at[heads_at[pos], g]
            feature(3, y, t, pos, g, dev_y)
            feature(2, y, t, pos, g, dev_xc, other)
            feature(1, y, t, pos, g, dev_x)
            feature(4, y, t, pos, g, dev_yc, other)
            feature(0, y, t, pos, g, dev_c, other)

    def second_stage(pos, g):
        take(3, pos, g)
        feature(5, yo, t, pos, g, dev_x)
        take(2, pos, g)
        feature(6, y, txc, pos, g, dev_y)

    def near(pos, g):
        wait_for(3 * size_of(x_buf.at[y, t, 0, g]), feat_r.at[0, feature_at(pos, g)])

    def far(pos, g):
        wait_for(2 * size_of(x_buf.at[y, t, 0, g]), feat_r.at[3, feature_at(pos, g)])

    def expert_parts(parts, pos, g):
        depth = g.size * most * group_rows
        left, right = [], []
        square = square_buf[g].reshape(depth, 1)
        for py, pt in parts:
            start = pl.multiple_of((2 * pt + py) * half + heads_at[pos] * HEAD_DIM, HEAD_DIM)
            value = x_buf[py, pt, heads_at[pos], g].reshape(depth, HEAD_DIM).astype(F32)
            square = square + jnp.sum(value * value, axis=1, keepdims=True)
            left.append((value * gain_ref[:, pl.ds(start, HEAD_DIM)]).astype(BF16))
            right.append(
                jnp.concatenate(
                    [w_buf[i, pl.ds(start, HEAD_DIM), :] for i in range(4)], axis=1
                )
            )
        square_buf[g] = square.reshape(g.size, most * group_rows, 1)
        acc_buf[g] += jnp.dot(
            jnp.concatenate(left, axis=1),
            jnp.concatenate(right, axis=0),
            preferred_element_type=F32,
        ).reshape(g.size, most * group_rows, 4 * units)

    every_part = [(y, t)] + list(arrivals)

    g0, g1 = groups_of(ends)
    both = groups_of(0)[0]
    planes(0)
    gather(0)
    first_stage(0)
    planes(1)
    gather(1)
    first_stage(1)
    with mark("second0"):
        second_stage(0, both)
    planes(2)
    gather(2)
    first_stage(2)
    with mark("second1"):
        second_stage(1, both)
    planes(3)
    gather(3)
    first_stage(3, [g0])
    with mark("second2"):
        second_stage(2, both)
    first_stage(3, [g1])
    acc_buf[...] = jnp.zeros_like(acc_buf)
    square_buf[...] = jnp.zeros_like(square_buf)
    with mark("weights"):
        every = w_buf.at[pl.ds(0, len(weights))]
        loaded(every, weight_s.at[0])
        got(every, weight_r.at[0])

    def whole(pos):
        with mark(f"feat{pos}"):
            near(pos, both)
            far(pos, both)
        with mark(f"expert{pos}"):
            expert_parts(every_part, pos, both)

    whole(0)
    with mark("secondL0"):
        second_stage(ends, g0)
    with mark("secondL1"):
        second_stage(ends, g1)
    whole(1)
    whole(2)
    for g in (g0, g1):
        with mark(f"nearL{g.start}"):
            near(ends, g)
        with mark(f"farL{g.start}"):
            far(ends, g)
        with mark(f"expertL{g.start}"):
            expert_parts(every_part, ends, g)
            i = g.start
            scale = lax.rsqrt(square_buf[i] * (1.0 / features) + epsilon)
            gate_val = acc_buf[i, :, pl.ds(0, 2 * units)] * scale
            up_val = acc_buf[i, :, pl.ds(2 * units, 2 * units)] * scale
            hid_buf[x, i] = (gate_val / (1.0 + jnp.exp(-gate_val)) * up_val).astype(BF16)
        push(hid_buf.at[x, i], hid_buf.at[x, i], hid_r.at[i], dev_x)

    wide = half // SPAN
    pieces = [(s, j) for s in range(2) for j in range(wide)]

    def chunk(i, s, j):
        return (i * 2 + s) * wide + j

    pair = 2 * SPAN

    def branch(i, s, which, j):
        hidden = jnp.concatenate([hid_buf[n, i] for n in range(2)], axis=1)
        at = pl.ds(pl.multiple_of(which * half + j * pair, pair), pair)
        weight = d_buf[c if s == 0 else co, :, at]
        value = jnp.dot(hidden, weight, preferred_element_type=F32).astype(BF16)
        return [(chunk(i, s, 2 * j + m), value[:, m * SPAN : (m + 1) * SPAN]) for m in range(2)]

    def down(i):
        with mark(f"hid{i}"):
            got(hid_buf.at[xo, i], hid_r.at[i])
        with mark(f"down{i}"):
            doubles = [(s, j) for s in range(2) for j in range(wide // 2)]
            for s, j in doubles:
                for k, value in branch(i, s, yo, j):
                    b_out[k] = value
                    push(b_out.at[k], b_in.at[k], branch_r.at[k], dev_y)
            for s, j in doubles:
                for m, (k, value) in enumerate(branch(i, s, y, j)):
                    stream = x_buf[y, t if s == 0 else tc, 2 * j + m, i]
                    part[k] = stream.astype(F32) + value.astype(F32)

    def blend(i, s, j):
        k = chunk(i, s, j)
        with mark(f"blend{k}"):
            got(b_in.at[k], branch_r.at[k])
            total = part[k] + b_in[k].astype(F32)
            mix[k][...] = total.astype(BF16).reshape(most, group_rows, SPAN)
        for plane, device in ((0, dev_up), (PLANES - 1, dev_dn)):

            @pl.when(z == plane)
            def _():
                push_plane(plane, mix[k], end_in[k], end_r.at[k], device)

    def pick(flag, a, b):
        mask = jnp.full(a.shape, flag.astype(jnp.int32), jnp.int32) > 0
        return jnp.where(mask, a.astype(F32), b.astype(F32)).astype(BF16)

    def give(here, way, k, d, other):
        out, arrived = (up_out, up_in) if way == 0 else (dn_out, dn_in)
        for n in range(2):
            b = 2 * d + n
            out[k, d, n] = pick(expert[b] == here, mix[k][slot[b]], other(b, n))
        push_plane(
            here,
            out.at[k, d],
            arrived.at[k, d],
            ret_r.at[d % 2, k],
            dev_up if way == 0 else dev_dn,
        )

    def turn_in(i, s, j):
        k = chunk(i, s, j)
        for here, way, targets in ((1, 0, (3, 2)), (2, 1, (0, 1))):

            @pl.when(z == here)
            def _():
                with mark(f"turn{k}"):
                    got(end_in[k], end_r.at[k])
                for d in targets:
                    give(here, way, k, d, lambda b, n: end_in[k][slot[b]])

    def carry(i, s, j):
        k = chunk(i, s, j)
        for here, way, d, arrived in ((2, 0, 3, up_in), (1, 1, 0, dn_in)):

            @pl.when(z == here)
            def _():
                with mark(f"carry{k}"):
                    got(arrived.at[k, d], ret_r.at[d % 2, k])
                give(here, way, k, d, lambda b, n: arrived[k, d, n])

    def target(side, i, which, j):
        return out_ref.at[
            pl.ds(pl.multiple_of(side * core_rows + i * group_rows, group_rows), group_rows),
            pl.ds(pl.multiple_of(which * half + j * SPAN, SPAN), SPAN),
        ]

    def arrive(i, s, j):
        k = chunk(i, s, j)
        for d in range(PLANES):

            @pl.when(z == d)
            def _():
                with mark(f"arrive{k}"):
                    if d > 1:
                        got(up_in.at[k, d], ret_r.at[d % 2, k])
                    if d < PLANES - 2:
                        got(dn_in.at[k, d], ret_r.at[d % 2, k])
                for n in range(2):
                    b = 2 * d + n
                    value = mix[k][slot[b]]
                    if d > 0:
                        lower = up_in[k, d, n] if d > 1 else end_in[k][slot[b]]
                        value = pick(expert[b] < d, lower, value)
                    if d < PLANES - 1:
                        higher = dn_in[k, d, n] if d < PLANES - 2 else end_in[k][slot[b]]
                        value = pick(expert[b] > d, higher, value)
                    fin[k, n] = value

        mine = target(c, i, y, j)
        push(fin.at[k, yo], mine, last_r.at[0], dev_y if s == 0 else dev_yc)
        if s == 0:
            mine[...] = fin[k, y]
        else:
            push(fin.at[k, y], mine, last_r.at[0], dev_c)

    every = [(i, s, j) for i in range(GROUPS) for s, j in pieces]
    for i in range(GROUPS):
        down(i)
    stages = ((0, blend), (4, turn_in), (8, carry), (11, arrive))
    for n in range(len(every) + stages[-1][0]):
        for lag, stage in stages:
            if 0 <= n - lag < len(every):
                stage(*every[n - lag])
    with mark("lastwait"):
        wait_for(3 * size_of(out_ref) // 4, last_r.at[0])

    def all_sent(sem, amount):
        if amount:
            ref = w_buf.at[0, pl.ds(0, amount // (2 * units))]
            remote(ref, ref, sem, hid_r.at[0], dev_y).wait_send()

    with mark("drain"):
        for lot, amount in enumerate(all_lots):
            all_sent(sent.at[lot], amount)
        for plane in range(PLANES):

            @pl.when(z == plane)
            def _():
                for lot, amount in enumerate(plane_lots[plane]):
                    all_sent(plane_sent.at[lot], amount)


def local(
    queries, keys, values, residual_in, norm_gain, routing, gate_weight, up_weight, down_weight
):
    seq_count = lax.axis_size("seq")
    tp_count = lax.axis_size("tp")
    rows, width = queries.shape
    units = gate_weight.shape[2]
    planes = seq_count // 2
    fits = (
        tp_count == 4
        and seq_count == 2 * PLANES
        and rows == BLOCK
        and WINDOW == 4 * rows
        and units == 128
        and width == 8 * HEAD_DIM
    )
    if not fits:
        return local_general(
            queries,
            keys,
            values,
            residual_in,
            norm_gain,
            routing,
            gate_weight,
            up_weight,
            down_weight,
        )
    half = width // 2
    heads = half // HEAD_DIM
    most = min(2 * seq_count // planes, seq_count - planes + 1)
    core_rows = rows // 2
    group_rows = core_rows // GROUPS
    wide = half // SPAN
    chunks = GROUPS * 2 * wide
    vmem = pl.BlockSpec(memory_space=pltpu.VMEM)
    anywhere = pl.BlockSpec(memory_space=pltpu.MemorySpace.HBM)
    dma = pltpu.SemaphoreType.DMA

    def room(*shape, kind=BF16):
        return pltpu.VMEM(shape, kind)

    scratch = (
        room(4, heads, 2, 2, rows, HEAD_DIM),
        room(2, heads, 2, 2, rows, HEAD_DIM),
        room(2, heads, 2, rows, HEAD_DIM),
        [room(2 * planes, 2, core_rows, HEAD_DIM) for _ in range(heads)],
        room(2, tp_count, heads, GROUPS, most * group_rows, HEAD_DIM),
        room(heads, GROUPS, most * group_rows, HEAD_DIM),
        room(4, gate_weight.shape[1], units),
        room(2, down_weight.shape[1], width),
        room(GROUPS, most * group_rows, 4 * units, kind=F32),
        room(GROUPS, most * group_rows, 1, kind=F32),
        room(2, GROUPS, most * group_rows, 2 * units),
        room(chunks, most * group_rows, SPAN),
        room(chunks, most * group_rows, SPAN),
        room(chunks, most * group_rows, SPAN, kind=F32),
        [room(most, group_rows, SPAN) for _ in range(chunks)],
        [room(most, group_rows, SPAN) for _ in range(chunks)],
        room(chunks, planes, 2, group_rows, SPAN),
        room(chunks, planes, 2, group_rows, SPAN),
        room(chunks, planes, 2, group_rows, SPAN),
        room(chunks, planes, 2, group_rows, SPAN),
        room(chunks, 2, group_rows, SPAN),
        dma((1,)),
        dma((1,)),
        dma((1,)),
        dma((2, heads)),
        dma((2 * heads + 1,)),
        dma((planes, heads)),
        dma((4, heads + GROUPS - 1)),
        dma((1,)),
        dma((GROUPS,)),
        dma((chunks,)),
        dma((chunks,)),
        dma((2, chunks)),
        dma((1,)),
        dma((8,)),
        dma((4,)),
    )
    flat, tree = jax.tree.flatten(scratch, is_leaf=lambda leaf: not isinstance(leaf, (list, tuple)))

    def kernel(*refs):
        layer_kernel(most, refs[:9], refs[9], jax.tree.unflatten(tree, refs[10:]))

    return pl.pallas_call(
        kernel,
        name="layer",
        out_shape=jax.ShapeDtypeStruct((rows, width), BF16),
        in_specs=[pl.BlockSpec(memory_space=pltpu.SMEM)]
        + [anywhere] * 4
        + [vmem]
        + [anywhere] * 3,
        out_specs=vmem,
        scratch_shapes=flat,
        compiler_params=pltpu.CompilerParams(
            collective_id=0, has_side_effects=True, vmem_limit_bytes=67043328
        ),
    )(
        routing.reshape(-1),
        queries,
        keys,
        values,
        residual_in,
        norm_gain.reshape(1, -1),
        gate_weight,
        up_weight,
        down_weight,
    )


def solution(mesh):
    in_specs = (
        P("seq", "tp"),
        P("seq", "tp"),
        P("seq", "tp"),
        P("seq", "tp"),
        P(),
        P(),
        P("seq", None, "tp"),
        P("seq", None, "tp"),
        P("seq", None, "tp"),
    )
    out_specs = P("seq", "tp")
    return jax.shard_map(local, mesh=mesh, in_specs=in_specs, out_specs=out_specs, check_vma=False)
```

```python
import contextlib
import math

import jax
import jax.numpy as jnp
from jax import lax
from jax.experimental import pallas as pl
from jax.experimental.pallas import tpu as pltpu
from jax.sharding import PartitionSpec as P

HEAD_DIM = 128
BLOCK = 128
WINDOW = 512


epsilon = 1e-05
masked_score = -1e30


def shifted(block, axis, distance):
    devices = range(lax.axis_size(axis))
    route = [(i - distance, i) for i in devices if i - distance in devices]
    return lax.ppermute(block, axis, route)


def local_general(
    queries, keys, values, residual_in, norm_gain, routing, gate_weight, up_weight, down_weight
):
    seq_count = lax.axis_size("seq")
    seq_place = lax.axis_index("seq")
    tok_rows = queries.shape[0]
    feat_width = queries.shape[1]
    head_count = feat_width // HEAD_DIM
    prior_count = (WINDOW - 1) // tok_rows + 1
    earlier_keys = []
    earlier_values = []
    for distance in range(1, prior_count + 1):
        moved_keys, moved_values = shifted((keys, values), "seq", distance)
        earlier_keys.insert(0, moved_keys)
        earlier_values.insert(0, moved_values)
    key_all = jnp.concatenate(earlier_keys + [keys], axis=0).reshape(-1, head_count, HEAD_DIM)
    value_all = jnp.concatenate(earlier_values + [values], axis=0).reshape(-1, head_count, HEAD_DIM)
    query_heads = queries.reshape(tok_rows, head_count, HEAD_DIM)
    query_pos = seq_place * tok_rows + jnp.arange(tok_rows, dtype=jnp.int32)
    key_pos = (
        seq_place * tok_rows
        - prior_count * tok_rows
        + jnp.arange((prior_count + 1) * tok_rows, dtype=jnp.int32)
    )
    visible = (
        (key_pos[None, :] >= 0)
        & (key_pos[None, :] <= query_pos[:, None])
        & (key_pos[None, :] > query_pos[:, None] - WINDOW)
    )
    scores = jnp.einsum(
        "qhd,khd->hqk", query_heads, key_all, preferred_element_type=jnp.float32
    ) * (1.0 / math.sqrt(HEAD_DIM))
    scores = jnp.where(visible[None], scores, masked_score)
    top_score = jnp.max(scores, axis=2, keepdims=True)
    expo = jnp.exp(scores - top_score)
    weights_soft = (expo / jnp.sum(expo, axis=2, keepdims=True)).astype(jnp.bfloat16)
    attended = jnp.einsum(
        "hqk,khd->qhd", weights_soft, value_all, preferred_element_type=jnp.float32
    ).reshape(tok_rows, feat_width)
    stream = (residual_in.astype(jnp.float32) + attended).astype(jnp.bfloat16)
    send_width = stream.shape[1]
    blocks_dev = tok_rows // BLOCK
    piece_rows = BLOCK // seq_count
    spread_in = stream.reshape(blocks_dev, seq_count, piece_rows, send_width)
    spread_out = lax.all_to_all(spread_in, "seq", split_axis=1, concat_axis=0, tiled=True)
    block_count = blocks_dev * seq_count
    spread_rows = spread_out.reshape(block_count, piece_rows, send_width)
    expert_ids = routing[:, 0]
    expert_count = seq_count // 2
    most_blocks = min(2 * block_count // expert_count, block_count - expert_count + 1)
    order_index = jnp.arange(block_count, dtype=jnp.int32)
    same_expert = expert_ids[None, :] == expert_ids[:, None]
    rank_of = jnp.sum(same_expert & (order_index[None, :] < order_index[:, None]), axis=1)
    expert_range = jnp.arange(expert_count, dtype=jnp.int32)
    slot_range = jnp.arange(most_blocks, dtype=jnp.int32)
    selector = (
        (expert_ids[None, None, :] == expert_range[:, None, None])
        & (rank_of[None, None, :] == slot_range[None, :, None])
    ).astype(jnp.bfloat16)
    picked = jnp.einsum(
        "erb,bqf->erqf", selector, spread_rows, preferred_element_type=jnp.float32
    ).astype(jnp.bfloat16)
    outgoing = jnp.broadcast_to(
        picked[:, None], (expert_count, 2, most_blocks, piece_rows, send_width)
    )
    outgoing = outgoing.reshape(seq_count, most_blocks, piece_rows, send_width)
    features_full = lax.all_gather(
        lax.all_to_all(outgoing, "seq", split_axis=0, concat_axis=0, tiled=True),
        "tp",
        axis=3,
        tiled=True,
    )
    source_count = features_full.shape[0]
    slot_count = features_full.shape[1]
    stream_f32 = features_full.astype(jnp.float32)
    mean_square = jnp.mean(stream_f32 * stream_f32, axis=3, keepdims=True)
    normed = (stream_f32 * lax.rsqrt(mean_square + epsilon) * norm_gain).astype(jnp.bfloat16)
    normed = normed.reshape(-1, normed.shape[3])
    gate_val = jnp.dot(normed, gate_weight[0], preferred_element_type=jnp.float32)
    up_val = jnp.dot(normed, up_weight[0], preferred_element_type=jnp.float32)
    hidden = (jax.nn.silu(gate_val) * up_val).astype(jnp.bfloat16)
    hidden_half = lax.all_gather(hidden, "tp", axis=1, tiled=True)
    partial_value = jnp.dot(hidden_half, down_weight[0], preferred_element_type=jnp.float32).astype(
        jnp.bfloat16
    )
    partial_value = partial_value.reshape(source_count, slot_count, piece_rows, feat_width)
    returned = lax.all_to_all(partial_value, "seq", split_axis=0, concat_axis=0, tiled=True)
    returned = returned.reshape(expert_count, 2, most_blocks, piece_rows * feat_width)
    combined = jnp.einsum("erb,epry->pby", selector, returned, preferred_element_type=jnp.float32)
    residual_rows = spread_rows
    residual_rows = residual_rows.reshape(block_count, piece_rows * feat_width).astype(jnp.float32)
    finished = (residual_rows + combined[0] + combined[1]).astype(jnp.bfloat16)
    finished = finished.reshape(seq_count, blocks_dev, piece_rows, feat_width)
    restored = lax.all_to_all(finished, "seq", split_axis=0, concat_axis=2, tiled=True)
    return restored.reshape(tok_rows, feat_width)


BF16 = jnp.bfloat16
F32 = jnp.float32
PLANES = 4
GROUPS = 2
SPAN = HEAD_DIM
STAY_HEAD = 3


def mark(name):
    return contextlib.nullcontext()


def remote(src, dst, send_sem, recv_sem, device):
    return pltpu.make_async_remote_copy(
        src_ref=src,
        dst_ref=dst,
        send_sem=send_sem,
        recv_sem=recv_sem,
        device_id=device,
        device_id_type=pl.DeviceIdType.MESH,
    )


def size_of(ref):
    return math.prod(ref.shape) * ref.dtype.itemsize


def layer_kernel(most, arguments, out_ref, scratch):
    routing_ref, q_ref, k_ref, v_ref, r_ref, gain_ref, gate_ref, up_ref, down_ref = arguments
    (
        kv_buf,
        qr_buf,
        away,
        line,
        x_buf,
        x_other,
        w_buf,
        d_buf,
        acc_buf,
        square_buf,
        hid_buf,
        b_out,
        b_in,
        part,
        mix,
        end_in,
        up_out,
        up_in,
        dn_out,
        dn_in,
        fin,
        own_s,
        away_s,
        weight_s,
        swap_r,
        kv_r,
        line_r,
        feat_r,
        weight_r,
        hid_r,
        branch_r,
        end_r,
        ret_r,
        last_r,
        sent,
        plane_sent,
    ) = scratch
    rows = q_ref.shape[0]
    half = q_ref.shape[1] // 2
    heads = half // HEAD_DIM
    units = gate_ref.shape[2]
    features = gain_ref.shape[1]
    core_rows = rows // 2
    group_rows = core_rows // GROUPS
    me = lax.axis_index("seq")
    t = lax.axis_index("tp")
    z = me // 2
    y = me % 2
    x = t // 2
    c = t % 2
    yo, xo, co = 1 - y, 1 - x, 1 - c
    tc = 2 * x + co
    tx = 2 * xo + c
    txc = 2 * xo + co
    mate = 2 * z + yo
    dev_y, dev_yc = (mate, t), (mate, tc)
    dev_x, dev_xc = (me, tx), (me, txc)
    dev_c = (me, tc)
    dev_up, dev_dn = (me + 2, t), (me - 2, t)
    has_up, has_dn = z < PLANES - 1, z > 0

    limit = size_of(w_buf.at[0])
    all_lots = [0]
    plane_lots = [[0] for _ in range(PLANES)]

    def lot_for(lots, ref):
        if lots[-1] + size_of(ref) > limit:
            lots.append(0)
        lots[-1] += size_of(ref)
        return len(lots) - 1

    final_lot = sent.shape[0] - 1

    def push(src, dst, recv_sem, device, lot=None):
        lot = lot_for(all_lots, src) if lot is None else lot
        remote(src, dst, sent.at[lot], recv_sem, device).start()

    def push_plane(plane, src, dst, recv_sem, device):
        lot = lot_for(plane_lots[plane], src)
        remote(src, dst, plane_sent.at[lot], recv_sem, device).start()

    def got(ref, recv_sem):
        remote(ref, ref, sent.at[0], recv_sem, dev_y).wait_recv()

    def wait_for(amount, recv_sem):
        got(w_buf.at[0, pl.ds(0, amount // (2 * units))], recv_sem)

    def loaded(ref, sem):
        pltpu.make_async_copy(ref, ref, sem).wait()

    barrier = pltpu.get_barrier_semaphore()

    def greet(device):
        pl.semaphore_signal(
            barrier, inc=1, device_id=device, device_id_type=pl.DeviceIdType.MESH
        )

    for device in (dev_y, dev_yc, dev_c, dev_x, dev_xc):
        greet(device)
    pl.when(has_up)(lambda: greet(dev_up))
    pl.when(has_dn)(lambda: greet(dev_dn))

    def cols(which, h):
        return pl.ds(pl.multiple_of(which * half + h * HEAD_DIM, HEAD_DIM), HEAD_DIM)

    sources = ((k_ref, v_ref), (q_ref, r_ref))

    def place(kind, h, n, block):
        buf = kv_buf if kind == 0 else qr_buf
        return buf.at[0, h, n, block]

    def load_own(kind, h):
        for n, ref in enumerate(sources[kind]):
            pltpu.make_async_copy(
                ref.at[:, cols(y, h)], place(kind, h, n, y), own_s.at[0]
            ).start()

    def load_away(kind, h):
        for n, ref in enumerate(sources[kind]):
            pltpu.make_async_copy(
                ref.at[:, cols(yo, h)], away.at[kind, h, n], away_s.at[0]
            ).start()

    def swap(kind, h):
        buf = kv_buf if kind == 0 else qr_buf
        push(away.at[kind, h], buf.at[0, h, :, y], swap_r.at[kind, h], dev_y)

    def own(kind, h):
        buf = kv_buf if kind == 0 else qr_buf
        got(buf.at[0, h, :, yo], swap_r.at[kind, h])

    for kind in range(2):
        for h in range(heads):
            load_away(kind, h)
    for kind in range(2):
        for h in range(heads):
            load_own(kind, h)

    expert = [routing_ref[b] for b in range(2 * PLANES)]
    slot = []
    for b in range(2 * PLANES):
        count = jnp.int32(0)
        for j in range(b):
            count = count + jnp.where(expert[j] == expert[b], 1, 0)
        slot.append(jnp.minimum(count, most - 1))
    chosen = []
    for r in range(most):
        index = jnp.int32(0)
        for b in range(2 * PLANES):
            index = jnp.where((expert[b] == z) & (slot[b] == r), b, index)
        chosen.append(index)

    with mark("barwait"):
        pl.semaphore_wait(barrier, 5 + jnp.where(has_up, 1, 0) + jnp.where(has_dn, 1, 0))

    low_order = ((0, 3), (0, 0), (1, 3), (1, 0), (0, 1), (1, 1), (0, 2), (1, 2))
    high_order = ((0, 0), (1, 0), (0, 3), (0, 1), (1, 1), (1, 3), (0, 2), (1, 2))

    with mark("away"):
        loaded(away, away_s.at[0])

    @pl.when(z < 2)
    def _():
        for kind, h in low_order:
            swap(kind, h)

    all_lots[:] = [0]

    @pl.when(z >= 2)
    def _():
        for kind, h in high_order:
            swap(kind, h)

    with mark("ownwait"):
        loaded(away, own_s.at[0])
    row_at = lax.broadcasted_iota(jnp.int32, (rows, rows), 0)
    col_at = lax.broadcasted_iota(jnp.int32, (rows, rows), 1)
    below, above, farther = 1, 2, 3

    def attend(here, plane, h):
        side = 0 if plane == here else 1
        keep = {here: 0, here - 1: below, here + 1: above, here - 2: farther}
        reach = WINDOW // rows
        for n in range(2):
            block = 2 * plane + n
            seen = [
                (back, keep[(block - back) // 2], (block - back) % 2)
                for back in range(reach + 1)
                if block >= back
            ]
            query = qr_buf[side, h, 0, n]
            parts = []
            for back, at, odd in seen:
                score = lax.dot_general(
                    query,
                    kv_buf[at, h, 0, odd],
                    (((1,), (1,)), ((), ())),
                    preferred_element_type=F32,
                )
                if back == 0:
                    score = jnp.where(col_at <= row_at, score, masked_score)
                if back == reach:
                    score = jnp.where(col_at > row_at, score, masked_score)
                parts.append(score)
            top = parts[0]
            for score in parts[1:]:
                top = jnp.maximum(top, score)
            top = jnp.max(top, axis=1, keepdims=True)
            parts = [jnp.exp((score - top) * (1.0 / math.sqrt(HEAD_DIM))) for score in parts]
            total = parts[0]
            for score in parts[1:]:
                total = total + score
            share = 1.0 / jnp.sum(total, axis=1, keepdims=True)
            attended = jnp.dot(
                jnp.concatenate([(score * share).astype(BF16) for score in parts], axis=1),
                jnp.concatenate([kv_buf[at, h, 1, odd] for _, at, odd in seen], axis=0),
                preferred_element_type=F32,
            )
            stream = (qr_buf[side, h, 1, n].astype(F32) + attended).astype(BF16)
            line[h][block] = stream.reshape(2, core_rows, HEAD_DIM)

    def device_at(way):
        return dev_up if way > 0 else dev_dn

    def kv_sem(at, h):
        return kv_r.at[2 * heads if at == farther else (at - 1) * heads + h]

    def send_kv(here, way, src, dst, h):
        push_plane(here, kv_buf.at[src, h], kv_buf.at[dst, h], kv_sem(dst, h), device_at(way))

    def got_kv(at, h):
        got(kv_buf.at[at, h], kv_sem(at, h))

    def send_part(here, way, kind, h, block):
        at = below if way > 0 else above
        buf, to = (kv_buf, at) if kind == 0 else (qr_buf, 1)
        push_plane(
            here, buf.at[0, h, :, block], buf.at[to, h, :, block], kv_sem(at, h), device_at(way)
        )

    def send_home(here, way, h, kinds=(0,)):
        for kind in kinds:
            send_part(here, way, kind, h, y)

    def got_above(h):
        wait_for(size_of(kv_buf.at[0, h]) + size_of(qr_buf.at[0, h]), kv_sem(above, h))

    def send_line(here, way, plane, h):
        ref = line[h].at[pl.ds(2 * plane, 2)]
        push_plane(here, ref, ref, line_r.at[plane, h], device_at(way))

    def got_line(plane, h):
        got(line[h].at[pl.ds(2 * plane, 2)], line_r.at[plane, h])

    taken = [set() for _ in range(PLANES)]

    def made(here, plane, h):
        taken[here].add((plane, h))
        with mark(f"attend{plane}_{h}"):
            attend(here, plane, h)
        if here < PLANES - 1:
            send_line(here, 1, plane, h)
        if here > 0:
            send_line(here, -1, plane, h)

    def pass_on(here, way, plane, h):
        with mark(f"pass{plane}_{h}"):
            taken[here].add((plane, h))
            got_line(plane, h)
            send_line(here, way, plane, h)

    def steps_0(step):
        if step == 0:
            for kind, h in low_order:
                with mark(f"own{kind}_{h}"):
                    own(kind, h)
                if kind == 0:
                    send_part(0, 1, 0, h, yo)
                else:
                    made(0, 0, h)

    def steps_1(step):
        def first(h):
            with mark(f"own0_{h}"):
                own(0, h)
            send_part(1, 1, 0, h, yo)

        def home(h):
            with mark(f"own1_{h}"):
                own(1, h)
                got_kv(below, h)
            if h == STAY_HEAD:
                send_kv(1, 1, below, farther, h)
            made(1, 1, h)

        def lower(h):
            with mark(f"lower{h}"):
                got_above(h)
            made(1, 2, h)

        if step == 0:
            first(3)
            first(0)
            home(3)
            home(0)
            first(1)
            lower(0)
            pass_on(1, 1, 0, 3)
            pass_on(1, 1, 0, 0)
            first(2)
            home(1)
            lower(1)
            pass_on(1, -1, 3, 0)
        if step == 1:
            pass_on(1, 1, 0, 1)
            home(2)
            pass_on(1, 1, 0, 2)
            lower(2)
            pass_on(1, -1, 3, 1)
        if step == 3:
            pass_on(1, -1, 2, 3)
            pass_on(1, -1, 3, 3)
        if step == 4:
            pass_on(1, -1, 3, 2)

    def steps_2(step):
        def first(h):
            with mark(f"own0_{h}"):
                own(0, h)
            send_part(2, 1 if h == STAY_HEAD else -1, 0, h, yo)

        def second(h):
            with mark(f"own1_{h}"):
                own(1, h)
            if h != STAY_HEAD:
                send_part(2, -1, 1, h, yo)

        def lower(h):
            with mark(f"lower{h}"):
                got_above(h)
                got_kv(below, h)
            made(2, 3, h)

        if step == 0:
            first(0)
            second(0)
            send_home(2, -1, 2, (0, 1))
            first(3)
            first(1)
            with mark("below3"):
                got_kv(below, 3)
            send_kv(2, 1, below, farther, 3)
            second(1)
            lower(0)
            second(3)
            first(2)
            with mark("farther3"):
                got_kv(farther, 3)
            second(2)
            made(2, 2, 3)
            pass_on(2, 1, 1, 3)
            lower(1)
            pass_on(2, -1, 3, 3)
            pass_on(2, 1, 1, 0)
            pass_on(2, 1, 0, 3)
        if step == 1:
            pass_on(2, 1, 2, 0)
            pass_on(2, 1, 0, 0)
        if step == 2:
            lower(2)
            pass_on(2, 1, 1, 1)
            pass_on(2, 1, 2, 1)
        if step == 3:
            pass_on(2, 1, 0, 1)
        if step == 4:
            pass_on(2, 1, 1, 2)
            pass_on(2, 1, 0, 2)
            pass_on(2, 1, 2, 2)

    def steps_3(step):
        if step == 0:
            for kind, h in high_order:
                with mark(f"own{kind}_{h}"):
                    own(kind, h)
                if h != STAY_HEAD:
                    send_part(3, -1, kind, h, yo)
                    if (kind, h) == (1, 0):
                        send_home(3, -1, 2, (0, 1))
                elif kind == 1:
                    with mark("below3"):
                        got_kv(below, 3)
                        got_kv(farther, 3)
                    made(3, 3, 3)

    def early(plane):
        if plane < 2:
            for h in (3, 0, 1, 2):
                send_home(plane, 1, h)
        else:
            for h in (0, 1):
                send_home(plane, -1, h, (0, 1))
            if plane == 2:
                send_home(plane, 1, STAY_HEAD)

    for plane in range(PLANES):
        pl.when(z == plane)(lambda: early(plane))

    def planes(step):
        for plane, steps in enumerate((steps_0, steps_1, steps_2, steps_3)):

            @pl.when(z == plane)
            def _():
                steps(step)

    def collect(order, pos):
        h = order[pos]
        for plane in range(PLANES):
            if orders[plane // 2][pos] != h:
                continue

            @pl.when(z == plane)
            def _():
                for other in range(PLANES):
                    if (other, h) not in taken[plane]:
                        taken[plane].add((other, h))
                        got_line(other, h)

    high = jnp.where(z < 2, 0, 1)
    orders = ((0, 1, 3, 2), (3, 0, 1, 2))
    heads_at = [low + high * (up - low) for low, up in zip(*orders)]
    ends = len(heads_at) - 1

    def groups_of(pos):
        return [pl.ds(g, 1) for g in range(GROUPS)] if pos == ends else [pl.ds(0, GROUPS)]

    def feature_at(pos, g):
        return pos + g.start

    def feature(n, py, pt, pos, g, device, src=None):
        ref = x_buf.at[py, pt, heads_at[pos], g]
        push(ref if src is None else src, ref, feat_r.at[lot_of[n], feature_at(pos, g)], device)

    lot_of = (0, 0, 1, 2, 0, 3, 3)
    arrivals = (
        (y, tc),
        (y, tx),
        (y, txc),
        (yo, t),
        (yo, tc),
        (yo, tx),
        (yo, txc),
    )

    def take(n, pos, g):
        py, pt = arrivals[n]
        got(x_buf.at[py, pt, heads_at[pos], g], feat_r.at[lot_of[n], feature_at(pos, g)])

    def choose(h, g):
        for r in range(most):
            at = pl.ds(r * group_rows, group_rows)
            for ref, side in ((x_buf.at[y, t, h], c), (x_other.at[h], co)):
                block = line[h][chosen[r], side]
                for i in range(GROUPS):
                    if g.start <= i < g.start + g.size:
                        ref[i, at] = block[i * group_rows : (i + 1) * group_rows]

    def gather(pos):
        with mark(f"collect{pos}"):
            for order in orders:
                if order is orders[0] or order[pos] != orders[0][pos]:
                    collect(order, pos)

    def first_stage(pos, lots=None):
        for g in lots or groups_of(pos):
            if orders[0][pos] == orders[1][pos]:
                choose(orders[0][pos], g)
            else:
                pl.when(z < 2)(lambda: choose(orders[0][pos], g))
                pl.when(z >= 2)(lambda: choose(orders[1][pos], g))
            other = x_other.at[heads_at[pos], g]
            feature(3, y, t, pos, g, dev_y)
            feature(2, y, t, pos, g, dev_xc, other)
            feature(1, y, t, pos, g, dev_x)
            feature(4, y, t, pos, g, dev_yc, other)
            feature(0, y, t, pos, g, dev_c, other)

    def second_stage(pos, g):
        take(3, pos, g)
        feature(5, yo, t, pos, g, dev_x)
        take(2, pos, g)
        feature(6, y, txc, pos, g, dev_y)

    def near(pos, g):
        wait_for(3 * size_of(x_buf.at[y, t, 0, g]), feat_r.at[0, feature_at(pos, g)])

    def far(pos, g):
        wait_for(2 * size_of(x_buf.at[y, t, 0, g]), feat_r.at[3, feature_at(pos, g)])

    def expert_parts(parts, pos, g):
        depth = g.size * most * group_rows
        left, right = [], []
        square = square_buf[g].reshape(depth, 1)
        for py, pt in parts:
            start = pl.multiple_of((2 * pt + py) * half + heads_at[pos] * HEAD_DIM, HEAD_DIM)
            value = x_buf[py, pt, heads_at[pos], g].reshape(depth, HEAD_DIM).astype(F32)
            square = square + jnp.sum(value * value, axis=1, keepdims=True)
            left.append((value * gain_ref[:, pl.ds(start, HEAD_DIM)]).astype(BF16))
            right.append(
                jnp.concatenate(
                    [w_buf[i, pl.ds(start, HEAD_DIM), :] for i in range(4)], axis=1
                )
            )
        square_buf[g] = square.reshape(g.size, most * group_rows, 1)
        acc_buf[g] += jnp.dot(
            jnp.concatenate(left, axis=1),
            jnp.concatenate(right, axis=0),
            preferred_element_type=F32,
        ).reshape(g.size, most * group_rows, 4 * units)

    every_part = [(y, t)] + list(arrivals)

    g0, g1 = groups_of(ends)
    both = groups_of(0)[0]
    planes(0)
    weights = (
        (gate_ref.at[0], w_buf.at[c]),
        (up_ref.at[0], w_buf.at[2 + c]),
        (down_ref.at[0], d_buf.at[c]),
    )
    for src, dst in weights:
        pltpu.make_async_copy(src, dst, weight_s.at[0]).start()
        push(src, dst, weight_r.at[0], dev_c)

    gather(0)
    first_stage(0)
    planes(1)
    gather(1)
    first_stage(1)
    planes(2)
    with mark("second0"):
        second_stage(0, both)
    planes(3)
    gather(2)
    first_stage(2)
    with mark("second1"):
        second_stage(1, both)
    planes(4)
    gather(3)
    first_stage(3, [g0])
    with mark("second2"):
        second_stage(2, both)
    first_stage(3, [g1])
    acc_buf[...] = jnp.zeros_like(acc_buf)
    square_buf[...] = jnp.zeros_like(square_buf)
    with mark("weights"):
        every = w_buf.at[pl.ds(0, len(weights))]
        loaded(every, weight_s.at[0])
        got(every, weight_r.at[0])

    def whole(pos):
        with mark(f"feat{pos}"):
            near(pos, both)
            far(pos, both)
        with mark(f"expert{pos}"):
            expert_parts(every_part, pos, both)

    whole(0)
    with mark("secondL0"):
        second_stage(ends, g0)
    with mark("secondL1"):
        second_stage(ends, g1)
    whole(1)
    whole(2)
    for g in (g0, g1):
        with mark(f"nearL{g.start}"):
            near(ends, g)
        with mark(f"farL{g.start}"):
            far(ends, g)
        with mark(f"expertL{g.start}"):
            expert_parts(every_part, ends, g)
            i = g.start
            scale = lax.rsqrt(square_buf[i] * (1.0 / features) + epsilon)
            gate_val = acc_buf[i, :, pl.ds(0, 2 * units)] * scale
            up_val = acc_buf[i, :, pl.ds(2 * units, 2 * units)] * scale
            hid_buf[x, i] = (gate_val / (1.0 + jnp.exp(-gate_val)) * up_val).astype(BF16)
        push(hid_buf.at[x, i], hid_buf.at[x, i], hid_r.at[i], dev_x)

    wide = half // SPAN
    pieces = [(s, j) for s in range(2) for j in range(wide)]

    def chunk(i, s, j):
        return (i * 2 + s) * wide + j

    pair = 2 * SPAN

    def branch(i, s, which, j):
        hidden = jnp.concatenate([hid_buf[n, i] for n in range(2)], axis=1)
        at = pl.ds(pl.multiple_of(which * half + j * pair, pair), pair)
        weight = d_buf[c if s == 0 else co, :, at]
        value = jnp.dot(hidden, weight, preferred_element_type=F32).astype(BF16)
        return [(chunk(i, s, 2 * j + m), value[:, m * SPAN : (m + 1) * SPAN]) for m in range(2)]

    def down(i):
        with mark(f"hid{i}"):
            got(hid_buf.at[xo, i], hid_r.at[i])
        with mark(f"down{i}"):
            doubles = [(s, j) for s in range(2) for j in range(wide // 2)]
            for s, j in doubles:
                for k, value in branch(i, s, yo, j):
                    b_out[k] = value
                    push(b_out.at[k], b_in.at[k], branch_r.at[k], dev_y)
            for s, j in doubles:
                for m, (k, value) in enumerate(branch(i, s, y, j)):
                    stream = x_buf[y, t if s == 0 else tc, 2 * j + m, i]
                    part[k] = stream.astype(F32) + value.astype(F32)

    def blend(i, s, j):
        k = chunk(i, s, j)
        with mark(f"blend{k}"):
            got(b_in.at[k], branch_r.at[k])
            total = part[k] + b_in[k].astype(F32)
            mix[k][...] = total.astype(BF16).reshape(most, group_rows, SPAN)
        for plane, device in ((0, dev_up), (PLANES - 1, dev_dn)):

            @pl.when(z == plane)
            def _():
                push_plane(plane, mix[k], end_in[k], end_r.at[k], device)

    def pick(flag, a, b):
        mask = jnp.full(a.shape, flag.astype(jnp.int32), jnp.int32) > 0
        return jnp.where(mask, a.astype(F32), b.astype(F32)).astype(BF16)

    def give(here, way, k, d, other):
        out, arrived = (up_out, up_in) if way == 0 else (dn_out, dn_in)
        for n in range(2):
            b = 2 * d + n
            out[k, d, n] = pick(expert[b] == here, mix[k][slot[b]], other(b, n))
        push_plane(
            here,
            out.at[k, d],
            arrived.at[k, d],
            ret_r.at[d % 2, k],
            dev_up if way == 0 else dev_dn,
        )

    def turn_in(i, s, j):
        k = chunk(i, s, j)
        for here, way, targets in ((1, 0, (3, 2)), (2, 1, (0, 1))):

            @pl.when(z == here)
            def _():
                with mark(f"turn{k}"):
                    got(end_in[k], end_r.at[k])
                for d in targets:
                    give(here, way, k, d, lambda b, n: end_in[k][slot[b]])

    def carry(i, s, j):
        k = chunk(i, s, j)
        for here, way, d, arrived in ((2, 0, 3, up_in), (1, 1, 0, dn_in)):

            @pl.when(z == here)
            def _():
                with mark(f"carry{k}"):
                    got(arrived.at[k, d], ret_r.at[d % 2, k])
                give(here, way, k, d, lambda b, n: arrived[k, d, n])

    def target(side, i, which, j):
        return out_ref.at[
            pl.ds(pl.multiple_of(side * core_rows + i * group_rows, group_rows), group_rows),
            pl.ds(pl.multiple_of(which * half + j * SPAN, SPAN), SPAN),
        ]

    def arrive(i, s, j, d):
        k = chunk(i, s, j)

        @pl.when(z == d)
        def _():
            with mark(f"arrive{k}"):
                if d > 1:
                    got(up_in.at[k, d], ret_r.at[d % 2, k])
                if d < PLANES - 2:
                    got(dn_in.at[k, d], ret_r.at[d % 2, k])
            for n in range(2):
                b = 2 * d + n
                value = mix[k][slot[b]]
                if d > 0:
                    lower = up_in[k, d, n] if d > 1 else end_in[k][slot[b]]
                    value = pick(expert[b] < d, lower, value)
                if d < PLANES - 1:
                    higher = dn_in[k, d, n] if d < PLANES - 2 else end_in[k][slot[b]]
                    value = pick(expert[b] > d, higher, value)
                fin[k, n] = value
            mine = target(c, i, y, j)
            device = dev_y if s == 0 else dev_yc
            push(fin.at[k, yo], mine, last_r.at[0], device, final_lot)
            if s == 0:
                mine[...] = fin[k, y]
            else:
                push(fin.at[k, y], mine, last_r.at[0], dev_c, final_lot)

    def arrive_end(i, s, j):
        arrive(i, s, j, 0)
        arrive(i, s, j, PLANES - 1)

    def arrive_middle(i, s, j):
        arrive(i, s, j, 1)
        arrive(i, s, j, 2)

    every = [(i, s, j) for i in range(GROUPS) for s, j in pieces]
    for i in range(GROUPS):
        down(i)
    stages = ((0, blend), (4, turn_in), (9, carry), (12, arrive_middle), (16, arrive_end))
    for n in range(len(every) + stages[-1][0]):
        for lag, stage in stages:
            if 0 <= n - lag < len(every):
                stage(*every[n - lag])
    with mark("lastwait"):
        wait_for(3 * size_of(out_ref) // 4, last_r.at[0])

    def all_sent(sem, amount):
        if amount:
            ref = w_buf.at[0, pl.ds(0, amount // (2 * units))]
            remote(ref, ref, sem, hid_r.at[0], dev_y).wait_send()

    with mark("drain"):
        for lot, amount in enumerate(all_lots):
            all_sent(sent.at[lot], amount)
        all_sent(sent.at[final_lot], 3 * size_of(out_ref) // 4)
        for plane in range(PLANES):

            @pl.when(z == plane)
            def _():
                for lot, amount in enumerate(plane_lots[plane]):
                    all_sent(plane_sent.at[lot], amount)


def local(
    queries, keys, values, residual_in, norm_gain, routing, gate_weight, up_weight, down_weight
):
    seq_count = lax.axis_size("seq")
    tp_count = lax.axis_size("tp")
    rows, width = queries.shape
    units = gate_weight.shape[2]
    planes = seq_count // 2
    fits = (
        tp_count == 4
        and seq_count == 2 * PLANES
        and rows == BLOCK
        and WINDOW == 4 * rows
        and units == 128
        and width == 8 * HEAD_DIM
    )
    if not fits:
        return local_general(
            queries,
            keys,
            values,
            residual_in,
            norm_gain,
            routing,
            gate_weight,
            up_weight,
            down_weight,
        )
    half = width // 2
    heads = half // HEAD_DIM
    most = min(2 * seq_count // planes, seq_count - planes + 1)
    core_rows = rows // 2
    group_rows = core_rows // GROUPS
    wide = half // SPAN
    chunks = GROUPS * 2 * wide
    vmem = pl.BlockSpec(memory_space=pltpu.VMEM)
    anywhere = pl.BlockSpec(memory_space=pltpu.MemorySpace.HBM)
    dma = pltpu.SemaphoreType.DMA

    def room(*shape, kind=BF16):
        return pltpu.VMEM(shape, kind)

    scratch = (
        room(4, heads, 2, 2, rows, HEAD_DIM),
        room(2, heads, 2, 2, rows, HEAD_DIM),
        room(2, heads, 2, rows, HEAD_DIM),
        [room(2 * planes, 2, core_rows, HEAD_DIM) for _ in range(heads)],
        room(2, tp_count, heads, GROUPS, most * group_rows, HEAD_DIM),
        room(heads, GROUPS, most * group_rows, HEAD_DIM),
        room(4, gate_weight.shape[1], units),
        room(2, down_weight.shape[1], width),
        room(GROUPS, most * group_rows, 4 * units, kind=F32),
        room(GROUPS, most * group_rows, 1, kind=F32),
        room(2, GROUPS, most * group_rows, 2 * units),
        room(chunks, most * group_rows, SPAN),
        room(chunks, most * group_rows, SPAN),
        room(chunks, most * group_rows, SPAN, kind=F32),
        [room(most, group_rows, SPAN) for _ in range(chunks)],
        [room(most, group_rows, SPAN) for _ in range(chunks)],
        room(chunks, planes, 2, group_rows, SPAN),
        room(chunks, planes, 2, group_rows, SPAN),
        room(chunks, planes, 2, group_rows, SPAN),
        room(chunks, planes, 2, group_rows, SPAN),
        room(chunks, 2, group_rows, SPAN),
        dma((1,)),
        dma((1,)),
        dma((1,)),
        dma((2, heads)),
        dma((2 * heads + 1,)),
        dma((planes, heads)),
        dma((4, heads + GROUPS - 1)),
        dma((1,)),
        dma((GROUPS,)),
        dma((chunks,)),
        dma((chunks,)),
        dma((2, chunks)),
        dma((1,)),
        dma((8,)),
        dma((4,)),
    )
    flat, tree = jax.tree.flatten(scratch, is_leaf=lambda leaf: not isinstance(leaf, (list, tuple)))

    def kernel(*refs):
        layer_kernel(most, refs[:9], refs[9], jax.tree.unflatten(tree, refs[10:]))

    return pl.pallas_call(
        kernel,
        name="layer",
        out_shape=jax.ShapeDtypeStruct((rows, width), BF16),
        in_specs=[pl.BlockSpec(memory_space=pltpu.SMEM)]
        + [anywhere] * 4
        + [vmem]
        + [anywhere] * 3,
        out_specs=vmem,
        scratch_shapes=flat,
        compiler_params=pltpu.CompilerParams(
            collective_id=0, has_side_effects=True, vmem_limit_bytes=67043328
        ),
    )(
        routing.reshape(-1),
        queries,
        keys,
        values,
        residual_in,
        norm_gain.reshape(1, -1),
        gate_weight,
        up_weight,
        down_weight,
    )


def solution(mesh):
    in_specs = (
        P("seq", "tp"),
        P("seq", "tp"),
        P("seq", "tp"),
        P("seq", "tp"),
        P(),
        P(),
        P("seq", None, "tp"),
        P("seq", None, "tp"),
        P("seq", None, "tp"),
    )
    out_specs = P("seq", "tp")
    return jax.shard_map(local, mesh=mesh, in_specs=in_specs, out_specs=out_specs, check_vma=False)
```

```python
import contextlib
import math

import jax
import jax.numpy as jnp
from jax import lax
from jax.experimental import pallas as pl
from jax.experimental.pallas import tpu as pltpu
from jax.sharding import PartitionSpec as P

HEAD_DIM = 128
BLOCK = 128
WINDOW = 512


epsilon = 1e-05
masked_score = -1e30


def shifted(block, axis, distance):
    devices = range(lax.axis_size(axis))
    route = [(i - distance, i) for i in devices if i - distance in devices]
    return lax.ppermute(block, axis, route)


def local_general(
    queries, keys, values, residual_in, norm_gain, routing, gate_weight, up_weight, down_weight
):
    seq_count = lax.axis_size("seq")
    seq_place = lax.axis_index("seq")
    tok_rows = queries.shape[0]
    feat_width = queries.shape[1]
    head_count = feat_width // HEAD_DIM
    prior_count = (WINDOW - 1) // tok_rows + 1
    earlier_keys = []
    earlier_values = []
    for distance in range(1, prior_count + 1):
        moved_keys, moved_values = shifted((keys, values), "seq", distance)
        earlier_keys.insert(0, moved_keys)
        earlier_values.insert(0, moved_values)
    key_all = jnp.concatenate(earlier_keys + [keys], axis=0).reshape(-1, head_count, HEAD_DIM)
    value_all = jnp.concatenate(earlier_values + [values], axis=0).reshape(-1, head_count, HEAD_DIM)
    query_heads = queries.reshape(tok_rows, head_count, HEAD_DIM)
    query_pos = seq_place * tok_rows + jnp.arange(tok_rows, dtype=jnp.int32)
    key_pos = (
        seq_place * tok_rows
        - prior_count * tok_rows
        + jnp.arange((prior_count + 1) * tok_rows, dtype=jnp.int32)
    )
    visible = (
        (key_pos[None, :] >= 0)
        & (key_pos[None, :] <= query_pos[:, None])
        & (key_pos[None, :] > query_pos[:, None] - WINDOW)
    )
    scores = jnp.einsum(
        "qhd,khd->hqk", query_heads, key_all, preferred_element_type=jnp.float32
    ) * (1.0 / math.sqrt(HEAD_DIM))
    scores = jnp.where(visible[None], scores, masked_score)
    top_score = jnp.max(scores, axis=2, keepdims=True)
    expo = jnp.exp(scores - top_score)
    weights_soft = (expo / jnp.sum(expo, axis=2, keepdims=True)).astype(jnp.bfloat16)
    attended = jnp.einsum(
        "hqk,khd->qhd", weights_soft, value_all, preferred_element_type=jnp.float32
    ).reshape(tok_rows, feat_width)
    stream = (residual_in.astype(jnp.float32) + attended).astype(jnp.bfloat16)
    send_width = stream.shape[1]
    blocks_dev = tok_rows // BLOCK
    piece_rows = BLOCK // seq_count
    spread_in = stream.reshape(blocks_dev, seq_count, piece_rows, send_width)
    spread_out = lax.all_to_all(spread_in, "seq", split_axis=1, concat_axis=0, tiled=True)
    block_count = blocks_dev * seq_count
    spread_rows = spread_out.reshape(block_count, piece_rows, send_width)
    expert_ids = routing[:, 0]
    expert_count = seq_count // 2
    most_blocks = min(2 * block_count // expert_count, block_count - expert_count + 1)
    order_index = jnp.arange(block_count, dtype=jnp.int32)
    same_expert = expert_ids[None, :] == expert_ids[:, None]
    rank_of = jnp.sum(same_expert & (order_index[None, :] < order_index[:, None]), axis=1)
    expert_range = jnp.arange(expert_count, dtype=jnp.int32)
    slot_range = jnp.arange(most_blocks, dtype=jnp.int32)
    selector = (
        (expert_ids[None, None, :] == expert_range[:, None, None])
        & (rank_of[None, None, :] == slot_range[None, :, None])
    ).astype(jnp.bfloat16)
    picked = jnp.einsum(
        "erb,bqf->erqf", selector, spread_rows, preferred_element_type=jnp.float32
    ).astype(jnp.bfloat16)
    outgoing = jnp.broadcast_to(
        picked[:, None], (expert_count, 2, most_blocks, piece_rows, send_width)
    )
    outgoing = outgoing.reshape(seq_count, most_blocks, piece_rows, send_width)
    features_full = lax.all_gather(
        lax.all_to_all(outgoing, "seq", split_axis=0, concat_axis=0, tiled=True),
        "tp",
        axis=3,
        tiled=True,
    )
    source_count = features_full.shape[0]
    slot_count = features_full.shape[1]
    stream_f32 = features_full.astype(jnp.float32)
    mean_square = jnp.mean(stream_f32 * stream_f32, axis=3, keepdims=True)
    normed = (stream_f32 * lax.rsqrt(mean_square + epsilon) * norm_gain).astype(jnp.bfloat16)
    normed = normed.reshape(-1, normed.shape[3])
    gate_val = jnp.dot(normed, gate_weight[0], preferred_element_type=jnp.float32)
    up_val = jnp.dot(normed, up_weight[0], preferred_element_type=jnp.float32)
    hidden = (jax.nn.silu(gate_val) * up_val).astype(jnp.bfloat16)
    hidden_half = lax.all_gather(hidden, "tp", axis=1, tiled=True)
    partial_value = jnp.dot(hidden_half, down_weight[0], preferred_element_type=jnp.float32).astype(
        jnp.bfloat16
    )
    partial_value = partial_value.reshape(source_count, slot_count, piece_rows, feat_width)
    returned = lax.all_to_all(partial_value, "seq", split_axis=0, concat_axis=0, tiled=True)
    returned = returned.reshape(expert_count, 2, most_blocks, piece_rows * feat_width)
    combined = jnp.einsum("erb,epry->pby", selector, returned, preferred_element_type=jnp.float32)
    residual_rows = spread_rows
    residual_rows = residual_rows.reshape(block_count, piece_rows * feat_width).astype(jnp.float32)
    finished = (residual_rows + combined[0] + combined[1]).astype(jnp.bfloat16)
    finished = finished.reshape(seq_count, blocks_dev, piece_rows, feat_width)
    restored = lax.all_to_all(finished, "seq", split_axis=0, concat_axis=2, tiled=True)
    return restored.reshape(tok_rows, feat_width)


BF16 = jnp.bfloat16
F32 = jnp.float32
PLANES = 4
GROUPS = 2
SPAN = HEAD_DIM
STAY_HEAD = 3


def mark(name):
    return contextlib.nullcontext()


def remote(src, dst, send_sem, recv_sem, device):
    return pltpu.make_async_remote_copy(
        src_ref=src,
        dst_ref=dst,
        send_sem=send_sem,
        recv_sem=recv_sem,
        device_id=device,
        device_id_type=pl.DeviceIdType.MESH,
    )


def size_of(ref):
    return math.prod(ref.shape) * ref.dtype.itemsize


def layer_kernel(most, arguments, out_ref, scratch):
    routing_ref, q_ref, k_ref, v_ref, r_ref, gain_ref, gate_ref, up_ref, down_ref = arguments
    (
        kv_buf,
        qr_buf,
        away,
        line,
        x_buf,
        x_other,
        w_buf,
        d_buf,
        acc_buf,
        square_buf,
        hid_buf,
        b_out,
        b_in,
        part,
        mix,
        end_in,
        up_out,
        up_in,
        dn_out,
        dn_in,
        fin,
        own_s,
        away_s,
        weight_s,
        swap_r,
        kv_r,
        line_r,
        feat_r,
        weight_r,
        hid_r,
        branch_r,
        end_r,
        ret_r,
        last_r,
        sent,
        plane_sent,
    ) = scratch
    rows = q_ref.shape[0]
    half = q_ref.shape[1] // 2
    heads = half // HEAD_DIM
    units = gate_ref.shape[2]
    features = gain_ref.shape[1]
    core_rows = rows // 2
    group_rows = core_rows // GROUPS
    me = lax.axis_index("seq")
    t = lax.axis_index("tp")
    z = me // 2
    y = me % 2
    x = t // 2
    c = t % 2
    yo, xo, co = 1 - y, 1 - x, 1 - c
    tc = 2 * x + co
    tx = 2 * xo + c
    txc = 2 * xo + co
    mate = 2 * z + yo
    dev_y, dev_yc = (mate, t), (mate, tc)
    dev_x, dev_xc = (me, tx), (me, txc)
    dev_c = (me, tc)
    dev_up, dev_dn = (me + 2, t), (me - 2, t)
    has_up, has_dn = z < PLANES - 1, z > 0

    limit = size_of(w_buf.at[0])
    all_lots = [0]
    plane_lots = [[0] for _ in range(PLANES)]

    def lot_for(lots, ref):
        if lots[-1] + size_of(ref) > limit:
            lots.append(0)
        lots[-1] += size_of(ref)
        return len(lots) - 1

    final_lot = sent.shape[0] - 1
    relay_lot = final_lot - 1

    def push(src, dst, recv_sem, device, lot=None):
        lot = lot_for(all_lots, src) if lot is None else lot
        remote(src, dst, sent.at[lot], recv_sem, device).start()

    def push_plane(plane, src, dst, recv_sem, device):
        lot = lot_for(plane_lots[plane], src)
        remote(src, dst, plane_sent.at[lot], recv_sem, device).start()

    def got(ref, recv_sem):
        remote(ref, ref, sent.at[0], recv_sem, dev_y).wait_recv()

    def wait_for(amount, recv_sem):
        got(w_buf.at[0, pl.ds(0, amount // (2 * units))], recv_sem)

    def loaded(ref, sem):
        pltpu.make_async_copy(ref, ref, sem).wait()

    barrier = pltpu.get_barrier_semaphore()

    def greet(device):
        pl.semaphore_signal(
            barrier, inc=1, device_id=device, device_id_type=pl.DeviceIdType.MESH
        )

    for device in (dev_y, dev_yc, dev_c, dev_x, dev_xc):
        greet(device)
    pl.when(has_up)(lambda: greet(dev_up))
    pl.when(has_dn)(lambda: greet(dev_dn))

    def cols(which, h):
        return pl.ds(pl.multiple_of(which * half + h * HEAD_DIM, HEAD_DIM), HEAD_DIM)

    sources = ((k_ref, v_ref), (q_ref, r_ref))

    def place(kind, h, n, block):
        buf = kv_buf if kind == 0 else qr_buf
        return buf.at[0, h, n, block]

    def load_own(kind, h):
        for n, ref in enumerate(sources[kind]):
            pltpu.make_async_copy(
                ref.at[:, cols(y, h)], place(kind, h, n, y), own_s.at[0]
            ).start()

    def load_away(kind, h):
        for n, ref in enumerate(sources[kind]):
            pltpu.make_async_copy(
                ref.at[:, cols(yo, h)], away.at[kind, h, n], away_s.at[0]
            ).start()

    def swap(kind, h):
        buf = kv_buf if kind == 0 else qr_buf
        push(away.at[kind, h], buf.at[0, h, :, y], swap_r.at[kind, h], dev_y)

    def own(kind, h):
        buf = kv_buf if kind == 0 else qr_buf
        got(buf.at[0, h, :, yo], swap_r.at[kind, h])

    for kind in range(2):
        for h in range(heads):
            load_away(kind, h)
    for kind in range(2):
        for h in range(heads):
            load_own(kind, h)

    expert = [routing_ref[b] for b in range(2 * PLANES)]
    slot = []
    for b in range(2 * PLANES):
        count = jnp.int32(0)
        for j in range(b):
            count = count + jnp.where(expert[j] == expert[b], 1, 0)
        slot.append(jnp.minimum(count, most - 1))
    chosen = []
    for r in range(most):
        index = jnp.int32(0)
        for b in range(2 * PLANES):
            index = jnp.where((expert[b] == z) & (slot[b] == r), b, index)
        chosen.append(index)

    with mark("barwait"):
        pl.semaphore_wait(barrier, 5 + jnp.where(has_up, 1, 0) + jnp.where(has_dn, 1, 0))

    low_order = ((0, 3), (0, 0), (1, 3), (1, 0), (0, 1), (1, 1), (0, 2), (1, 2))
    high_order = ((0, 0), (1, 0), (0, 3), (0, 1), (1, 1), (1, 3), (0, 2), (1, 2))

    with mark("away"):
        loaded(away, away_s.at[0])

    @pl.when(z < 2)
    def _():
        for kind, h in low_order:
            swap(kind, h)

    all_lots[:] = [0]

    @pl.when(z >= 2)
    def _():
        for kind, h in high_order:
            swap(kind, h)

    with mark("ownwait"):
        loaded(away, own_s.at[0])
    row_at = lax.broadcasted_iota(jnp.int32, (rows, rows), 0)
    col_at = lax.broadcasted_iota(jnp.int32, (rows, rows), 1)
    below, above, farther = 1, 2, 3

    def attend(here, plane, h):
        side = 0 if plane == here else 1
        keep = {here: 0, here - 1: below, here + 1: above, here - 2: farther}
        reach = WINDOW // rows
        for n in range(2):
            block = 2 * plane + n
            seen = [
                (back, keep[(block - back) // 2], (block - back) % 2)
                for back in range(reach + 1)
                if block >= back
            ]
            query = qr_buf[side, h, 0, n]
            parts = []
            for back, at, odd in seen:
                score = lax.dot_general(
                    query,
                    kv_buf[at, h, 0, odd],
                    (((1,), (1,)), ((), ())),
                    preferred_element_type=F32,
                )
                if back == 0:
                    score = jnp.where(col_at <= row_at, score, masked_score)
                if back == reach:
                    score = jnp.where(col_at > row_at, score, masked_score)
                parts.append(score)
            top = parts[0]
            for score in parts[1:]:
                top = jnp.maximum(top, score)
            top = jnp.max(top, axis=1, keepdims=True)
            parts = [jnp.exp((score - top) * (1.0 / math.sqrt(HEAD_DIM))) for score in parts]
            total = parts[0]
            for score in parts[1:]:
                total = total + score
            share = 1.0 / jnp.sum(total, axis=1, keepdims=True)
            attended = jnp.dot(
                jnp.concatenate([(score * share).astype(BF16) for score in parts], axis=1),
                jnp.concatenate([kv_buf[at, h, 1, odd] for _, at, odd in seen], axis=0),
                preferred_element_type=F32,
            )
            stream = (qr_buf[side, h, 1, n].astype(F32) + attended).astype(BF16)
            line[h][block] = stream.reshape(2, core_rows, HEAD_DIM)

    def device_at(way):
        return dev_up if way > 0 else dev_dn

    def kv_sem(at, h):
        return kv_r.at[2 * heads if at == farther else (at - 1) * heads + h]

    def send_kv(here, way, src, dst, h):
        push_plane(here, kv_buf.at[src, h], kv_buf.at[dst, h], kv_sem(dst, h), device_at(way))

    def got_kv(at, h):
        got(kv_buf.at[at, h], kv_sem(at, h))

    def send_part(here, way, kind, h, block):
        at = below if way > 0 else above
        buf, to = (kv_buf, at) if kind == 0 else (qr_buf, 1)
        push_plane(
            here, buf.at[0, h, :, block], buf.at[to, h, :, block], kv_sem(at, h), device_at(way)
        )

    def send_home(here, way, h, kinds=(0,)):
        for kind in kinds:
            send_part(here, way, kind, h, y)

    def got_above(h):
        wait_for(size_of(kv_buf.at[0, h]) + size_of(qr_buf.at[0, h]), kv_sem(above, h))

    def send_line(here, way, plane, h):
        ref = line[h].at[pl.ds(2 * plane, 2)]
        push_plane(here, ref, ref, line_r.at[plane, h], device_at(way))

    def got_line(plane, h):
        got(line[h].at[pl.ds(2 * plane, 2)], line_r.at[plane, h])

    taken = [set() for _ in range(PLANES)]

    def made(here, plane, h, hold=False):
        taken[here].add((plane, h))
        with mark(f"attend{plane}_{h}"):
            attend(here, plane, h)
        if here < PLANES - 1 and not hold:
            send_line(here, 1, plane, h)
        if here > 0:
            send_line(here, -1, plane, h)

    def pass_on(here, way, plane, h):
        with mark(f"pass{plane}_{h}"):
            taken[here].add((plane, h))
            got_line(plane, h)
            send_line(here, way, plane, h)

    def steps_0(step):
        if step == 0:
            for kind, h in low_order:
                with mark(f"own{kind}_{h}"):
                    own(kind, h)
                if kind == 0:
                    send_part(0, 1, 0, h, yo)
                else:
                    made(0, 0, h)

    def steps_1(step):
        def first(h):
            with mark(f"own0_{h}"):
                own(0, h)
            send_part(1, 1, 0, h, yo)

        def home(h):
            with mark(f"own1_{h}"):
                own(1, h)
                got_kv(below, h)
            if h == STAY_HEAD:
                send_kv(1, 1, below, farther, h)
            made(1, 1, h)

        def lower(h):
            with mark(f"lower{h}"):
                got_above(h)
            made(1, 2, h)

        if step == 0:
            first(3)
            first(0)
            home(3)
            home(0)
            first(1)
            lower(0)
            pass_on(1, 1, 0, 3)
            pass_on(1, 1, 0, 0)
            first(2)
            home(1)
            lower(1)
            pass_on(1, -1, 3, 0)
        if step == 1:
            pass_on(1, 1, 0, 1)
            home(2)
            pass_on(1, 1, 0, 2)
            pass_on(1, -1, 3, 1)
        if step == 2:
            pass_on(1, -1, 2, 3)
            pass_on(1, -1, 3, 3)
        if step == 3:
            lower(2)
        if step == 4:
            pass_on(1, -1, 3, 2)

    def steps_2(step):
        def first(h):
            with mark(f"own0_{h}"):
                own(0, h)
            send_part(2, 1 if h == STAY_HEAD else -1, 0, h, yo)

        def second(h):
            with mark(f"own1_{h}"):
                own(1, h)
            if h != STAY_HEAD:
                send_part(2, -1, 1, h, yo)

        def lower(h, hold=False):
            with mark(f"lower{h}"):
                got_above(h)
                got_kv(below, h)
            made(2, 3, h, hold)

        if step == 0:
            first(0)
            second(0)
            send_home(2, -1, 2, (0, 1))
            first(3)
            first(1)
            with mark("below3"):
                got_kv(below, 3)
            send_kv(2, 1, below, farther, 3)
            second(1)
            lower(0)
            second(3)
            with mark("farther3"):
                got_kv(farther, 3)
            made(2, 2, 3)
            pass_on(2, 1, 1, 3)
            lower(1)
            pass_on(2, -1, 3, 3)
            first(2)
            second(2)
            pass_on(2, 1, 1, 0)
            pass_on(2, 1, 0, 3)
        if step == 1:
            pass_on(2, 1, 2, 0)
            pass_on(2, 1, 0, 0)
        if step == 2:
            lower(2, True)
            pass_on(2, 1, 1, 1)
            pass_on(2, 1, 2, 1)
        if step == 3:
            pass_on(2, 1, 0, 1)
            send_line(2, 1, 3, 2)
        if step == 4:
            pass_on(2, 1, 1, 2)
            pass_on(2, 1, 0, 2)
            pass_on(2, 1, 2, 2)

    def steps_3(step):
        if step == 0:
            for kind, h in high_order:
                with mark(f"own{kind}_{h}"):
                    own(kind, h)
                if h != STAY_HEAD:
                    send_part(3, -1, kind, h, yo)
                    if (kind, h) == (1, 0):
                        send_home(3, -1, 2, (0, 1))
                elif kind == 1:
                    with mark("below3"):
                        got_kv(below, 3)
                        got_kv(farther, 3)
                    made(3, 3, 3)

    def early(plane):
        if plane < 2:
            for h in (3, 0, 1, 2):
                send_home(plane, 1, h)
        else:
            for h in (0, 1):
                send_home(plane, -1, h, (0, 1))
            if plane == 2:
                send_home(plane, 1, STAY_HEAD)

    for plane in range(PLANES):
        pl.when(z == plane)(lambda: early(plane))

    def planes(step):
        for plane, steps in enumerate((steps_0, steps_1, steps_2, steps_3)):

            @pl.when(z == plane)
            def _():
                steps(step)

    def collect(order, pos):
        h = order[pos]
        for plane in range(PLANES):
            if orders[plane // 2][pos] != h:
                continue

            @pl.when(z == plane)
            def _():
                for other in range(PLANES):
                    if (other, h) not in taken[plane]:
                        taken[plane].add((other, h))
                        got_line(other, h)

    high = jnp.where(z < 2, 0, 1)
    orders = ((0, 1, 3, 2), (3, 0, 1, 2))
    heads_at = [low + high * (up - low) for low, up in zip(*orders)]
    ends = len(heads_at) - 1

    def groups_of(pos):
        return [pl.ds(g, 1) for g in range(GROUPS)] if pos == ends else [pl.ds(0, GROUPS)]

    def feature_at(pos, g):
        return pos + g.start

    def feature(n, py, pt, pos, g, device, src=None, lot=None):
        ref = x_buf.at[py, pt, heads_at[pos], g]
        src = ref if src is None else src
        push(src, ref, feat_r.at[lot_of[n], feature_at(pos, g)], device, lot)

    lot_of = (0, 0, 1, 2, 0, 3, 3)
    arrivals = (
        (y, tc),
        (y, tx),
        (y, txc),
        (yo, t),
        (yo, tc),
        (yo, tx),
        (yo, txc),
    )

    def take(n, pos, g):
        py, pt = arrivals[n]
        got(x_buf.at[py, pt, heads_at[pos], g], feat_r.at[lot_of[n], feature_at(pos, g)])

    def choose(h, g):
        for r in range(most):
            at = pl.ds(r * group_rows, group_rows)
            for ref, side in ((x_buf.at[y, t, h], c), (x_other.at[h], co)):
                block = line[h][chosen[r], side]
                for i in range(GROUPS):
                    if g.start <= i < g.start + g.size:
                        ref[i, at] = block[i * group_rows : (i + 1) * group_rows]

    def gather(pos):
        with mark(f"collect{pos}"):
            for order in orders:
                if order is orders[0] or order[pos] != orders[0][pos]:
                    collect(order, pos)

    def first_stage(pos, lots=None):
        for g in lots or groups_of(pos):
            if orders[0][pos] == orders[1][pos]:
                choose(orders[0][pos], g)
            else:
                pl.when(z < 2)(lambda: choose(orders[0][pos], g))
                pl.when(z >= 2)(lambda: choose(orders[1][pos], g))
            other = x_other.at[heads_at[pos], g]
            feature(3, y, t, pos, g, dev_y)
            feature(2, y, t, pos, g, dev_xc, other)
            feature(1, y, t, pos, g, dev_x)
            feature(4, y, t, pos, g, dev_yc, other)
            feature(0, y, t, pos, g, dev_c, other)

    def second_stage(pos, g, lot=None):
        take(3, pos, g)
        feature(5, yo, t, pos, g, dev_x, lot=lot)
        take(2, pos, g)
        feature(6, y, txc, pos, g, dev_y, lot=lot)

    def near(pos, g):
        wait_for(3 * size_of(x_buf.at[y, t, 0, g]), feat_r.at[0, feature_at(pos, g)])

    def far(pos, g):
        wait_for(2 * size_of(x_buf.at[y, t, 0, g]), feat_r.at[3, feature_at(pos, g)])

    def expert_parts(parts, pos, g):
        depth = g.size * most * group_rows
        left, right = [], []
        square = square_buf[g].reshape(depth, 1)
        for py, pt in parts:
            start = pl.multiple_of((2 * pt + py) * half + heads_at[pos] * HEAD_DIM, HEAD_DIM)
            value = x_buf[py, pt, heads_at[pos], g].reshape(depth, HEAD_DIM).astype(F32)
            square = square + jnp.sum(value * value, axis=1, keepdims=True)
            left.append((value * gain_ref[:, pl.ds(start, HEAD_DIM)]).astype(BF16))
            right.append(
                jnp.concatenate(
                    [w_buf[i, pl.ds(start, HEAD_DIM), :] for i in range(4)], axis=1
                )
            )
        square_buf[g] = square.reshape(g.size, most * group_rows, 1)
        acc_buf[g] += jnp.dot(
            jnp.concatenate(left, axis=1),
            jnp.concatenate(right, axis=0),
            preferred_element_type=F32,
        ).reshape(g.size, most * group_rows, 4 * units)

    every_part = [(y, t)] + list(arrivals)

    g0, g1 = groups_of(ends)
    both = groups_of(0)[0]
    planes(0)
    weights = (
        (gate_ref.at[0], w_buf.at[c]),
        (up_ref.at[0], w_buf.at[2 + c]),
        (down_ref.at[0], d_buf.at[c]),
    )
    for src, dst in weights:
        pltpu.make_async_copy(src, dst, weight_s.at[0]).start()
        push(src, dst, weight_r.at[0], dev_c)

    gather(0)
    first_stage(0)
    planes(1)

    @pl.when(z == 0)
    def _():
        with mark("second0"):
            second_stage(0, both, relay_lot)

    gather(1)
    first_stage(1)
    planes(2)

    @pl.when(z > 0)
    def _():
        with mark("second0"):
            second_stage(0, both, relay_lot)

    planes(3)
    gather(2)
    first_stage(2)
    with mark("second1"):
        second_stage(1, both)
    planes(4)
    gather(3)
    first_stage(3, [g0])
    with mark("second2"):
        second_stage(2, both)
    first_stage(3, [g1])
    acc_buf[...] = jnp.zeros_like(acc_buf)
    square_buf[...] = jnp.zeros_like(square_buf)
    with mark("weights"):
        every = w_buf.at[pl.ds(0, len(weights))]
        loaded(every, weight_s.at[0])
        got(every, weight_r.at[0])

    def whole(pos):
        with mark(f"feat{pos}"):
            near(pos, both)
            far(pos, both)
        with mark(f"expert{pos}"):
            expert_parts(every_part, pos, both)

    whole(0)
    with mark("secondL0"):
        second_stage(ends, g0)
    with mark("secondL1"):
        second_stage(ends, g1)
    whole(1)
    whole(2)
    for g in (g0, g1):
        with mark(f"nearL{g.start}"):
            near(ends, g)
        with mark(f"farL{g.start}"):
            far(ends, g)
        with mark(f"expertL{g.start}"):
            expert_parts(every_part, ends, g)
            i = g.start
            scale = lax.rsqrt(square_buf[i] * (1.0 / features) + epsilon)
            gate_val = acc_buf[i, :, pl.ds(0, 2 * units)] * scale
            up_val = acc_buf[i, :, pl.ds(2 * units, 2 * units)] * scale
            hid_buf[x, i] = (gate_val / (1.0 + jnp.exp(-gate_val)) * up_val).astype(BF16)
        push(hid_buf.at[x, i], hid_buf.at[x, i], hid_r.at[i], dev_x)

    wide = half // SPAN
    pieces = [(s, j) for s in range(2) for j in range(wide)]

    def chunk(i, s, j):
        return (i * 2 + s) * wide + j

    pair = 2 * SPAN

    def branch(i, s, which, j):
        hidden = jnp.concatenate([hid_buf[n, i] for n in range(2)], axis=1)
        at = pl.ds(pl.multiple_of(which * half + j * pair, pair), pair)
        weight = d_buf[c if s == 0 else co, :, at]
        value = jnp.dot(hidden, weight, preferred_element_type=F32).astype(BF16)
        return [(chunk(i, s, 2 * j + m), value[:, m * SPAN : (m + 1) * SPAN]) for m in range(2)]

    def down(i):
        with mark(f"hid{i}"):
            got(hid_buf.at[xo, i], hid_r.at[i])
        with mark(f"down{i}"):
            doubles = [(s, j) for s in range(2) for j in range(wide // 2)]
            for s, j in doubles:
                for k, value in branch(i, s, yo, j):
                    b_out[k] = value
                    push(b_out.at[k], b_in.at[k], branch_r.at[k], dev_y)
            for s, j in doubles:
                for m, (k, value) in enumerate(branch(i, s, y, j)):
                    stream = x_buf[y, t if s == 0 else tc, 2 * j + m, i]
                    part[k] = stream.astype(F32) + value.astype(F32)

    def blend(i, s, j):
        k = chunk(i, s, j)
        with mark(f"blend{k}"):
            got(b_in.at[k], branch_r.at[k])
            total = part[k] + b_in[k].astype(F32)
            mix[k][...] = total.astype(BF16).reshape(most, group_rows, SPAN)
        for plane, device in ((0, dev_up), (PLANES - 1, dev_dn)):

            @pl.when(z == plane)
            def _():
                push_plane(plane, mix[k], end_in[k], end_r.at[k], device)

    def pick(flag, a, b):
        mask = jnp.full(a.shape, flag.astype(jnp.int32), jnp.int32) > 0
        return jnp.where(mask, a.astype(F32), b.astype(F32)).astype(BF16)

    def give(here, way, k, d, other):
        out, arrived = (up_out, up_in) if way == 0 else (dn_out, dn_in)
        for n in range(2):
            b = 2 * d + n
            out[k, d, n] = pick(expert[b] == here, mix[k][slot[b]], other(b, n))
        push_plane(
            here,
            out.at[k, d],
            arrived.at[k, d],
            ret_r.at[d % 2, k],
            dev_up if way == 0 else dev_dn,
        )

    def turn_in(i, s, j):
        k = chunk(i, s, j)
        for here, way, targets in ((1, 0, (3, 2)), (2, 1, (0, 1))):

            @pl.when(z == here)
            def _():
                with mark(f"turn{k}"):
                    got(end_in[k], end_r.at[k])
                for d in targets:
                    give(here, way, k, d, lambda b, n: end_in[k][slot[b]])

    def carry(i, s, j):
        k = chunk(i, s, j)
        for here, way, d, arrived in ((2, 0, 3, up_in), (1, 1, 0, dn_in)):

            @pl.when(z == here)
            def _():
                with mark(f"carry{k}"):
                    got(arrived.at[k, d], ret_r.at[d % 2, k])
                give(here, way, k, d, lambda b, n: arrived[k, d, n])

    def target(side, i, which, j):
        return out_ref.at[
            pl.ds(pl.multiple_of(side * core_rows + i * group_rows, group_rows), group_rows),
            pl.ds(pl.multiple_of(which * half + j * SPAN, SPAN), SPAN),
        ]

    def arrive(i, s, j, d):
        k = chunk(i, s, j)

        @pl.when(z == d)
        def _():
            with mark(f"arrive{k}"):
                if d > 1:
                    got(up_in.at[k, d], ret_r.at[d % 2, k])
                if d < PLANES - 2:
                    got(dn_in.at[k, d], ret_r.at[d % 2, k])
            for n in range(2):
                b = 2 * d + n
                value = mix[k][slot[b]]
                if d > 0:
                    lower = up_in[k, d, n] if d > 1 else end_in[k][slot[b]]
                    value = pick(expert[b] < d, lower, value)
                if d < PLANES - 1:
                    higher = dn_in[k, d, n] if d < PLANES - 2 else end_in[k][slot[b]]
                    value = pick(expert[b] > d, higher, value)
                fin[k, n] = value
            mine = target(c, i, y, j)
            device = dev_y if s == 0 else dev_yc
            push(fin.at[k, yo], mine, last_r.at[0], device, final_lot)
            if s == 0:
                mine[...] = fin[k, y]
            else:
                push(fin.at[k, y], mine, last_r.at[0], dev_c, final_lot)

    def arrive_end(i, s, j):
        arrive(i, s, j, 0)
        arrive(i, s, j, PLANES - 1)

    def arrive_middle(i, s, j):
        arrive(i, s, j, 1)
        arrive(i, s, j, 2)

    every = [(i, s, j) for i in range(GROUPS) for s, j in pieces]
    for i in range(GROUPS):
        down(i)
    stages = ((0, blend), (4, turn_in), (9, carry), (12, arrive_middle), (16, arrive_end))
    for n in range(len(every) + stages[-1][0]):
        for lag, stage in stages:
            if 0 <= n - lag < len(every):
                stage(*every[n - lag])
    with mark("lastwait"):
        wait_for(3 * size_of(out_ref) // 4, last_r.at[0])

    def all_sent(sem, amount):
        if amount:
            ref = w_buf.at[0, pl.ds(0, amount // (2 * units))]
            remote(ref, ref, sem, hid_r.at[0], dev_y).wait_send()

    with mark("drain"):
        for lot, amount in enumerate(all_lots):
            all_sent(sent.at[lot], amount)
        all_sent(sent.at[relay_lot], 2 * size_of(x_buf.at[0, 0, 0]))
        all_sent(sent.at[final_lot], 3 * size_of(out_ref) // 4)
        for plane in range(PLANES):

            @pl.when(z == plane)
            def _():
                for lot, amount in enumerate(plane_lots[plane]):
                    all_sent(plane_sent.at[lot], amount)


def local(
    queries, keys, values, residual_in, norm_gain, routing, gate_weight, up_weight, down_weight
):
    seq_count = lax.axis_size("seq")
    tp_count = lax.axis_size("tp")
    rows, width = queries.shape
    units = gate_weight.shape[2]
    planes = seq_count // 2
    fits = (
        tp_count == 4
        and seq_count == 2 * PLANES
        and rows == BLOCK
        and WINDOW == 4 * rows
        and units == 128
        and width == 8 * HEAD_DIM
    )
    if not fits:
        return local_general(
            queries,
            keys,
            values,
            residual_in,
            norm_gain,
            routing,
            gate_weight,
            up_weight,
            down_weight,
        )
    half = width // 2
    heads = half // HEAD_DIM
    most = min(2 * seq_count // planes, seq_count - planes + 1)
    core_rows = rows // 2
    group_rows = core_rows // GROUPS
    wide = half // SPAN
    chunks = GROUPS * 2 * wide
    vmem = pl.BlockSpec(memory_space=pltpu.VMEM)
    anywhere = pl.BlockSpec(memory_space=pltpu.MemorySpace.HBM)
    dma = pltpu.SemaphoreType.DMA

    def room(*shape, kind=BF16):
        return pltpu.VMEM(shape, kind)

    scratch = (
        room(4, heads, 2, 2, rows, HEAD_DIM),
        room(2, heads, 2, 2, rows, HEAD_DIM),
        room(2, heads, 2, rows, HEAD_DIM),
        [room(2 * planes, 2, core_rows, HEAD_DIM) for _ in range(heads)],
        room(2, tp_count, heads, GROUPS, most * group_rows, HEAD_DIM),
        room(heads, GROUPS, most * group_rows, HEAD_DIM),
        room(4, gate_weight.shape[1], units),
        room(2, down_weight.shape[1], width),
        room(GROUPS, most * group_rows, 4 * units, kind=F32),
        room(GROUPS, most * group_rows, 1, kind=F32),
        room(2, GROUPS, most * group_rows, 2 * units),
        room(chunks, most * group_rows, SPAN),
        room(chunks, most * group_rows, SPAN),
        room(chunks, most * group_rows, SPAN, kind=F32),
        [room(most, group_rows, SPAN) for _ in range(chunks)],
        [room(most, group_rows, SPAN) for _ in range(chunks)],
        room(chunks, planes, 2, group_rows, SPAN),
        room(chunks, planes, 2, group_rows, SPAN),
        room(chunks, planes, 2, group_rows, SPAN),
        room(chunks, planes, 2, group_rows, SPAN),
        room(chunks, 2, group_rows, SPAN),
        dma((1,)),
        dma((1,)),
        dma((1,)),
        dma((2, heads)),
        dma((2 * heads + 1,)),
        dma((planes, heads)),
        dma((4, heads + GROUPS - 1)),
        dma((1,)),
        dma((GROUPS,)),
        dma((chunks,)),
        dma((chunks,)),
        dma((2, chunks)),
        dma((1,)),
        dma((9,)),
        dma((4,)),
    )
    flat, tree = jax.tree.flatten(scratch, is_leaf=lambda leaf: not isinstance(leaf, (list, tuple)))

    def kernel(*refs):
        layer_kernel(most, refs[:9], refs[9], jax.tree.unflatten(tree, refs[10:]))

    return pl.pallas_call(
        kernel,
        name="layer",
        out_shape=pltpu.VMEM((rows, width), BF16),
        in_specs=[pl.BlockSpec(memory_space=pltpu.SMEM)]
        + [anywhere] * 4
        + [vmem]
        + [anywhere] * 3,
        out_specs=vmem,
        scratch_shapes=flat,
        compiler_params=pltpu.CompilerParams(
            collective_id=0, has_side_effects=True, vmem_limit_bytes=67043328 - 2 * rows * width
        ),
    )(
        routing.reshape(-1),
        queries,
        keys,
        values,
        residual_in,
        norm_gain.reshape(1, -1),
        gate_weight,
        up_weight,
        down_weight,
    )


def solution(mesh):
    in_specs = (
        P("seq", "tp"),
        P("seq", "tp"),
        P("seq", "tp"),
        P("seq", "tp"),
        P(),
        P(),
        P("seq", None, "tp"),
        P("seq", None, "tp"),
        P("seq", None, "tp"),
    )
    out_specs = P("seq", "tp")
    return jax.shard_map(local, mesh=mesh, in_specs=in_specs, out_specs=out_specs, check_vma=False)
```

```python
import contextlib
import math

import jax
import jax.numpy as jnp
from jax import lax
from jax.experimental import pallas as pl
from jax.experimental.pallas import tpu as pltpu
from jax.sharding import PartitionSpec as P

HEAD_DIM = 128
BLOCK = 128
WINDOW = 512


epsilon = 1e-05
masked_score = -1e30


def shifted(block, axis, distance):
    devices = range(lax.axis_size(axis))
    route = [(i - distance, i) for i in devices if i - distance in devices]
    return lax.ppermute(block, axis, route)


def local_general(
    queries, keys, values, residual_in, norm_gain, routing, gate_weight, up_weight, down_weight
):
    seq_count = lax.axis_size("seq")
    seq_place = lax.axis_index("seq")
    tok_rows = queries.shape[0]
    feat_width = queries.shape[1]
    head_count = feat_width // HEAD_DIM
    prior_count = (WINDOW - 1) // tok_rows + 1
    earlier_keys = []
    earlier_values = []
    for distance in range(1, prior_count + 1):
        moved_keys, moved_values = shifted((keys, values), "seq", distance)
        earlier_keys.insert(0, moved_keys)
        earlier_values.insert(0, moved_values)
    key_all = jnp.concatenate(earlier_keys + [keys], axis=0).reshape(-1, head_count, HEAD_DIM)
    value_all = jnp.concatenate(earlier_values + [values], axis=0).reshape(-1, head_count, HEAD_DIM)
    query_heads = queries.reshape(tok_rows, head_count, HEAD_DIM)
    query_pos = seq_place * tok_rows + jnp.arange(tok_rows, dtype=jnp.int32)
    key_pos = (
        seq_place * tok_rows
        - prior_count * tok_rows
        + jnp.arange((prior_count + 1) * tok_rows, dtype=jnp.int32)
    )
    visible = (
        (key_pos[None, :] >= 0)
        & (key_pos[None, :] <= query_pos[:, None])
        & (key_pos[None, :] > query_pos[:, None] - WINDOW)
    )
    scores = jnp.einsum(
        "qhd,khd->hqk", query_heads, key_all, preferred_element_type=jnp.float32
    ) * (1.0 / math.sqrt(HEAD_DIM))
    scores = jnp.where(visible[None], scores, masked_score)
    top_score = jnp.max(scores, axis=2, keepdims=True)
    expo = jnp.exp(scores - top_score)
    weights_soft = (expo / jnp.sum(expo, axis=2, keepdims=True)).astype(jnp.bfloat16)
    attended = jnp.einsum(
        "hqk,khd->qhd", weights_soft, value_all, preferred_element_type=jnp.float32
    ).reshape(tok_rows, feat_width)
    stream = (residual_in.astype(jnp.float32) + attended).astype(jnp.bfloat16)
    send_width = stream.shape[1]
    blocks_dev = tok_rows // BLOCK
    piece_rows = BLOCK // seq_count
    spread_in = stream.reshape(blocks_dev, seq_count, piece_rows, send_width)
    spread_out = lax.all_to_all(spread_in, "seq", split_axis=1, concat_axis=0, tiled=True)
    block_count = blocks_dev * seq_count
    spread_rows = spread_out.reshape(block_count, piece_rows, send_width)
    expert_ids = routing[:, 0]
    expert_count = seq_count // 2
    most_blocks = min(2 * block_count // expert_count, block_count - expert_count + 1)
    order_index = jnp.arange(block_count, dtype=jnp.int32)
    same_expert = expert_ids[None, :] == expert_ids[:, None]
    rank_of = jnp.sum(same_expert & (order_index[None, :] < order_index[:, None]), axis=1)
    expert_range = jnp.arange(expert_count, dtype=jnp.int32)
    slot_range = jnp.arange(most_blocks, dtype=jnp.int32)
    selector = (
        (expert_ids[None, None, :] == expert_range[:, None, None])
        & (rank_of[None, None, :] == slot_range[None, :, None])
    ).astype(jnp.bfloat16)
    picked = jnp.einsum(
        "erb,bqf->erqf", selector, spread_rows, preferred_element_type=jnp.float32
    ).astype(jnp.bfloat16)
    outgoing = jnp.broadcast_to(
        picked[:, None], (expert_count, 2, most_blocks, piece_rows, send_width)
    )
    outgoing = outgoing.reshape(seq_count, most_blocks, piece_rows, send_width)
    features_full = lax.all_gather(
        lax.all_to_all(outgoing, "seq", split_axis=0, concat_axis=0, tiled=True),
        "tp",
        axis=3,
        tiled=True,
    )
    source_count = features_full.shape[0]
    slot_count = features_full.shape[1]
    stream_f32 = features_full.astype(jnp.float32)
    mean_square = jnp.mean(stream_f32 * stream_f32, axis=3, keepdims=True)
    normed = (stream_f32 * lax.rsqrt(mean_square + epsilon) * norm_gain).astype(jnp.bfloat16)
    normed = normed.reshape(-1, normed.shape[3])
    gate_val = jnp.dot(normed, gate_weight[0], preferred_element_type=jnp.float32)
    up_val = jnp.dot(normed, up_weight[0], preferred_element_type=jnp.float32)
    hidden = (jax.nn.silu(gate_val) * up_val).astype(jnp.bfloat16)
    hidden_half = lax.all_gather(hidden, "tp", axis=1, tiled=True)
    partial_value = jnp.dot(hidden_half, down_weight[0], preferred_element_type=jnp.float32).astype(
        jnp.bfloat16
    )
    partial_value = partial_value.reshape(source_count, slot_count, piece_rows, feat_width)
    returned = lax.all_to_all(partial_value, "seq", split_axis=0, concat_axis=0, tiled=True)
    returned = returned.reshape(expert_count, 2, most_blocks, piece_rows * feat_width)
    combined = jnp.einsum("erb,epry->pby", selector, returned, preferred_element_type=jnp.float32)
    residual_rows = spread_rows
    residual_rows = residual_rows.reshape(block_count, piece_rows * feat_width).astype(jnp.float32)
    finished = (residual_rows + combined[0] + combined[1]).astype(jnp.bfloat16)
    finished = finished.reshape(seq_count, blocks_dev, piece_rows, feat_width)
    restored = lax.all_to_all(finished, "seq", split_axis=0, concat_axis=2, tiled=True)
    return restored.reshape(tok_rows, feat_width)


BF16 = jnp.bfloat16
F32 = jnp.float32
PLANES = 4
GROUPS = 4
SPAN = 2 * HEAD_DIM
STAY_HEAD = 3


def mark(name):
    return contextlib.nullcontext()


def remote(src, dst, send_sem, recv_sem, device):
    return pltpu.make_async_remote_copy(
        src_ref=src,
        dst_ref=dst,
        send_sem=send_sem,
        recv_sem=recv_sem,
        device_id=device,
        device_id_type=pl.DeviceIdType.MESH,
    )


def size_of(ref):
    return math.prod(ref.shape) * ref.dtype.itemsize


def layer_kernel(most, arguments, out_ref, scratch):
    routing_ref, q_ref, k_ref, v_ref, r_ref, gain_ref, gate_ref, up_ref, down_ref = arguments
    (
        kv_buf,
        qr_buf,
        away,
        line,
        x_buf,
        x_other,
        w_buf,
        d_buf,
        acc_buf,
        square_buf,
        hid_buf,
        b_out,
        b_in,
        part,
        mix,
        end_in,
        up_out,
        up_in,
        dn_out,
        dn_in,
        fin,
        own_s,
        away_s,
        weight_s,
        swap_r,
        kv_r,
        line_r,
        feat_r,
        weight_r,
        hid_r,
        branch_r,
        end_r,
        ret_r,
        last_r,
        sent,
        plane_sent,
    ) = scratch
    rows = q_ref.shape[0]
    half = q_ref.shape[1] // 2
    heads = half // HEAD_DIM
    units = gate_ref.shape[2]
    features = gain_ref.shape[1]
    core_rows = rows // 2
    group_rows = core_rows // GROUPS
    me = lax.axis_index("seq")
    t = lax.axis_index("tp")
    z = me // 2
    y = me % 2
    x = t // 2
    c = t % 2
    yo, xo, co = 1 - y, 1 - x, 1 - c
    tc = 2 * x + co
    tx = 2 * xo + c
    txc = 2 * xo + co
    mate = 2 * z + yo
    dev_y, dev_yc = (mate, t), (mate, tc)
    dev_x, dev_xc = (me, tx), (me, txc)
    dev_c = (me, tc)
    dev_up, dev_dn = (me + 2, t), (me - 2, t)
    has_up, has_dn = z < PLANES - 1, z > 0

    limit = size_of(w_buf.at[0])
    all_lots = [0]
    plane_lots = [[0] for _ in range(PLANES)]

    def lot_for(lots, ref):
        if lots[-1] + size_of(ref) > limit:
            lots.append(0)
        lots[-1] += size_of(ref)
        return len(lots) - 1

    final_lot = sent.shape[0] - 1
    relay_lot = final_lot - 1

    def push(src, dst, recv_sem, device, lot=None):
        lot = lot_for(all_lots, src) if lot is None else lot
        remote(src, dst, sent.at[lot], recv_sem, device).start()

    def push_plane(plane, src, dst, recv_sem, device):
        lot = lot_for(plane_lots[plane], src)
        remote(src, dst, plane_sent.at[lot], recv_sem, device).start()

    def got(ref, recv_sem):
        remote(ref, ref, sent.at[0], recv_sem, dev_y).wait_recv()

    def wait_for(amount, recv_sem):
        got(w_buf.at[0, pl.ds(0, amount // (2 * units))], recv_sem)

    def loaded(ref, sem):
        pltpu.make_async_copy(ref, ref, sem).wait()

    barrier = pltpu.get_barrier_semaphore()

    def greet(device):
        pl.semaphore_signal(
            barrier, inc=1, device_id=device, device_id_type=pl.DeviceIdType.MESH
        )

    for device in (dev_y, dev_yc, dev_c, dev_x, dev_xc):
        greet(device)
    pl.when(has_up)(lambda: greet(dev_up))
    pl.when(has_dn)(lambda: greet(dev_dn))

    def cols(which, h):
        return pl.ds(pl.multiple_of(which * half + h * HEAD_DIM, HEAD_DIM), HEAD_DIM)

    sources = ((k_ref, v_ref), (q_ref, r_ref))

    def place(kind, h, n, block):
        buf = kv_buf if kind == 0 else qr_buf
        return buf.at[0, h, n, block]

    def load_own(kind, h):
        for n, ref in enumerate(sources[kind]):
            pltpu.make_async_copy(
                ref.at[:, cols(y, h)], place(kind, h, n, y), own_s.at[0]
            ).start()

    def load_away(kind, h):
        for n, ref in enumerate(sources[kind]):
            pltpu.make_async_copy(
                ref.at[:, cols(yo, h)], away.at[kind, h, n], away_s.at[0]
            ).start()

    def swap(kind, h):
        buf = kv_buf if kind == 0 else qr_buf
        push(away.at[kind, h], buf.at[0, h, :, y], swap_r.at[kind, h], dev_y)

    def own(kind, h):
        buf = kv_buf if kind == 0 else qr_buf
        got(buf.at[0, h, :, yo], swap_r.at[kind, h])

    for kind in range(2):
        for h in range(heads):
            load_away(kind, h)
    for kind in range(2):
        for h in range(heads):
            load_own(kind, h)

    expert = [routing_ref[b] for b in range(2 * PLANES)]
    slot = []
    for b in range(2 * PLANES):
        count = jnp.int32(0)
        for j in range(b):
            count = count + jnp.where(expert[j] == expert[b], 1, 0)
        slot.append(jnp.minimum(count, most - 1))
    chosen = []
    for r in range(most):
        index = jnp.int32(0)
        for b in range(2 * PLANES):
            index = jnp.where((expert[b] == z) & (slot[b] == r), b, index)
        chosen.append(index)

    with mark("barwait"):
        pl.semaphore_wait(barrier, 5 + jnp.where(has_up, 1, 0) + jnp.where(has_dn, 1, 0))

    low_order = ((0, 3), (0, 0), (1, 3), (1, 0), (0, 1), (1, 1), (0, 2), (1, 2))
    high_order = ((0, 0), (1, 0), (0, 3), (0, 1), (1, 1), (1, 3), (0, 2), (1, 2))

    with mark("away"):
        loaded(away, away_s.at[0])

    @pl.when(z < 2)
    def _():
        for kind, h in low_order:
            swap(kind, h)

    all_lots[:] = [0]

    @pl.when(z >= 2)
    def _():
        for kind, h in high_order:
            swap(kind, h)

    with mark("ownwait"):
        loaded(away, own_s.at[0])
    row_at = lax.broadcasted_iota(jnp.int32, (rows, rows), 0)
    col_at = lax.broadcasted_iota(jnp.int32, (rows, rows), 1)
    below, above, farther = 1, 2, 3

    def attend(here, plane, h):
        side = 0 if plane == here else 1
        keep = {here: 0, here - 1: below, here + 1: above, here - 2: farther}
        reach = WINDOW // rows
        for n in range(2):
            block = 2 * plane + n
            seen = [
                (back, keep[(block - back) // 2], (block - back) % 2)
                for back in range(reach + 1)
                if block >= back
            ]
            query = qr_buf[side, h, 0, n]
            parts = []
            for back, at, odd in seen:
                score = lax.dot_general(
                    query,
                    kv_buf[at, h, 0, odd],
                    (((1,), (1,)), ((), ())),
                    preferred_element_type=F32,
                )
                if back == 0:
                    score = jnp.where(col_at <= row_at, score, masked_score)
                if back == reach:
                    score = jnp.where(col_at > row_at, score, masked_score)
                parts.append(score)
            top = parts[0]
            for score in parts[1:]:
                top = jnp.maximum(top, score)
            top = jnp.max(top, axis=1, keepdims=True)
            parts = [jnp.exp((score - top) * (1.0 / math.sqrt(HEAD_DIM))) for score in parts]
            total = parts[0]
            for score in parts[1:]:
                total = total + score
            share = 1.0 / jnp.sum(total, axis=1, keepdims=True)
            attended = jnp.dot(
                jnp.concatenate([(score * share).astype(BF16) for score in parts], axis=1),
                jnp.concatenate([kv_buf[at, h, 1, odd] for _, at, odd in seen], axis=0),
                preferred_element_type=F32,
            )
            stream = (qr_buf[side, h, 1, n].astype(F32) + attended).astype(BF16)
            line[h][block] = stream.reshape(2, core_rows, HEAD_DIM)

    def device_at(way):
        return dev_up if way > 0 else dev_dn

    def kv_sem(at, h):
        return kv_r.at[2 * heads if at == farther else (at - 1) * heads + h]

    def send_kv(here, way, src, dst, h):
        push_plane(here, kv_buf.at[src, h], kv_buf.at[dst, h], kv_sem(dst, h), device_at(way))

    def got_kv(at, h):
        got(kv_buf.at[at, h], kv_sem(at, h))

    def send_part(here, way, kind, h, block):
        at = below if way > 0 else above
        buf, to = (kv_buf, at) if kind == 0 else (qr_buf, 1)
        push_plane(
            here, buf.at[0, h, :, block], buf.at[to, h, :, block], kv_sem(at, h), device_at(way)
        )

    def send_home(here, way, h, kinds=(0,)):
        for kind in kinds:
            send_part(here, way, kind, h, y)

    def got_above(h):
        wait_for(size_of(kv_buf.at[0, h]) + size_of(qr_buf.at[0, h]), kv_sem(above, h))

    def send_line(here, way, plane, h):
        ref = line[h].at[pl.ds(2 * plane, 2)]
        push_plane(here, ref, ref, line_r.at[plane, h], device_at(way))

    def got_line(plane, h):
        got(line[h].at[pl.ds(2 * plane, 2)], line_r.at[plane, h])

    taken = [set() for _ in range(PLANES)]

    def made(here, plane, h, hold=False):
        taken[here].add((plane, h))
        with mark(f"attend{plane}_{h}"):
            attend(here, plane, h)
        if here < PLANES - 1 and not hold:
            send_line(here, 1, plane, h)
        if here > 0:
            send_line(here, -1, plane, h)

    def pass_on(here, way, plane, h):
        with mark(f"pass{plane}_{h}"):
            taken[here].add((plane, h))
            got_line(plane, h)
            send_line(here, way, plane, h)

    def steps_0(step):
        if step == 0:
            for kind, h in low_order:
                with mark(f"own{kind}_{h}"):
                    own(kind, h)
                if kind == 0:
                    send_part(0, 1, 0, h, yo)
                else:
                    made(0, 0, h)

    def steps_1(step):
        def first(h):
            with mark(f"own0_{h}"):
                own(0, h)
            send_part(1, 1, 0, h, yo)

        def home(h):
            with mark(f"own1_{h}"):
                own(1, h)
                got_kv(below, h)
            if h == STAY_HEAD:
                send_kv(1, 1, below, farther, h)
            made(1, 1, h)

        def lower(h):
            with mark(f"lower{h}"):
                got_above(h)
            made(1, 2, h)

        if step == 0:
            first(3)
            first(0)
            home(3)
            first(1)
            home(0)
            lower(0)
            pass_on(1, 1, 0, 3)
            pass_on(1, 1, 0, 0)
            first(2)
            home(1)
            lower(1)
            pass_on(1, -1, 3, 0)
        if step == 1:
            pass_on(1, 1, 0, 1)
            home(2)
            pass_on(1, 1, 0, 2)
            pass_on(1, -1, 3, 1)
        if step == 2:
            pass_on(1, -1, 2, 3)
            pass_on(1, -1, 3, 3)
        if step == 3:
            lower(2)
        if step == 4:
            pass_on(1, -1, 3, 2)

    def steps_2(step):
        def first(h):
            with mark(f"own0_{h}"):
                own(0, h)
            send_part(2, 1 if h == STAY_HEAD else -1, 0, h, yo)

        def second(h):
            with mark(f"own1_{h}"):
                own(1, h)
            if h != STAY_HEAD:
                send_part(2, -1, 1, h, yo)

        def lower(h, hold=False):
            with mark(f"lower{h}"):
                got_above(h)
                got_kv(below, h)
            made(2, 3, h, hold)

        if step == 0:
            first(0)
            second(0)
            first(3)
            first(1)
            with mark("below3"):
                got_kv(below, 3)
            send_kv(2, 1, below, farther, 3)
            second(1)
            send_home(2, -1, 2, (0, 1))
            lower(0)
            second(3)
            with mark("farther3"):
                got_kv(farther, 3)
            made(2, 2, 3)
            pass_on(2, 1, 1, 3)
            lower(1)
            pass_on(2, -1, 3, 3)
            first(2)
            second(2)
            pass_on(2, 1, 1, 0)
            pass_on(2, 1, 0, 3)
        if step == 1:
            pass_on(2, 1, 2, 0)
            pass_on(2, 1, 0, 0)
        if step == 2:
            lower(2, True)
            pass_on(2, 1, 1, 1)
            pass_on(2, 1, 2, 1)
        if step == 3:
            pass_on(2, 1, 0, 1)
            send_line(2, 1, 3, 2)
        if step == 4:
            pass_on(2, 1, 1, 2)
            pass_on(2, 1, 0, 2)
            pass_on(2, 1, 2, 2)

    def steps_3(step):
        if step == 0:
            for kind, h in high_order:
                with mark(f"own{kind}_{h}"):
                    own(kind, h)
                if h != STAY_HEAD:
                    send_part(3, -1, kind, h, yo)
                    if (kind, h) == (1, 1):
                        send_home(3, -1, 2, (0, 1))
                elif kind == 1:
                    with mark("below3"):
                        got_kv(below, 3)
                        got_kv(farther, 3)
                    made(3, 3, 3)

    def early(plane):
        if plane < 2:
            for h in (3, 0, 1, 2):
                send_home(plane, 1, h)
        else:
            for h in (0, 1):
                send_home(plane, -1, h, (0, 1))
            if plane == 2:
                send_home(plane, 1, STAY_HEAD)

    for plane in range(PLANES):
        pl.when(z == plane)(lambda: early(plane))

    def planes(step):
        for plane, steps in enumerate((steps_0, steps_1, steps_2, steps_3)):

            @pl.when(z == plane)
            def _():
                steps(step)

    def collect(order, pos):
        h = order[pos]
        for plane in range(PLANES):
            if orders[plane // 2][pos] != h:
                continue

            @pl.when(z == plane)
            def _():
                for other in range(PLANES):
                    if (other, h) not in taken[plane]:
                        taken[plane].add((other, h))
                        got_line(other, h)

    high = jnp.where(z < 2, 0, 1)
    orders = ((0, 1, 3, 2), (3, 0, 1, 2))
    heads_at = [low + high * (up - low) for low, up in zip(*orders)]
    ends = len(heads_at) - 1

    def groups_of(pos):
        return [pl.ds(g, 1) for g in range(GROUPS)] if pos == ends else [pl.ds(0, GROUPS)]

    def feature_at(pos, g):
        return pos + g.start

    def feature(n, py, pt, pos, g, device, src=None, lot=None):
        ref = x_buf.at[py, pt, heads_at[pos], g]
        src = ref if src is None else src
        push(src, ref, feat_r.at[lot_of(n, pos), feature_at(pos, g)], device, lot)

    def lot_of(n, pos):
        return ((0, 2, 1, 0, 0, 3, 3) if pos == ends else (0, 0, 1, 2, 0, 3, 3))[n]

    arrivals = (
        (y, tc),
        (y, tx),
        (y, txc),
        (yo, t),
        (yo, tc),
        (yo, tx),
        (yo, txc),
    )

    def take(n, pos, g):
        py, pt = arrivals[n]
        got(x_buf.at[py, pt, heads_at[pos], g], feat_r.at[lot_of(n, pos), feature_at(pos, g)])

    def choose(h, g):
        for r in range(most):
            at = pl.ds(r * group_rows, group_rows)
            for ref, side in ((x_buf.at[y, t, h], c), (x_other.at[h], co)):
                block = line[h][chosen[r], side]
                for i in range(GROUPS):
                    if g.start <= i < g.start + g.size:
                        ref[i, at] = block[i * group_rows : (i + 1) * group_rows]

    def gather(pos):
        with mark(f"collect{pos}"):
            for order in orders:
                if order is orders[0] or order[pos] != orders[0][pos]:
                    collect(order, pos)

    def first_stage(pos, lots=None):
        for g in lots or groups_of(pos):
            if orders[0][pos] == orders[1][pos]:
                choose(orders[0][pos], g)
            else:
                pl.when(z < 2)(lambda: choose(orders[0][pos], g))
                pl.when(z >= 2)(lambda: choose(orders[1][pos], g))
            other = x_other.at[heads_at[pos], g]
            feature(3, y, t, pos, g, dev_y)
            feature(2, y, t, pos, g, dev_xc, other)
            feature(1, y, t, pos, g, dev_x)
            feature(4, y, t, pos, g, dev_yc, other)
            feature(0, y, t, pos, g, dev_c, other)

    def second_stage(pos, g, lot=None):
        if pos == ends:
            take(1, pos, g)
            feature(5, y, tx, pos, g, dev_y, lot=lot)
        else:
            take(3, pos, g)
            feature(5, yo, t, pos, g, dev_x, lot=lot)
        take(2, pos, g)
        feature(6, y, txc, pos, g, dev_y, lot=lot)

    def near(pos, g):
        wait_for(3 * size_of(x_buf.at[y, t, 0, g]), feat_r.at[0, feature_at(pos, g)])

    def far(pos, g):
        wait_for(2 * size_of(x_buf.at[y, t, 0, g]), feat_r.at[3, feature_at(pos, g)])

    def expert_parts(parts, pos, g):
        depth = g.size * most * group_rows
        left, right = [], []
        square = square_buf[g].reshape(depth, 1)
        for py, pt in parts:
            start = pl.multiple_of((2 * pt + py) * half + heads_at[pos] * HEAD_DIM, HEAD_DIM)
            value = x_buf[py, pt, heads_at[pos], g].reshape(depth, HEAD_DIM).astype(F32)
            square = square + jnp.sum(value * value, axis=1, keepdims=True)
            left.append((value * gain_ref[:, pl.ds(start, HEAD_DIM)]).astype(BF16))
            right.append(
                jnp.concatenate(
                    [w_buf[i, pl.ds(start, HEAD_DIM), :] for i in range(4)], axis=1
                )
            )
        square_buf[g] = square.reshape(g.size, most * group_rows, 1)
        acc_buf[g] += jnp.dot(
            jnp.concatenate(left, axis=1),
            jnp.concatenate(right, axis=0),
            preferred_element_type=F32,
        ).reshape(g.size, most * group_rows, 4 * units)

    every_part = [(y, t)] + list(arrivals)

    parts_last = groups_of(ends)
    both = groups_of(0)[0]
    planes(0)
    weights = (
        (gate_ref.at[0], w_buf.at[c]),
        (up_ref.at[0], w_buf.at[2 + c]),
        (down_ref.at[0], d_buf.at[c]),
    )
    for src, dst in weights:
        pltpu.make_async_copy(src, dst, weight_s.at[0]).start()
        push(src, dst, weight_r.at[0], dev_c)

    gather(0)
    first_stage(0)
    planes(1)

    @pl.when(z == 0)
    def _():
        with mark("second0"):
            second_stage(0, both, relay_lot)

    gather(1)
    first_stage(1)
    planes(2)

    @pl.when(z > 0)
    def _():
        with mark("second0"):
            second_stage(0, both, relay_lot)

    planes(3)
    gather(2)
    first_stage(2)
    with mark("second1"):
        second_stage(1, both)
    planes(4)
    gather(3)
    first_stage(3, parts_last[:1])
    with mark("second2"):
        second_stage(2, both)
    first_stage(3, parts_last[1:])
    acc_buf[...] = jnp.zeros_like(acc_buf)
    square_buf[...] = jnp.zeros_like(square_buf)
    with mark("weights"):
        every = w_buf.at[pl.ds(0, len(weights))]
        loaded(every, weight_s.at[0])
        got(every, weight_r.at[0])

    def whole(pos):
        with mark(f"feat{pos}"):
            near(pos, both)
            far(pos, both)
        with mark(f"expert{pos}"):
            expert_parts(every_part, pos, both)

    def relay_last(g):
        with mark(f"secondL{g.start}"):
            second_stage(ends, g)

    def hide(g):
        i = g.start
        with mark(f"nearL{i}"):
            near(ends, g)
        with mark(f"farL{i}"):
            far(ends, g)
        with mark(f"expertL{i}"):
            expert_parts(every_part, ends, g)
            scale = lax.rsqrt(square_buf[i] * (1.0 / features) + epsilon)
            gate_val = acc_buf[i, :, pl.ds(0, 2 * units)] * scale
            up_val = acc_buf[i, :, pl.ds(2 * units, 2 * units)] * scale
            hid_buf[x, i] = (gate_val / (1.0 + jnp.exp(-gate_val)) * up_val).astype(BF16)
        push(hid_buf.at[x, i], hid_buf.at[x, i], hid_r.at[i], dev_x)

    whole(0)
    relay_last(parts_last[0])
    whole(1)
    relay_last(parts_last[1])
    whole(2)
    for g in parts_last[2:]:
        relay_last(g)

    wide = half // SPAN
    pieces = [(s, j) for s in range(2) for j in range(wide)]

    def chunk(i, s, j):
        return (i * 2 + s) * wide + j

    pair = 2 * SPAN
    per = SPAN // HEAD_DIM

    def branch(i, s, which, j):
        hidden = jnp.concatenate([hid_buf[n, i] for n in range(2)], axis=1)
        at = pl.ds(pl.multiple_of(which * half + j * pair, pair), pair)
        weight = d_buf[c if s == 0 else co, :, at]
        value = jnp.dot(hidden, weight, preferred_element_type=F32).astype(BF16)
        return [(chunk(i, s, 2 * j + m), value[:, m * SPAN : (m + 1) * SPAN]) for m in range(2)]

    def down(i):
        with mark(f"hid{i}"):
            got(hid_buf.at[xo, i], hid_r.at[i])
        with mark(f"down{i}"):
            doubles = [(s, j) for s in range(2) for j in range(wide // 2)]
            for s, j in doubles:
                for k, value in branch(i, s, yo, j):
                    b_out[k] = value
                    push(b_out.at[k], b_in.at[k], branch_r.at[k], dev_y)
            for s, j in doubles:
                for m, (k, value) in enumerate(branch(i, s, y, j)):
                    stream = jnp.concatenate(
                        [
                            x_buf[y, t if s == 0 else tc, (2 * j + m) * per + q, i]
                            for q in range(per)
                        ],
                        axis=1,
                    )
                    part[k] = stream.astype(F32) + value.astype(F32)

    def blend(i, s, j):
        k = chunk(i, s, j)
        with mark(f"blend{k}"):
            got(b_in.at[k], branch_r.at[k])
            total = part[k] + b_in[k].astype(F32)
            mix[k][...] = total.astype(BF16).reshape(most, group_rows, SPAN)
        for plane, device in ((0, dev_up), (PLANES - 1, dev_dn)):

            @pl.when(z == plane)
            def _():
                push_plane(plane, mix[k], end_in[k], end_r.at[k], device)

    def pick(flag, a, b):
        mask = jnp.full(a.shape, flag.astype(jnp.int32), jnp.int32) > 0
        return jnp.where(mask, a.astype(F32), b.astype(F32)).astype(BF16)

    def give(here, way, k, d, other):
        out, arrived = (up_out, up_in) if way == 0 else (dn_out, dn_in)
        for n in range(2):
            b = 2 * d + n
            out[k, d, n] = pick(expert[b] == here, mix[k][slot[b]], other(b, n))
        push_plane(
            here,
            out.at[k, d],
            arrived.at[k, d],
            ret_r.at[d % 2, k],
            dev_up if way == 0 else dev_dn,
        )

    def turn_in(i, s, j):
        k = chunk(i, s, j)
        for here, way, targets in ((1, 0, (3, 2)), (2, 1, (0, 1))):

            @pl.when(z == here)
            def _():
                with mark(f"turn{k}"):
                    got(end_in[k], end_r.at[k])
                for d in targets:
                    give(here, way, k, d, lambda b, n: end_in[k][slot[b]])

    def carry(i, s, j):
        k = chunk(i, s, j)
        for here, way, d, arrived in ((2, 0, 3, up_in), (1, 1, 0, dn_in)):

            @pl.when(z == here)
            def _():
                with mark(f"carry{k}"):
                    got(arrived.at[k, d], ret_r.at[d % 2, k])
                give(here, way, k, d, lambda b, n: arrived[k, d, n])

    def target(side, i, which, j):
        return out_ref.at[
            pl.ds(pl.multiple_of(side * core_rows + i * group_rows, group_rows), group_rows),
            pl.ds(pl.multiple_of(which * half + j * SPAN, SPAN), SPAN),
        ]

    def arrive(i, s, j, d):
        k = chunk(i, s, j)

        @pl.when(z == d)
        def _():
            with mark(f"arrive{k}"):
                if d > 1:
                    got(up_in.at[k, d], ret_r.at[d % 2, k])
                if d < PLANES - 2:
                    got(dn_in.at[k, d], ret_r.at[d % 2, k])
            for n in range(2):
                b = 2 * d + n
                value = mix[k][slot[b]]
                if d > 0:
                    lower = up_in[k, d, n] if d > 1 else end_in[k][slot[b]]
                    value = pick(expert[b] < d, lower, value)
                if d < PLANES - 1:
                    higher = dn_in[k, d, n] if d < PLANES - 2 else end_in[k][slot[b]]
                    value = pick(expert[b] > d, higher, value)
                fin[k, n] = value
            mine = target(c, i, y, j)
            device = dev_y if s == 0 else dev_yc
            push(fin.at[k, yo], mine, last_r.at[0], device, final_lot)
            if s == 0:
                mine[...] = fin[k, y]
            else:
                push(fin.at[k, y], mine, last_r.at[0], dev_c, final_lot)

    def arrive_end(i, s, j):
        arrive(i, s, j, 0)
        arrive(i, s, j, PLANES - 1)

    def arrive_middle(i, s, j):
        arrive(i, s, j, 1)
        arrive(i, s, j, 2)

    every = [(i, s, j) for i in range(GROUPS) for s, j in pieces]
    for g in parts_last[:3]:
        hide(g)
    down(0)
    hide(parts_last[3])
    down(1)
    down(2)
    stages = (
        (0, blend),
        (4, turn_in),
        (9, carry),
        (12, arrive_middle),
        (16, arrive_end),
    )
    for n in range(len(every) + stages[-1][0]):
        if n == len(pieces):
            down(3)
        for lag, stage in stages:
            if 0 <= n - lag < len(every):
                stage(*every[n - lag])
    with mark("lastwait"):
        wait_for(3 * size_of(out_ref) // 4, last_r.at[0])

    def all_sent(sem, amount):
        if amount:
            ref = w_buf.at[0, pl.ds(0, amount // (2 * units))]
            remote(ref, ref, sem, hid_r.at[0], dev_y).wait_send()

    with mark("drain"):
        for lot, amount in enumerate(all_lots):
            all_sent(sent.at[lot], amount)
        all_sent(sent.at[relay_lot], 2 * size_of(x_buf.at[0, 0, 0]))
        all_sent(sent.at[final_lot], 3 * size_of(out_ref) // 4)
        for plane in range(PLANES):

            @pl.when(z == plane)
            def _():
                for lot, amount in enumerate(plane_lots[plane]):
                    all_sent(plane_sent.at[lot], amount)


def local(
    queries, keys, values, residual_in, norm_gain, routing, gate_weight, up_weight, down_weight
):
    seq_count = lax.axis_size("seq")
    tp_count = lax.axis_size("tp")
    rows, width = queries.shape
    units = gate_weight.shape[2]
    planes = seq_count // 2
    fits = (
        tp_count == 4
        and seq_count == 2 * PLANES
        and rows == BLOCK
        and WINDOW == 4 * rows
        and units == 128
        and width == 8 * HEAD_DIM
    )
    if not fits:
        return local_general(
            queries,
            keys,
            values,
            residual_in,
            norm_gain,
            routing,
            gate_weight,
            up_weight,
            down_weight,
        )
    half = width // 2
    heads = half // HEAD_DIM
    most = min(2 * seq_count // planes, seq_count - planes + 1)
    core_rows = rows // 2
    group_rows = core_rows // GROUPS
    wide = half // SPAN
    chunks = GROUPS * 2 * wide
    vmem = pl.BlockSpec(memory_space=pltpu.VMEM)
    anywhere = pl.BlockSpec(memory_space=pltpu.MemorySpace.HBM)
    dma = pltpu.SemaphoreType.DMA

    def room(*shape, kind=BF16):
        return pltpu.VMEM(shape, kind)

    scratch = (
        room(4, heads, 2, 2, rows, HEAD_DIM),
        room(2, heads, 2, 2, rows, HEAD_DIM),
        room(2, heads, 2, rows, HEAD_DIM),
        [room(2 * planes, 2, core_rows, HEAD_DIM) for _ in range(heads)],
        room(2, tp_count, heads, GROUPS, most * group_rows, HEAD_DIM),
        room(heads, GROUPS, most * group_rows, HEAD_DIM),
        room(4, gate_weight.shape[1], units),
        room(2, down_weight.shape[1], width),
        room(GROUPS, most * group_rows, 4 * units, kind=F32),
        room(GROUPS, most * group_rows, 1, kind=F32),
        room(2, GROUPS, most * group_rows, 2 * units),
        room(chunks, most * group_rows, SPAN),
        room(chunks, most * group_rows, SPAN),
        room(chunks, most * group_rows, SPAN, kind=F32),
        [room(most, group_rows, SPAN) for _ in range(chunks)],
        [room(most, group_rows, SPAN) for _ in range(chunks)],
        room(chunks, planes, 2, group_rows, SPAN),
        room(chunks, planes, 2, group_rows, SPAN),
        room(chunks, planes, 2, group_rows, SPAN),
        room(chunks, planes, 2, group_rows, SPAN),
        room(chunks, 2, group_rows, SPAN),
        dma((1,)),
        dma((1,)),
        dma((1,)),
        dma((2, heads)),
        dma((2 * heads + 1,)),
        dma((planes, heads)),
        dma((4, heads + GROUPS - 1)),
        dma((1,)),
        dma((GROUPS,)),
        dma((chunks,)),
        dma((chunks,)),
        dma((2, chunks)),
        dma((1,)),
        dma((9,)),
        dma((4,)),
    )
    flat, tree = jax.tree.flatten(scratch, is_leaf=lambda leaf: not isinstance(leaf, (list, tuple)))

    def kernel(*refs):
        layer_kernel(most, refs[:9], refs[9], jax.tree.unflatten(tree, refs[10:]))

    return pl.pallas_call(
        kernel,
        name="layer",
        out_shape=pltpu.VMEM((rows, width), BF16),
        in_specs=[pl.BlockSpec(memory_space=pltpu.SMEM)]
        + [anywhere] * 4
        + [vmem]
        + [anywhere] * 3,
        out_specs=vmem,
        scratch_shapes=flat,
        compiler_params=pltpu.CompilerParams(
            collective_id=0, has_side_effects=True, vmem_limit_bytes=67043328 - 2 * rows * width
        ),
    )(
        routing.reshape(-1),
        queries,
        keys,
        values,
        residual_in,
        norm_gain.reshape(1, -1),
        gate_weight,
        up_weight,
        down_weight,
    )


def solution(mesh):
    in_specs = (
        P("seq", "tp"),
        P("seq", "tp"),
        P("seq", "tp"),
        P("seq", "tp"),
        P(),
        P(),
        P("seq", None, "tp"),
        P("seq", None, "tp"),
        P("seq", None, "tp"),
    )
    out_specs = P("seq", "tp")
    return jax.shard_map(local, mesh=mesh, in_specs=in_specs, out_specs=out_specs, check_vma=False)
```

```python
import contextlib
import math

import jax
import jax.numpy as jnp
from jax import lax
from jax.experimental import pallas as pl
from jax.experimental.pallas import tpu as pltpu
from jax.sharding import PartitionSpec as P

HEAD_DIM = 128
BLOCK = 128
WINDOW = 512


epsilon = 1e-05
masked_score = -1e30


def shifted(block, axis, distance):
    devices = range(lax.axis_size(axis))
    route = [(i - distance, i) for i in devices if i - distance in devices]
    return lax.ppermute(block, axis, route)


def local_general(
    queries, keys, values, residual_in, norm_gain, routing, gate_weight, up_weight, down_weight
):
    seq_count = lax.axis_size("seq")
    seq_place = lax.axis_index("seq")
    tok_rows = queries.shape[0]
    feat_width = queries.shape[1]
    head_count = feat_width // HEAD_DIM
    prior_count = (WINDOW - 1) // tok_rows + 1
    earlier_keys = []
    earlier_values = []
    for distance in range(1, prior_count + 1):
        moved_keys, moved_values = shifted((keys, values), "seq", distance)
        earlier_keys.insert(0, moved_keys)
        earlier_values.insert(0, moved_values)
    key_all = jnp.concatenate(earlier_keys + [keys], axis=0).reshape(-1, head_count, HEAD_DIM)
    value_all = jnp.concatenate(earlier_values + [values], axis=0).reshape(-1, head_count, HEAD_DIM)
    query_heads = queries.reshape(tok_rows, head_count, HEAD_DIM)
    query_pos = seq_place * tok_rows + jnp.arange(tok_rows, dtype=jnp.int32)
    key_pos = (
        seq_place * tok_rows
        - prior_count * tok_rows
        + jnp.arange((prior_count + 1) * tok_rows, dtype=jnp.int32)
    )
    visible = (
        (key_pos[None, :] >= 0)
        & (key_pos[None, :] <= query_pos[:, None])
        & (key_pos[None, :] > query_pos[:, None] - WINDOW)
    )
    scores = jnp.einsum(
        "qhd,khd->hqk", query_heads, key_all, preferred_element_type=jnp.float32
    ) * (1.0 / math.sqrt(HEAD_DIM))
    scores = jnp.where(visible[None], scores, masked_score)
    top_score = jnp.max(scores, axis=2, keepdims=True)
    expo = jnp.exp(scores - top_score)
    weights_soft = (expo / jnp.sum(expo, axis=2, keepdims=True)).astype(jnp.bfloat16)
    attended = jnp.einsum(
        "hqk,khd->qhd", weights_soft, value_all, preferred_element_type=jnp.float32
    ).reshape(tok_rows, feat_width)
    stream = (residual_in.astype(jnp.float32) + attended).astype(jnp.bfloat16)
    send_width = stream.shape[1]
    blocks_dev = tok_rows // BLOCK
    piece_rows = BLOCK // seq_count
    spread_in = stream.reshape(blocks_dev, seq_count, piece_rows, send_width)
    spread_out = lax.all_to_all(spread_in, "seq", split_axis=1, concat_axis=0, tiled=True)
    block_count = blocks_dev * seq_count
    spread_rows = spread_out.reshape(block_count, piece_rows, send_width)
    expert_ids = routing[:, 0]
    expert_count = seq_count // 2
    most_blocks = min(2 * block_count // expert_count, block_count - expert_count + 1)
    order_index = jnp.arange(block_count, dtype=jnp.int32)
    same_expert = expert_ids[None, :] == expert_ids[:, None]
    rank_of = jnp.sum(same_expert & (order_index[None, :] < order_index[:, None]), axis=1)
    expert_range = jnp.arange(expert_count, dtype=jnp.int32)
    slot_range = jnp.arange(most_blocks, dtype=jnp.int32)
    selector = (
        (expert_ids[None, None, :] == expert_range[:, None, None])
        & (rank_of[None, None, :] == slot_range[None, :, None])
    ).astype(jnp.bfloat16)
    picked = jnp.einsum(
        "erb,bqf->erqf", selector, spread_rows, preferred_element_type=jnp.float32
    ).astype(jnp.bfloat16)
    outgoing = jnp.broadcast_to(
        picked[:, None], (expert_count, 2, most_blocks, piece_rows, send_width)
    )
    outgoing = outgoing.reshape(seq_count, most_blocks, piece_rows, send_width)
    features_full = lax.all_gather(
        lax.all_to_all(outgoing, "seq", split_axis=0, concat_axis=0, tiled=True),
        "tp",
        axis=3,
        tiled=True,
    )
    source_count = features_full.shape[0]
    slot_count = features_full.shape[1]
    stream_f32 = features_full.astype(jnp.float32)
    mean_square = jnp.mean(stream_f32 * stream_f32, axis=3, keepdims=True)
    normed = (stream_f32 * lax.rsqrt(mean_square + epsilon) * norm_gain).astype(jnp.bfloat16)
    normed = normed.reshape(-1, normed.shape[3])
    gate_val = jnp.dot(normed, gate_weight[0], preferred_element_type=jnp.float32)
    up_val = jnp.dot(normed, up_weight[0], preferred_element_type=jnp.float32)
    hidden = (jax.nn.silu(gate_val) * up_val).astype(jnp.bfloat16)
    hidden_half = lax.all_gather(hidden, "tp", axis=1, tiled=True)
    partial_value = jnp.dot(hidden_half, down_weight[0], preferred_element_type=jnp.float32).astype(
        jnp.bfloat16
    )
    partial_value = partial_value.reshape(source_count, slot_count, piece_rows, feat_width)
    returned = lax.all_to_all(partial_value, "seq", split_axis=0, concat_axis=0, tiled=True)
    returned = returned.reshape(expert_count, 2, most_blocks, piece_rows * feat_width)
    combined = jnp.einsum("erb,epry->pby", selector, returned, preferred_element_type=jnp.float32)
    residual_rows = spread_rows
    residual_rows = residual_rows.reshape(block_count, piece_rows * feat_width).astype(jnp.float32)
    finished = (residual_rows + combined[0] + combined[1]).astype(jnp.bfloat16)
    finished = finished.reshape(seq_count, blocks_dev, piece_rows, feat_width)
    restored = lax.all_to_all(finished, "seq", split_axis=0, concat_axis=2, tiled=True)
    return restored.reshape(tok_rows, feat_width)


BF16 = jnp.bfloat16
F32 = jnp.float32
PLANES = 4
GROUPS = 4
SPAN = 2 * HEAD_DIM
STAY_HEAD = 3


def mark(name):
    return contextlib.nullcontext()


def remote(src, dst, send_sem, recv_sem, device):
    return pltpu.make_async_remote_copy(
        src_ref=src,
        dst_ref=dst,
        send_sem=send_sem,
        recv_sem=recv_sem,
        device_id=device,
        device_id_type=pl.DeviceIdType.MESH,
    )


def size_of(ref):
    return math.prod(ref.shape) * ref.dtype.itemsize


def layer_kernel(most, arguments, out_ref, scratch):
    routing_ref, q_ref, k_ref, v_ref, r_ref, gain_ref, gate_ref, up_ref, down_ref = arguments
    (
        kv_buf,
        qr_buf,
        away,
        line,
        x_buf,
        x_other,
        w_buf,
        d_buf,
        acc_buf,
        square_buf,
        hid_buf,
        b_out,
        b_in,
        part,
        mix,
        end_in,
        up_out,
        up_in,
        dn_out,
        dn_in,
        fin,
        own_s,
        away_s,
        weight_s,
        swap_r,
        kv_r,
        line_r,
        feat_r,
        weight_r,
        hid_r,
        branch_r,
        end_r,
        ret_r,
        last_r,
        sent,
        plane_sent,
    ) = scratch
    rows = q_ref.shape[0]
    half = q_ref.shape[1] // 2
    heads = half // HEAD_DIM
    units = gate_ref.shape[2]
    features = gain_ref.shape[1]
    core_rows = rows // 2
    group_rows = core_rows // GROUPS
    me = lax.axis_index("seq")
    t = lax.axis_index("tp")
    z = me // 2
    y = me % 2
    x = t // 2
    c = t % 2
    yo, xo, co = 1 - y, 1 - x, 1 - c
    tc = 2 * x + co
    tx = 2 * xo + c
    txc = 2 * xo + co
    mate = 2 * z + yo
    dev_y, dev_yc = (mate, t), (mate, tc)
    dev_x, dev_xc = (me, tx), (me, txc)
    dev_c = (me, tc)
    dev_d, dev_dc = (mate, tx), (mate, txc)
    dev_up, dev_dn = (me + 2, t), (me - 2, t)
    has_up, has_dn = z < PLANES - 1, z > 0

    limit = size_of(w_buf.at[0])
    all_lots = [0]
    plane_lots = [[0] for _ in range(PLANES)]

    def lot_for(lots, ref):
        if lots[-1] + size_of(ref) > limit:
            lots.append(0)
        lots[-1] += size_of(ref)
        return len(lots) - 1

    final_lot = sent.shape[0] - 1
    relay_lot = final_lot - 1

    def push(src, dst, recv_sem, device, lot=None):
        lot = lot_for(all_lots, src) if lot is None else lot
        remote(src, dst, sent.at[lot], recv_sem, device).start()

    def push_plane(plane, src, dst, recv_sem, device):
        lot = lot_for(plane_lots[plane], src)
        remote(src, dst, plane_sent.at[lot], recv_sem, device).start()

    def got(ref, recv_sem):
        remote(ref, ref, sent.at[0], recv_sem, dev_y).wait_recv()

    def wait_for(amount, recv_sem):
        got(w_buf.at[0, pl.ds(0, amount // (2 * units))], recv_sem)

    def loaded(ref, sem):
        pltpu.make_async_copy(ref, ref, sem).wait()

    barrier = pltpu.get_barrier_semaphore()

    def greet(device):
        pl.semaphore_signal(
            barrier, inc=1, device_id=device, device_id_type=pl.DeviceIdType.MESH
        )

    for device in (dev_y, dev_yc, dev_c, dev_x, dev_xc):
        greet(device)
    pl.when(has_up)(lambda: greet(dev_up))
    pl.when(has_dn)(lambda: greet(dev_dn))

    def cols(which, h):
        return pl.ds(pl.multiple_of(which * half + h * HEAD_DIM, HEAD_DIM), HEAD_DIM)

    sources = ((k_ref, v_ref), (q_ref, r_ref))

    def place(kind, h, n, block):
        buf = kv_buf if kind == 0 else qr_buf
        return buf.at[0, h, n, block]

    def load_own(kind, h):
        for n, ref in enumerate(sources[kind]):
            pltpu.make_async_copy(
                ref.at[:, cols(y, h)], place(kind, h, n, y), own_s.at[0]
            ).start()

    def load_away(kind, h):
        for n, ref in enumerate(sources[kind]):
            pltpu.make_async_copy(
                ref.at[:, cols(yo, h)], away.at[kind, h, n], away_s.at[0]
            ).start()

    def swap(kind, h):
        buf = kv_buf if kind == 0 else qr_buf
        push(away.at[kind, h], buf.at[0, h, :, y], swap_r.at[kind, h], dev_y)

    def own(kind, h):
        buf = kv_buf if kind == 0 else qr_buf
        got(buf.at[0, h, :, yo], swap_r.at[kind, h])

    for kind in range(2):
        for h in range(heads):
            load_away(kind, h)
    for kind in range(2):
        for h in range(heads):
            load_own(kind, h)

    expert = [routing_ref[b] for b in range(2 * PLANES)]
    slot = []
    for b in range(2 * PLANES):
        count = jnp.int32(0)
        for j in range(b):
            count = count + jnp.where(expert[j] == expert[b], 1, 0)
        slot.append(jnp.minimum(count, most - 1))
    chosen = []
    for r in range(most):
        index = jnp.int32(0)
        for b in range(2 * PLANES):
            index = jnp.where((expert[b] == z) & (slot[b] == r), b, index)
        chosen.append(index)

    with mark("barwait"):
        pl.semaphore_wait(barrier, 5 + jnp.where(has_up, 1, 0) + jnp.where(has_dn, 1, 0))

    low_order = ((0, 3), (0, 0), (1, 3), (1, 0), (0, 1), (1, 1), (0, 2), (1, 2))
    high_order = ((0, 0), (1, 0), (0, 3), (0, 1), (1, 1), (1, 3), (0, 2), (1, 2))

    with mark("away"):
        loaded(away, away_s.at[0])

    @pl.when(z < 2)
    def _():
        for kind, h in low_order:
            swap(kind, h)

    all_lots[:] = [0]

    @pl.when(z >= 2)
    def _():
        for kind, h in high_order:
            swap(kind, h)

    with mark("ownwait"):
        loaded(away, own_s.at[0])
    row_at = lax.broadcasted_iota(jnp.int32, (rows, rows), 0)
    col_at = lax.broadcasted_iota(jnp.int32, (rows, rows), 1)
    below, above, farther = 1, 2, 3

    def attend(here, plane, h):
        side = 0 if plane == here else 1
        keep = {here: 0, here - 1: below, here + 1: above, here - 2: farther}
        reach = WINDOW // rows
        for n in range(2):
            block = 2 * plane + n
            seen = [
                (back, keep[(block - back) // 2], (block - back) % 2)
                for back in range(reach + 1)
                if block >= back
            ]
            query = qr_buf[side, h, 0, n]
            parts = []
            for back, at, odd in seen:
                score = lax.dot_general(
                    query,
                    kv_buf[at, h, 0, odd],
                    (((1,), (1,)), ((), ())),
                    preferred_element_type=F32,
                )
                if back == 0:
                    score = jnp.where(col_at <= row_at, score, masked_score)
                if back == reach:
                    score = jnp.where(col_at > row_at, score, masked_score)
                parts.append(score)
            top = parts[0]
            for score in parts[1:]:
                top = jnp.maximum(top, score)
            top = jnp.max(top, axis=1, keepdims=True)
            parts = [jnp.exp((score - top) * (1.0 / math.sqrt(HEAD_DIM))) for score in parts]
            total = parts[0]
            for score in parts[1:]:
                total = total + score
            share = 1.0 / jnp.sum(total, axis=1, keepdims=True)
            attended = jnp.dot(
                jnp.concatenate([(score * share).astype(BF16) for score in parts], axis=1),
                jnp.concatenate([kv_buf[at, h, 1, odd] for _, at, odd in seen], axis=0),
                preferred_element_type=F32,
            )
            stream = (qr_buf[side, h, 1, n].astype(F32) + attended).astype(BF16)
            line[h][block] = stream.reshape(2, core_rows, HEAD_DIM)

    def device_at(way):
        return dev_up if way > 0 else dev_dn

    def kv_sem(at, h):
        return kv_r.at[2 * heads if at == farther else (at - 1) * heads + h]

    def send_kv(here, way, src, dst, h):
        push_plane(here, kv_buf.at[src, h], kv_buf.at[dst, h], kv_sem(dst, h), device_at(way))

    def got_kv(at, h):
        got(kv_buf.at[at, h], kv_sem(at, h))

    def send_part(here, way, kind, h, block):
        at = below if way > 0 else above
        buf, to = (kv_buf, at) if kind == 0 else (qr_buf, 1)
        push_plane(
            here, buf.at[0, h, :, block], buf.at[to, h, :, block], kv_sem(at, h), device_at(way)
        )

    def send_home(here, way, h, kinds=(0,)):
        for kind in kinds:
            send_part(here, way, kind, h, y)

    def got_above(h):
        wait_for(size_of(kv_buf.at[0, h]) + size_of(qr_buf.at[0, h]), kv_sem(above, h))

    def send_line(here, way, plane, h):
        ref = line[h].at[pl.ds(2 * plane, 2)]
        push_plane(here, ref, ref, line_r.at[plane, h], device_at(way))

    def got_line(plane, h):
        got(line[h].at[pl.ds(2 * plane, 2)], line_r.at[plane, h])

    taken = [set() for _ in range(PLANES)]

    def made(here, plane, h, hold=False):
        taken[here].add((plane, h))
        with mark(f"attend{plane}_{h}"):
            attend(here, plane, h)
        if here < PLANES - 1 and not hold:
            send_line(here, 1, plane, h)
        if here > 0:
            send_line(here, -1, plane, h)

    def pass_on(here, way, plane, h):
        with mark(f"pass{plane}_{h}"):
            taken[here].add((plane, h))
            got_line(plane, h)
            send_line(here, way, plane, h)

    def steps_0(step):
        if step == 0:
            for kind, h in low_order:
                with mark(f"own{kind}_{h}"):
                    own(kind, h)
                if kind == 0:
                    send_part(0, 1, 0, h, yo)
                else:
                    made(0, 0, h)

    def steps_1(step):
        def first(h):
            with mark(f"own0_{h}"):
                own(0, h)
            send_part(1, 1, 0, h, yo)

        def home(h):
            with mark(f"own1_{h}"):
                own(1, h)
                got_kv(below, h)
            if h == STAY_HEAD:
                send_kv(1, 1, below, farther, h)
            made(1, 1, h)

        def lower(h):
            with mark(f"lower{h}"):
                got_above(h)
            made(1, 2, h)

        if step == 0:
            first(3)
            first(0)
            home(3)
            first(1)
            home(0)
            lower(0)
            pass_on(1, 1, 0, 3)
            pass_on(1, 1, 0, 0)
            first(2)
            home(1)
            lower(1)
            pass_on(1, -1, 3, 0)
        if step == 1:
            pass_on(1, 1, 0, 1)
            home(2)
            pass_on(1, 1, 0, 2)
            pass_on(1, -1, 3, 1)
        if step == 2:
            pass_on(1, -1, 2, 3)
            pass_on(1, -1, 3, 3)
        if step == 3:
            lower(2)
        if step == 4:
            pass_on(1, -1, 3, 2)

    def steps_2(step):
        def first(h):
            with mark(f"own0_{h}"):
                own(0, h)
            send_part(2, 1 if h == STAY_HEAD else -1, 0, h, yo)

        def second(h):
            with mark(f"own1_{h}"):
                own(1, h)
            if h != STAY_HEAD:
                send_part(2, -1, 1, h, yo)

        def lower(h, hold=False):
            with mark(f"lower{h}"):
                got_above(h)
                got_kv(below, h)
            made(2, 3, h, hold)

        if step == 0:
            first(0)
            second(0)
            first(3)
            first(1)
            with mark("below3"):
                got_kv(below, 3)
            send_kv(2, 1, below, farther, 3)
            second(1)
            send_home(2, -1, 2, (0, 1))
            lower(0)
            second(3)
            with mark("farther3"):
                got_kv(farther, 3)
            made(2, 2, 3)
            pass_on(2, 1, 1, 3)
            lower(1)
            pass_on(2, -1, 3, 3)
            first(2)
            second(2)
            pass_on(2, 1, 1, 0)
            pass_on(2, 1, 0, 3)
        if step == 1:
            pass_on(2, 1, 2, 0)
            pass_on(2, 1, 0, 0)
        if step == 2:
            lower(2, True)
            pass_on(2, 1, 1, 1)
            pass_on(2, 1, 2, 1)
        if step == 3:
            pass_on(2, 1, 0, 1)
            send_line(2, 1, 3, 2)
        if step == 4:
            pass_on(2, 1, 1, 2)
            pass_on(2, 1, 0, 2)
            pass_on(2, 1, 2, 2)

    def steps_3(step):
        if step == 0:
            for kind, h in high_order:
                with mark(f"own{kind}_{h}"):
                    own(kind, h)
                if h != STAY_HEAD:
                    send_part(3, -1, kind, h, yo)
                    if (kind, h) == (1, 1):
                        send_home(3, -1, 2, (0, 1))
                elif kind == 1:
                    with mark("below3"):
                        got_kv(below, 3)
                        got_kv(farther, 3)
                    made(3, 3, 3)

    def early(plane):
        if plane < 2:
            for h in (3, 0, 1, 2):
                send_home(plane, 1, h)
        else:
            for h in (0, 1):
                send_home(plane, -1, h, (0, 1))
            if plane == 2:
                send_home(plane, 1, STAY_HEAD)

    for plane in range(PLANES):
        pl.when(z == plane)(lambda: early(plane))

    def planes(step):
        for plane, steps in enumerate((steps_0, steps_1, steps_2, steps_3)):

            @pl.when(z == plane)
            def _():
                steps(step)

    def collect(order, pos):
        h = order[pos]
        for plane in range(PLANES):
            if orders[plane // 2][pos] != h:
                continue

            @pl.when(z == plane)
            def _():
                for other in range(PLANES):
                    if (other, h) not in taken[plane]:
                        taken[plane].add((other, h))
                        got_line(other, h)

    high = jnp.where(z < 2, 0, 1)
    orders = ((0, 1, 3, 2), (3, 0, 1, 2))
    heads_at = [low + high * (up - low) for low, up in zip(*orders)]
    ends = len(heads_at) - 1

    def groups_of(pos):
        return [pl.ds(g, 1) for g in range(GROUPS)] if pos == ends else [pl.ds(0, GROUPS)]

    def feature_at(pos, g):
        return pos + g.start

    def feature(n, py, pt, pos, g, device, src=None, lot=None):
        ref = x_buf.at[py, pt, heads_at[pos], g]
        src = ref if src is None else src
        push(src, ref, feat_r.at[lot_of(n, pos), feature_at(pos, g)], device, lot)

    def lot_of(n, pos):
        return 0 if pos == ends else (0, 0, 1, 2, 0, 3, 3)[n]

    arrivals = (
        (y, tc),
        (y, tx),
        (y, txc),
        (yo, t),
        (yo, tc),
        (yo, tx),
        (yo, txc),
    )

    def take(n, pos, g):
        py, pt = arrivals[n]
        got(x_buf.at[py, pt, heads_at[pos], g], feat_r.at[lot_of(n, pos), feature_at(pos, g)])

    def choose(h, g):
        for r in range(most):
            at = pl.ds(r * group_rows, group_rows)
            for ref, side in ((x_buf.at[y, t, h], c), (x_other.at[h], co)):
                block = line[h][chosen[r], side]
                for i in range(GROUPS):
                    if g.start <= i < g.start + g.size:
                        ref[i, at] = block[i * group_rows : (i + 1) * group_rows]

    def gather(pos):
        with mark(f"collect{pos}"):
            for order in orders:
                if order is orders[0] or order[pos] != orders[0][pos]:
                    collect(order, pos)

    def first_stage(pos, lots=None):
        for g in lots or groups_of(pos):
            if orders[0][pos] == orders[1][pos]:
                choose(orders[0][pos], g)
            else:
                pl.when(z < 2)(lambda: choose(orders[0][pos], g))
                pl.when(z >= 2)(lambda: choose(orders[1][pos], g))
            other = x_other.at[heads_at[pos], g]
            feature(3, y, t, pos, g, dev_y)
            feature(2, y, t, pos, g, dev_xc, other)
            feature(1, y, t, pos, g, dev_x)
            feature(4, y, t, pos, g, dev_yc, other)
            feature(0, y, t, pos, g, dev_c, other)
            if pos == ends:
                feature(5, y, t, pos, g, dev_d)
                feature(6, y, t, pos, g, dev_dc, other)

    def second_stage(pos, g, lot=None):
        take(3, pos, g)
        feature(5, yo, t, pos, g, dev_x, lot=lot)
        take(2, pos, g)
        feature(6, y, txc, pos, g, dev_y, lot=lot)

    def near(pos, g):
        wait_for(3 * size_of(x_buf.at[y, t, 0, g]), feat_r.at[0, feature_at(pos, g)])

    def far(pos, g):
        wait_for(2 * size_of(x_buf.at[y, t, 0, g]), feat_r.at[3, feature_at(pos, g)])

    def expert_parts(parts, pos, g):
        depth = g.size * most * group_rows
        left, right = [], []
        square = square_buf[g].reshape(depth, 1)
        for py, pt in parts:
            start = pl.multiple_of((2 * pt + py) * half + heads_at[pos] * HEAD_DIM, HEAD_DIM)
            value = x_buf[py, pt, heads_at[pos], g].reshape(depth, HEAD_DIM).astype(F32)
            square = square + jnp.sum(value * value, axis=1, keepdims=True)
            left.append((value * gain_ref[:, pl.ds(start, HEAD_DIM)]).astype(BF16))
            right.append(
                jnp.concatenate(
                    [w_buf[i, pl.ds(start, HEAD_DIM), :] for i in range(4)], axis=1
                )
            )
        square_buf[g] = square.reshape(g.size, most * group_rows, 1)
        acc_buf[g] += jnp.dot(
            jnp.concatenate(left, axis=1),
            jnp.concatenate(right, axis=0),
            preferred_element_type=F32,
        ).reshape(g.size, most * group_rows, 4 * units)

    every_part = [(y, t)] + list(arrivals)

    parts_last = groups_of(ends)
    both = groups_of(0)[0]
    planes(0)
    weights = (
        (gate_ref.at[0], w_buf.at[c]),
        (up_ref.at[0], w_buf.at[2 + c]),
        (down_ref.at[0], d_buf.at[c]),
    )
    for src, dst in weights:
        pltpu.make_async_copy(src, dst, weight_s.at[0]).start()
        push(src, dst, weight_r.at[0], dev_c)

    gather(0)
    first_stage(0)
    planes(1)

    @pl.when(z == 0)
    def _():
        with mark("second0"):
            second_stage(0, both, relay_lot)

    gather(1)
    first_stage(1)
    planes(2)

    @pl.when(z > 0)
    def _():
        with mark("second0"):
            second_stage(0, both, relay_lot)

    planes(3)
    gather(2)
    first_stage(2)
    with mark("second1"):
        second_stage(1, both)
    planes(4)
    gather(3)
    first_stage(3, parts_last[:1])
    with mark("second2"):
        second_stage(2, both)
    first_stage(3, parts_last[1:])
    acc_buf[...] = jnp.zeros_like(acc_buf)
    square_buf[...] = jnp.zeros_like(square_buf)
    with mark("weights"):
        every = w_buf.at[pl.ds(0, len(weights))]
        loaded(every, weight_s.at[0])
        got(every, weight_r.at[0])

    def whole(pos):
        with mark(f"feat{pos}"):
            near(pos, both)
            far(pos, both)
        with mark(f"expert{pos}"):
            expert_parts(every_part, pos, both)

    def hide(g):
        i = g.start
        with mark(f"farL{i}"):
            wait_for(7 * size_of(x_buf.at[y, t, 0, g]), feat_r.at[0, feature_at(ends, g)])
        with mark(f"expertL{i}"):
            expert_parts(every_part, ends, g)
            scale = lax.rsqrt(square_buf[i] * (1.0 / features) + epsilon)
            gate_val = acc_buf[i, :, pl.ds(0, 2 * units)] * scale
            up_val = acc_buf[i, :, pl.ds(2 * units, 2 * units)] * scale
            hid_buf[x, i] = (gate_val / (1.0 + jnp.exp(-gate_val)) * up_val).astype(BF16)
        push(hid_buf.at[x, i], hid_buf.at[x, i], hid_r.at[i], dev_x)

    for pos in range(ends):
        whole(pos)

    wide = half // SPAN
    pieces = [(s, j) for s in range(2) for j in range(wide)]

    def chunk(i, s, j):
        return (i * 2 + s) * wide + j

    pair = 2 * SPAN
    per = SPAN // HEAD_DIM

    def branch(i, s, which, j):
        hidden = jnp.concatenate([hid_buf[n, i] for n in range(2)], axis=1)
        at = pl.ds(pl.multiple_of(which * half + j * pair, pair), pair)
        weight = d_buf[c if s == 0 else co, :, at]
        value = jnp.dot(hidden, weight, preferred_element_type=F32).astype(BF16)
        return [(chunk(i, s, 2 * j + m), value[:, m * SPAN : (m + 1) * SPAN]) for m in range(2)]

    def down(i):
        with mark(f"hid{i}"):
            got(hid_buf.at[xo, i], hid_r.at[i])
        with mark(f"down{i}"):
            doubles = [(s, j) for s in range(2) for j in range(wide // 2)]
            for s, j in doubles:
                for k, value in branch(i, s, yo, j):
                    b_out[k] = value
                    push(b_out.at[k], b_in.at[k], branch_r.at[k], dev_y)
            for s, j in doubles:
                for m, (k, value) in enumerate(branch(i, s, y, j)):
                    stream = jnp.concatenate(
                        [
                            x_buf[y, t if s == 0 else tc, (2 * j + m) * per + q, i]
                            for q in range(per)
                        ],
                        axis=1,
                    )
                    part[k] = stream.astype(F32) + value.astype(F32)

    def blend(i, s, j):
        k = chunk(i, s, j)
        with mark(f"blend{k}"):
            got(b_in.at[k], branch_r.at[k])
            total = part[k] + b_in[k].astype(F32)
            mix[k][...] = total.astype(BF16).reshape(most, group_rows, SPAN)
        for plane, device in ((0, dev_up), (PLANES - 1, dev_dn)):

            @pl.when(z == plane)
            def _():
                push_plane(plane, mix[k], end_in[k], end_r.at[k], device)

    def pick(flag, a, b):
        mask = jnp.full(a.shape, flag.astype(jnp.int32), jnp.int32) > 0
        return jnp.where(mask, a.astype(F32), b.astype(F32)).astype(BF16)

    def give(here, way, k, d, other):
        out, arrived = (up_out, up_in) if way == 0 else (dn_out, dn_in)
        for n in range(2):
            b = 2 * d + n
            out[k, d, n] = pick(expert[b] == here, mix[k][slot[b]], other(b, n))
        push_plane(
            here,
            out.at[k, d],
            arrived.at[k, d],
            ret_r.at[d % 2, k],
            dev_up if way == 0 else dev_dn,
        )

    def turn_in(i, s, j):
        k = chunk(i, s, j)
        for here, way, targets in ((1, 0, (3, 2)), (2, 1, (0, 1))):

            @pl.when(z == here)
            def _():
                with mark(f"turn{k}"):
                    got(end_in[k], end_r.at[k])
                for d in targets:
                    give(here, way, k, d, lambda b, n: end_in[k][slot[b]])

    def carry(i, s, j):
        k = chunk(i, s, j)
        for here, way, d, arrived in ((2, 0, 3, up_in), (1, 1, 0, dn_in)):

            @pl.when(z == here)
            def _():
                with mark(f"carry{k}"):
                    got(arrived.at[k, d], ret_r.at[d % 2, k])
                give(here, way, k, d, lambda b, n: arrived[k, d, n])

    def target(side, i, which, j):
        return out_ref.at[
            pl.ds(pl.multiple_of(side * core_rows + i * group_rows, group_rows), group_rows),
            pl.ds(pl.multiple_of(which * half + j * SPAN, SPAN), SPAN),
        ]

    def arrive(i, s, j, d):
        k = chunk(i, s, j)

        @pl.when(z == d)
        def _():
            with mark(f"arrive{k}"):
                if d > 1:
                    got(up_in.at[k, d], ret_r.at[d % 2, k])
                if d < PLANES - 2:
                    got(dn_in.at[k, d], ret_r.at[d % 2, k])
            for n in range(2):
                b = 2 * d + n
                value = mix[k][slot[b]]
                if d > 0:
                    lower = up_in[k, d, n] if d > 1 else end_in[k][slot[b]]
                    value = pick(expert[b] < d, lower, value)
                if d < PLANES - 1:
                    higher = dn_in[k, d, n] if d < PLANES - 2 else end_in[k][slot[b]]
                    value = pick(expert[b] > d, higher, value)
                fin[k, n] = value
            mine = target(c, i, y, j)
            device = dev_y if s == 0 else dev_yc
            push(fin.at[k, yo], mine, last_r.at[0], device, final_lot)
            if s == 0:
                mine[...] = fin[k, y]
            else:
                push(fin.at[k, y], mine, last_r.at[0], dev_c, final_lot)

    def arrive_end(i, s, j):
        arrive(i, s, j, 0)
        arrive(i, s, j, PLANES - 1)

    def arrive_middle(i, s, j):
        arrive(i, s, j, 1)
        arrive(i, s, j, 2)

    every = [(i, s, j) for i in range(GROUPS) for s, j in pieces]
    for g in parts_last[:3]:
        hide(g)
    down(0)
    hide(parts_last[3])
    down(1)
    down(2)
    stages = (
        (0, blend),
        (4, turn_in),
        (9, carry),
        (12, arrive_middle),
        (16, arrive_end),
    )
    for n in range(len(every) + stages[-1][0]):
        if n == len(pieces):
            down(3)
        for lag, stage in stages:
            if 0 <= n - lag < len(every):
                stage(*every[n - lag])
    with mark("lastwait"):
        wait_for(3 * size_of(out_ref) // 4, last_r.at[0])

    def all_sent(sem, amount):
        if amount:
            ref = w_buf.at[0, pl.ds(0, amount // (2 * units))]
            remote(ref, ref, sem, hid_r.at[0], dev_y).wait_send()

    with mark("drain"):
        for lot, amount in enumerate(all_lots):
            all_sent(sent.at[lot], amount)
        all_sent(sent.at[relay_lot], 2 * size_of(x_buf.at[0, 0, 0]))
        all_sent(sent.at[final_lot], 3 * size_of(out_ref) // 4)
        for plane in range(PLANES):

            @pl.when(z == plane)
            def _():
                for lot, amount in enumerate(plane_lots[plane]):
                    all_sent(plane_sent.at[lot], amount)


def local(
    queries, keys, values, residual_in, norm_gain, routing, gate_weight, up_weight, down_weight
):
    seq_count = lax.axis_size("seq")
    tp_count = lax.axis_size("tp")
    rows, width = queries.shape
    units = gate_weight.shape[2]
    planes = seq_count // 2
    fits = (
        tp_count == 4
        and seq_count == 2 * PLANES
        and rows == BLOCK
        and WINDOW == 4 * rows
        and units == 128
        and width == 8 * HEAD_DIM
    )
    if not fits:
        return local_general(
            queries,
            keys,
            values,
            residual_in,
            norm_gain,
            routing,
            gate_weight,
            up_weight,
            down_weight,
        )
    half = width // 2
    heads = half // HEAD_DIM
    most = min(2 * seq_count // planes, seq_count - planes + 1)
    core_rows = rows // 2
    group_rows = core_rows // GROUPS
    wide = half // SPAN
    chunks = GROUPS * 2 * wide
    vmem = pl.BlockSpec(memory_space=pltpu.VMEM)
    anywhere = pl.BlockSpec(memory_space=pltpu.MemorySpace.HBM)
    dma = pltpu.SemaphoreType.DMA

    def room(*shape, kind=BF16):
        return pltpu.VMEM(shape, kind)

    scratch = (
        room(4, heads, 2, 2, rows, HEAD_DIM),
        room(2, heads, 2, 2, rows, HEAD_DIM),
        room(2, heads, 2, rows, HEAD_DIM),
        [room(2 * planes, 2, core_rows, HEAD_DIM) for _ in range(heads)],
        room(2, tp_count, heads, GROUPS, most * group_rows, HEAD_DIM),
        room(heads, GROUPS, most * group_rows, HEAD_DIM),
        room(4, gate_weight.shape[1], units),
        room(2, down_weight.shape[1], width),
        room(GROUPS, most * group_rows, 4 * units, kind=F32),
        room(GROUPS, most * group_rows, 1, kind=F32),
        room(2, GROUPS, most * group_rows, 2 * units),
        room(chunks, most * group_rows, SPAN),
        room(chunks, most * group_rows, SPAN),
        room(chunks, most * group_rows, SPAN, kind=F32),
        [room(most, group_rows, SPAN) for _ in range(chunks)],
        [room(most, group_rows, SPAN) for _ in range(chunks)],
        room(chunks, planes, 2, group_rows, SPAN),
        room(chunks, planes, 2, group_rows, SPAN),
        room(chunks, planes, 2, group_rows, SPAN),
        room(chunks, planes, 2, group_rows, SPAN),
        room(chunks, 2, group_rows, SPAN),
        dma((1,)),
        dma((1,)),
        dma((1,)),
        dma((2, heads)),
        dma((2 * heads + 1,)),
        dma((planes, heads)),
        dma((4, heads + GROUPS - 1)),
        dma((1,)),
        dma((GROUPS,)),
        dma((chunks,)),
        dma((chunks,)),
        dma((2, chunks)),
        dma((1,)),
        dma((9,)),
        dma((4,)),
    )
    flat, tree = jax.tree.flatten(scratch, is_leaf=lambda leaf: not isinstance(leaf, (list, tuple)))

    def kernel(*refs):
        layer_kernel(most, refs[:9], refs[9], jax.tree.unflatten(tree, refs[10:]))

    return pl.pallas_call(
        kernel,
        name="layer",
        out_shape=pltpu.VMEM((rows, width), BF16),
        in_specs=[pl.BlockSpec(memory_space=pltpu.SMEM)]
        + [anywhere] * 4
        + [vmem]
        + [anywhere] * 3,
        out_specs=vmem,
        scratch_shapes=flat,
        compiler_params=pltpu.CompilerParams(
            collective_id=0, has_side_effects=True, vmem_limit_bytes=67043328 - 2 * rows * width
        ),
    )(
        routing.reshape(-1),
        queries,
        keys,
        values,
        residual_in,
        norm_gain.reshape(1, -1),
        gate_weight,
        up_weight,
        down_weight,
    )


def solution(mesh):
    in_specs = (
        P("seq", "tp"),
        P("seq", "tp"),
        P("seq", "tp"),
        P("seq", "tp"),
        P(),
        P(),
        P("seq", None, "tp"),
        P("seq", None, "tp"),
        P("seq", None, "tp"),
    )
    out_specs = P("seq", "tp")
    return jax.shard_map(local, mesh=mesh, in_specs=in_specs, out_specs=out_specs, check_vma=False)
```

```python
import contextlib
import math

import jax
import jax.numpy as jnp
from jax import lax
from jax.experimental import pallas as pl
from jax.experimental.pallas import tpu as pltpu
from jax.sharding import PartitionSpec as P

HEAD_DIM = 128
BLOCK = 128
WINDOW = 512


epsilon = 1e-05
masked_score = -1e30


def shifted(block, axis, distance):
    devices = range(lax.axis_size(axis))
    route = [(i - distance, i) for i in devices if i - distance in devices]
    return lax.ppermute(block, axis, route)


def local_general(
    queries, keys, values, residual_in, norm_gain, routing, gate_weight, up_weight, down_weight
):
    seq_count = lax.axis_size("seq")
    seq_place = lax.axis_index("seq")
    tok_rows = queries.shape[0]
    feat_width = queries.shape[1]
    head_count = feat_width // HEAD_DIM
    prior_count = (WINDOW - 1) // tok_rows + 1
    earlier_keys = []
    earlier_values = []
    for distance in range(1, prior_count + 1):
        moved_keys, moved_values = shifted((keys, values), "seq", distance)
        earlier_keys.insert(0, moved_keys)
        earlier_values.insert(0, moved_values)
    key_all = jnp.concatenate(earlier_keys + [keys], axis=0).reshape(-1, head_count, HEAD_DIM)
    value_all = jnp.concatenate(earlier_values + [values], axis=0).reshape(-1, head_count, HEAD_DIM)
    query_heads = queries.reshape(tok_rows, head_count, HEAD_DIM)
    query_pos = seq_place * tok_rows + jnp.arange(tok_rows, dtype=jnp.int32)
    key_pos = (
        seq_place * tok_rows
        - prior_count * tok_rows
        + jnp.arange((prior_count + 1) * tok_rows, dtype=jnp.int32)
    )
    visible = (
        (key_pos[None, :] >= 0)
        & (key_pos[None, :] <= query_pos[:, None])
        & (key_pos[None, :] > query_pos[:, None] - WINDOW)
    )
    scores = jnp.einsum(
        "qhd,khd->hqk", query_heads, key_all, preferred_element_type=jnp.float32
    ) * (1.0 / math.sqrt(HEAD_DIM))
    scores = jnp.where(visible[None], scores, masked_score)
    top_score = jnp.max(scores, axis=2, keepdims=True)
    expo = jnp.exp(scores - top_score)
    weights_soft = (expo / jnp.sum(expo, axis=2, keepdims=True)).astype(jnp.bfloat16)
    attended = jnp.einsum(
        "hqk,khd->qhd", weights_soft, value_all, preferred_element_type=jnp.float32
    ).reshape(tok_rows, feat_width)
    stream = (residual_in.astype(jnp.float32) + attended).astype(jnp.bfloat16)
    send_width = stream.shape[1]
    blocks_dev = tok_rows // BLOCK
    piece_rows = BLOCK // seq_count
    spread_in = stream.reshape(blocks_dev, seq_count, piece_rows, send_width)
    spread_out = lax.all_to_all(spread_in, "seq", split_axis=1, concat_axis=0, tiled=True)
    block_count = blocks_dev * seq_count
    spread_rows = spread_out.reshape(block_count, piece_rows, send_width)
    expert_ids = routing[:, 0]
    expert_count = seq_count // 2
    most_blocks = min(2 * block_count // expert_count, block_count - expert_count + 1)
    order_index = jnp.arange(block_count, dtype=jnp.int32)
    same_expert = expert_ids[None, :] == expert_ids[:, None]
    rank_of = jnp.sum(same_expert & (order_index[None, :] < order_index[:, None]), axis=1)
    expert_range = jnp.arange(expert_count, dtype=jnp.int32)
    slot_range = jnp.arange(most_blocks, dtype=jnp.int32)
    selector = (
        (expert_ids[None, None, :] == expert_range[:, None, None])
        & (rank_of[None, None, :] == slot_range[None, :, None])
    ).astype(jnp.bfloat16)
    picked = jnp.einsum(
        "erb,bqf->erqf", selector, spread_rows, preferred_element_type=jnp.float32
    ).astype(jnp.bfloat16)
    outgoing = jnp.broadcast_to(
        picked[:, None], (expert_count, 2, most_blocks, piece_rows, send_width)
    )
    outgoing = outgoing.reshape(seq_count, most_blocks, piece_rows, send_width)
    features_full = lax.all_gather(
        lax.all_to_all(outgoing, "seq", split_axis=0, concat_axis=0, tiled=True),
        "tp",
        axis=3,
        tiled=True,
    )
    source_count = features_full.shape[0]
    slot_count = features_full.shape[1]
    stream_f32 = features_full.astype(jnp.float32)
    mean_square = jnp.mean(stream_f32 * stream_f32, axis=3, keepdims=True)
    normed = (stream_f32 * lax.rsqrt(mean_square + epsilon) * norm_gain).astype(jnp.bfloat16)
    normed = normed.reshape(-1, normed.shape[3])
    gate_val = jnp.dot(normed, gate_weight[0], preferred_element_type=jnp.float32)
    up_val = jnp.dot(normed, up_weight[0], preferred_element_type=jnp.float32)
    hidden = (jax.nn.silu(gate_val) * up_val).astype(jnp.bfloat16)
    hidden_half = lax.all_gather(hidden, "tp", axis=1, tiled=True)
    partial_value = jnp.dot(hidden_half, down_weight[0], preferred_element_type=jnp.float32).astype(
        jnp.bfloat16
    )
    partial_value = partial_value.reshape(source_count, slot_count, piece_rows, feat_width)
    returned = lax.all_to_all(partial_value, "seq", split_axis=0, concat_axis=0, tiled=True)
    returned = returned.reshape(expert_count, 2, most_blocks, piece_rows * feat_width)
    combined = jnp.einsum("erb,epry->pby", selector, returned, preferred_element_type=jnp.float32)
    residual_rows = spread_rows
    residual_rows = residual_rows.reshape(block_count, piece_rows * feat_width).astype(jnp.float32)
    finished = (residual_rows + combined[0] + combined[1]).astype(jnp.bfloat16)
    finished = finished.reshape(seq_count, blocks_dev, piece_rows, feat_width)
    restored = lax.all_to_all(finished, "seq", split_axis=0, concat_axis=2, tiled=True)
    return restored.reshape(tok_rows, feat_width)


BF16 = jnp.bfloat16
F32 = jnp.float32
PLANES = 4
GROUPS = 4
SPAN = 2 * HEAD_DIM
STAY_HEAD = 3


def mark(name):
    return contextlib.nullcontext()


def remote(src, dst, send_sem, recv_sem, device):
    return pltpu.make_async_remote_copy(
        src_ref=src,
        dst_ref=dst,
        send_sem=send_sem,
        recv_sem=recv_sem,
        device_id=device,
        device_id_type=pl.DeviceIdType.MESH,
    )


def size_of(ref):
    return math.prod(ref.shape) * ref.dtype.itemsize


def layer_kernel(most, arguments, out_ref, scratch):
    routing_ref, q_ref, k_ref, v_ref, r_ref, gain_ref, gate_ref, up_ref, down_ref = arguments
    (
        kv_buf,
        qr_buf,
        away,
        line,
        x_buf,
        x_other,
        w_buf,
        d_buf,
        acc_buf,
        square_buf,
        hid_buf,
        b_out,
        b_in,
        part,
        mix,
        end_in,
        up_out,
        up_in,
        dn_out,
        dn_in,
        fin,
        home_in,
        far_in,
        own_s,
        away_s,
        weight_s,
        swap_r,
        kv_r,
        line_r,
        feat_r,
        weight_r,
        hid_r,
        branch_r,
        end_r,
        ret_r,
        last_r,
        home_r,
        far_r,
        sent,
        plane_sent,
    ) = scratch
    rows = q_ref.shape[0]
    half = q_ref.shape[1] // 2
    heads = half // HEAD_DIM
    units = gate_ref.shape[2]
    features = gain_ref.shape[1]
    core_rows = rows // 2
    group_rows = core_rows // GROUPS
    me = lax.axis_index("seq")
    t = lax.axis_index("tp")
    z = me // 2
    y = me % 2
    x = t // 2
    c = t % 2
    yo, xo, co = 1 - y, 1 - x, 1 - c
    tc = 2 * x + co
    tx = 2 * xo + c
    txc = 2 * xo + co
    mate = 2 * z + yo
    dev_y, dev_yc = (mate, t), (mate, tc)
    dev_x, dev_xc = (me, tx), (me, txc)
    dev_c = (me, tc)
    dev_up, dev_dn = (me + 2, t), (me - 2, t)
    has_up, has_dn = z < PLANES - 1, z > 0

    limit = size_of(w_buf.at[0])
    all_lots = [0]
    plane_lots = [[0] for _ in range(PLANES)]

    def lot_for(lots, ref):
        if lots[-1] + size_of(ref) > limit:
            lots.append(0)
        lots[-1] += size_of(ref)
        return len(lots) - 1

    relay_lot = sent.shape[0] - 1

    def push(src, dst, recv_sem, device, lot=None):
        lot = lot_for(all_lots, src) if lot is None else lot
        remote(src, dst, sent.at[lot], recv_sem, device).start()

    def push_plane(plane, src, dst, recv_sem, device):
        lot = lot_for(plane_lots[plane], src)
        remote(src, dst, plane_sent.at[lot], recv_sem, device).start()

    def got(ref, recv_sem):
        remote(ref, ref, sent.at[0], recv_sem, dev_y).wait_recv()

    def wait_for(amount, recv_sem):
        got(w_buf.at[0, pl.ds(0, amount // (2 * units))], recv_sem)

    def loaded(ref, sem):
        pltpu.make_async_copy(ref, ref, sem).wait()

    barrier = pltpu.get_barrier_semaphore()

    def greet(device):
        pl.semaphore_signal(
            barrier, inc=1, device_id=device, device_id_type=pl.DeviceIdType.MESH
        )

    for device in (dev_y, dev_yc, dev_c, dev_x, dev_xc):
        greet(device)
    pl.when(has_up)(lambda: greet(dev_up))
    pl.when(has_dn)(lambda: greet(dev_dn))

    def cols(which, h):
        return pl.ds(pl.multiple_of(which * half + h * HEAD_DIM, HEAD_DIM), HEAD_DIM)

    sources = ((k_ref, v_ref), (q_ref, r_ref))

    def place(kind, h, n, block):
        buf = kv_buf if kind == 0 else qr_buf
        return buf.at[0, h, n, block]

    def load_own(kind, h):
        for n, ref in enumerate(sources[kind]):
            pltpu.make_async_copy(
                ref.at[:, cols(y, h)], place(kind, h, n, y), own_s.at[0]
            ).start()

    def load_away(kind, h):
        for n, ref in enumerate(sources[kind]):
            pltpu.make_async_copy(
                ref.at[:, cols(yo, h)], away.at[kind, h, n], away_s.at[0]
            ).start()

    def swap(kind, h):
        buf = kv_buf if kind == 0 else qr_buf
        push(away.at[kind, h], buf.at[0, h, :, y], swap_r.at[kind, h], dev_y)

    def own(kind, h):
        buf = kv_buf if kind == 0 else qr_buf
        got(buf.at[0, h, :, yo], swap_r.at[kind, h])

    for kind in range(2):
        for h in range(heads):
            load_away(kind, h)
    for kind in range(2):
        for h in range(heads):
            load_own(kind, h)

    expert = [routing_ref[b] for b in range(2 * PLANES)]
    slot = []
    for b in range(2 * PLANES):
        count = jnp.int32(0)
        for j in range(b):
            count = count + jnp.where(expert[j] == expert[b], 1, 0)
        slot.append(jnp.minimum(count, most - 1))
    chosen = []
    for r in range(most):
        index = jnp.int32(0)
        for b in range(2 * PLANES):
            index = jnp.where((expert[b] == z) & (slot[b] == r), b, index)
        chosen.append(index)

    with mark("barwait"):
        pl.semaphore_wait(barrier, 5 + jnp.where(has_up, 1, 0) + jnp.where(has_dn, 1, 0))

    low_order = ((0, 3), (0, 0), (1, 3), (1, 0), (0, 1), (1, 1), (0, 2), (1, 2))
    high_order = ((0, 0), (1, 0), (0, 3), (0, 1), (1, 1), (1, 3), (0, 2), (1, 2))

    with mark("away"):
        loaded(away, away_s.at[0])

    @pl.when(z < 2)
    def _():
        for kind, h in low_order:
            swap(kind, h)

    all_lots[:] = [0]

    @pl.when(z >= 2)
    def _():
        for kind, h in high_order:
            swap(kind, h)

    with mark("ownwait"):
        loaded(away, own_s.at[0])
    row_at = lax.broadcasted_iota(jnp.int32, (rows, rows), 0)
    col_at = lax.broadcasted_iota(jnp.int32, (rows, rows), 1)
    below, above, farther = 1, 2, 3

    def attend(here, plane, h):
        side = 0 if plane == here else 1
        keep = {here: 0, here - 1: below, here + 1: above, here - 2: farther}
        reach = WINDOW // rows
        for n in range(2):
            block = 2 * plane + n
            seen = [
                (back, keep[(block - back) // 2], (block - back) % 2)
                for back in range(reach + 1)
                if block >= back
            ]
            query = qr_buf[side, h, 0, n]
            parts = []
            for back, at, odd in seen:
                score = lax.dot_general(
                    query,
                    kv_buf[at, h, 0, odd],
                    (((1,), (1,)), ((), ())),
                    preferred_element_type=F32,
                )
                if back == 0:
                    score = jnp.where(col_at <= row_at, score, masked_score)
                if back == reach:
                    score = jnp.where(col_at > row_at, score, masked_score)
                parts.append(score)
            top = parts[0]
            for score in parts[1:]:
                top = jnp.maximum(top, score)
            top = jnp.max(top, axis=1, keepdims=True)
            parts = [jnp.exp((score - top) * (1.0 / math.sqrt(HEAD_DIM))) for score in parts]
            total = parts[0]
            for score in parts[1:]:
                total = total + score
            share = 1.0 / jnp.sum(total, axis=1, keepdims=True)
            attended = jnp.dot(
                jnp.concatenate([(score * share).astype(BF16) for score in parts], axis=1),
                jnp.concatenate([kv_buf[at, h, 1, odd] for _, at, odd in seen], axis=0),
                preferred_element_type=F32,
            )
            stream = (qr_buf[side, h, 1, n].astype(F32) + attended).astype(BF16)
            line[h][block] = stream.reshape(2, core_rows, HEAD_DIM)

    def device_at(way):
        return dev_up if way > 0 else dev_dn

    def kv_sem(at, h):
        return kv_r.at[2 * heads if at == farther else (at - 1) * heads + h]

    def send_kv(here, way, src, dst, h):
        push_plane(here, kv_buf.at[src, h], kv_buf.at[dst, h], kv_sem(dst, h), device_at(way))

    def got_kv(at, h):
        got(kv_buf.at[at, h], kv_sem(at, h))

    def send_part(here, way, kind, h, block):
        at = below if way > 0 else above
        buf, to = (kv_buf, at) if kind == 0 else (qr_buf, 1)
        push_plane(
            here, buf.at[0, h, :, block], buf.at[to, h, :, block], kv_sem(at, h), device_at(way)
        )

    def send_home(here, way, h, kinds=(0,)):
        for kind in kinds:
            send_part(here, way, kind, h, y)

    def got_above(h):
        wait_for(size_of(kv_buf.at[0, h]) + size_of(qr_buf.at[0, h]), kv_sem(above, h))

    def send_line(here, way, plane, h):
        ref = line[h].at[pl.ds(2 * plane, 2)]
        push_plane(here, ref, ref, line_r.at[plane, h], device_at(way))

    def got_line(plane, h):
        got(line[h].at[pl.ds(2 * plane, 2)], line_r.at[plane, h])

    taken = [set() for _ in range(PLANES)]

    def made(here, plane, h, hold=False):
        taken[here].add((plane, h))
        with mark(f"attend{plane}_{h}"):
            attend(here, plane, h)
        if here < PLANES - 1 and not hold:
            send_line(here, 1, plane, h)
        if here > 0:
            send_line(here, -1, plane, h)

    def pass_on(here, way, plane, h):
        with mark(f"pass{plane}_{h}"):
            taken[here].add((plane, h))
            got_line(plane, h)
            send_line(here, way, plane, h)

    def steps_0(step):
        if step == 0:
            for kind, h in low_order:
                with mark(f"own{kind}_{h}"):
                    own(kind, h)
                if kind == 0:
                    send_part(0, 1, 0, h, yo)
                else:
                    made(0, 0, h)

    def steps_1(step):
        def first(h):
            with mark(f"own0_{h}"):
                own(0, h)
            send_part(1, 1, 0, h, yo)

        def home(h):
            with mark(f"own1_{h}"):
                own(1, h)
                got_kv(below, h)
            if h == STAY_HEAD:
                send_kv(1, 1, below, farther, h)
            made(1, 1, h)

        def lower(h):
            with mark(f"lower{h}"):
                got_above(h)
            made(1, 2, h)

        if step == 0:
            first(3)
            first(0)
            home(3)
            first(1)
            home(0)
            lower(0)
            pass_on(1, 1, 0, 3)
            pass_on(1, 1, 0, 0)
            first(2)
            home(1)
            lower(1)
            pass_on(1, -1, 3, 0)
        if step == 1:
            pass_on(1, 1, 0, 1)
            home(2)
            pass_on(1, 1, 0, 2)
            pass_on(1, -1, 3, 1)
        if step == 2:
            pass_on(1, -1, 2, 3)
            pass_on(1, -1, 3, 3)
        if step == 3:
            lower(2)
        if step == 4:
            pass_on(1, -1, 3, 2)

    def steps_2(step):
        def first(h):
            with mark(f"own0_{h}"):
                own(0, h)
            send_part(2, 1 if h == STAY_HEAD else -1, 0, h, yo)

        def second(h):
            with mark(f"own1_{h}"):
                own(1, h)
            if h != STAY_HEAD:
                send_part(2, -1, 1, h, yo)

        def lower(h, hold=False):
            with mark(f"lower{h}"):
                got_above(h)
                got_kv(below, h)
            made(2, 3, h, hold)

        if step == 0:
            first(0)
            second(0)
            first(3)
            first(1)
            with mark("below3"):
                got_kv(below, 3)
            send_kv(2, 1, below, farther, 3)
            second(1)
            send_home(2, -1, 2, (0, 1))
            lower(0)
            second(3)
            with mark("farther3"):
                got_kv(farther, 3)
            made(2, 2, 3)
            pass_on(2, 1, 1, 3)
            lower(1)
            pass_on(2, -1, 3, 3)
            first(2)
            second(2)
            pass_on(2, 1, 1, 0)
            pass_on(2, 1, 0, 3)
        if step == 1:
            pass_on(2, 1, 2, 0)
            pass_on(2, 1, 0, 0)
        if step == 2:
            lower(2, True)
            pass_on(2, 1, 1, 1)
            pass_on(2, 1, 2, 1)
        if step == 3:
            pass_on(2, 1, 0, 1)
            send_line(2, 1, 3, 2)
        if step == 4:
            pass_on(2, 1, 1, 2)
            pass_on(2, 1, 0, 2)
            pass_on(2, 1, 2, 2)

    def steps_3(step):
        if step == 0:
            for kind, h in high_order:
                with mark(f"own{kind}_{h}"):
                    own(kind, h)
                if h != STAY_HEAD:
                    send_part(3, -1, kind, h, yo)
                    if (kind, h) == (1, 1):
                        send_home(3, -1, 2, (0, 1))
                elif kind == 1:
                    with mark("below3"):
                        got_kv(below, 3)
                        got_kv(farther, 3)
                    made(3, 3, 3)

    def early(plane):
        if plane < 2:
            for h in (3, 0, 1, 2):
                send_home(plane, 1, h)
        else:
            for h in (0, 1):
                send_home(plane, -1, h, (0, 1))
            if plane == 2:
                send_home(plane, 1, STAY_HEAD)

    for plane in range(PLANES):
        pl.when(z == plane)(lambda: early(plane))

    def planes(step):
        for plane, steps in enumerate((steps_0, steps_1, steps_2, steps_3)):

            @pl.when(z == plane)
            def _():
                steps(step)

    def collect(order, pos):
        h = order[pos]
        for plane in range(PLANES):
            if orders[plane // 2][pos] != h:
                continue

            @pl.when(z == plane)
            def _():
                for other in range(PLANES):
                    if (other, h) not in taken[plane]:
                        taken[plane].add((other, h))
                        got_line(other, h)

    high = jnp.where(z < 2, 0, 1)
    orders = ((0, 1, 3, 2), (3, 0, 1, 2))
    heads_at = [low + high * (up - low) for low, up in zip(*orders)]
    ends = len(heads_at) - 1

    def groups_of(pos):
        return [pl.ds(g, 1) for g in range(GROUPS)] if pos == ends else [pl.ds(0, GROUPS)]

    def feature_at(pos, g):
        return pos + g.start

    def feature(n, py, pt, pos, g, device, src=None, lot=None):
        ref = x_buf.at[py, pt, heads_at[pos], g]
        src = ref if src is None else src
        push(src, ref, feat_r.at[lot_of[n], feature_at(pos, g)], device, lot)

    lot_of = (0, 0, 1, 2, 0, 3, 3)
    arrivals = (
        (y, tc),
        (y, tx),
        (y, txc),
        (yo, t),
        (yo, tc),
        (yo, tx),
        (yo, txc),
    )

    def take(n, pos, g):
        py, pt = arrivals[n]
        got(x_buf.at[py, pt, heads_at[pos], g], feat_r.at[lot_of[n], feature_at(pos, g)])

    def choose(h, g):
        for r in range(most):
            at = pl.ds(r * group_rows, group_rows)
            for ref, side in ((x_buf.at[y, t, h], c), (x_other.at[h], co)):
                block = line[h][chosen[r], side]
                for i in range(GROUPS):
                    if g.start <= i < g.start + g.size:
                        ref[i, at] = block[i * group_rows : (i + 1) * group_rows]

    def gather(pos):
        with mark(f"collect{pos}"):
            for order in orders:
                if order is orders[0] or order[pos] != orders[0][pos]:
                    collect(order, pos)

    def first_stage(pos, lots=None):
        for g in lots or groups_of(pos):
            if orders[0][pos] == orders[1][pos]:
                choose(orders[0][pos], g)
            else:
                pl.when(z < 2)(lambda: choose(orders[0][pos], g))
                pl.when(z >= 2)(lambda: choose(orders[1][pos], g))
            other = x_other.at[heads_at[pos], g]
            feature(3, y, t, pos, g, dev_y)
            feature(2, y, t, pos, g, dev_xc, other)
            feature(1, y, t, pos, g, dev_x)
            feature(4, y, t, pos, g, dev_yc, other)
            feature(0, y, t, pos, g, dev_c, other)

    def second_stage(pos, g, lot=None):
        take(3, pos, g)
        feature(5, yo, t, pos, g, dev_x, lot=lot)
        take(2, pos, g)
        feature(6, y, txc, pos, g, dev_y, lot=lot)

    def near(pos, g):
        wait_for(3 * size_of(x_buf.at[y, t, 0, g]), feat_r.at[0, feature_at(pos, g)])

    def far(pos, g):
        wait_for(2 * size_of(x_buf.at[y, t, 0, g]), feat_r.at[3, feature_at(pos, g)])

    def expert_parts(parts, pos, g):
        depth = g.size * most * group_rows
        left, right = [], []
        square = square_buf[g].reshape(depth, 1)
        for py, pt in parts:
            start = pl.multiple_of((2 * pt + py) * half + heads_at[pos] * HEAD_DIM, HEAD_DIM)
            value = x_buf[py, pt, heads_at[pos], g].reshape(depth, HEAD_DIM).astype(F32)
            square = square + jnp.sum(value * value, axis=1, keepdims=True)
            left.append((value * gain_ref[:, pl.ds(start, HEAD_DIM)]).astype(BF16))
            right.append(
                jnp.concatenate(
                    [w_buf[i, pl.ds(start, HEAD_DIM), :] for i in range(4)], axis=1
                )
            )
        square_buf[g] = square.reshape(g.size, most * group_rows, 1)
        acc_buf[g] += jnp.dot(
            jnp.concatenate(left, axis=1),
            jnp.concatenate(right, axis=0),
            preferred_element_type=F32,
        ).reshape(g.size, most * group_rows, 4 * units)

    every_part = [(y, t)] + list(arrivals)

    parts_last = groups_of(ends)
    both = groups_of(0)[0]
    planes(0)
    weights = (
        (gate_ref.at[0], w_buf.at[c]),
        (up_ref.at[0], w_buf.at[2 + c]),
        (down_ref.at[0], d_buf.at[c]),
    )
    for src, dst in weights:
        pltpu.make_async_copy(src, dst, weight_s.at[0]).start()
        push(src, dst, weight_r.at[0], dev_c)

    gather(0)
    first_stage(0)
    planes(1)

    @pl.when(z == 0)
    def _():
        with mark("second0"):
            second_stage(0, both, relay_lot)

    gather(1)
    first_stage(1)
    planes(2)

    @pl.when(z > 0)
    def _():
        with mark("second0"):
            second_stage(0, both, relay_lot)

    planes(3)
    gather(2)
    first_stage(2)
    with mark("second1"):
        second_stage(1, both)
    planes(4)
    gather(3)
    first_stage(3, parts_last[:1])
    with mark("second2"):
        second_stage(2, both)
    first_stage(3, parts_last[1:])
    acc_buf[...] = jnp.zeros_like(acc_buf)
    square_buf[...] = jnp.zeros_like(square_buf)
    with mark("weights"):
        every = w_buf.at[pl.ds(0, len(weights))]
        loaded(every, weight_s.at[0])
        got(every, weight_r.at[0])

    def whole(pos):
        with mark(f"feat{pos}"):
            near(pos, both)
            far(pos, both)
        with mark(f"expert{pos}"):
            expert_parts(every_part, pos, both)

    def relay_last(g):
        with mark(f"secondL{g.start}"):
            second_stage(ends, g)

    def hide(g):
        i = g.start
        with mark(f"nearL{i}"):
            near(ends, g)
        with mark(f"farL{i}"):
            far(ends, g)
        with mark(f"expertL{i}"):
            expert_parts(every_part, ends, g)
            scale = lax.rsqrt(square_buf[i] * (1.0 / features) + epsilon)
            gate_val = acc_buf[i, :, pl.ds(0, 2 * units)] * scale
            up_val = acc_buf[i, :, pl.ds(2 * units, 2 * units)] * scale
            hid_buf[x, i] = (gate_val / (1.0 + jnp.exp(-gate_val)) * up_val).astype(BF16)
        push(hid_buf.at[x, i], hid_buf.at[x, i], hid_r.at[i], dev_x)

    whole(0)
    relay_last(parts_last[0])
    whole(1)
    relay_last(parts_last[1])
    whole(2)
    for g in parts_last[2:]:
        relay_last(g)

    wide = half // SPAN
    pieces = [(s, j) for s in range(2) for j in range(wide)]

    def chunk(i, s, j):
        return (i * 2 + s) * wide + j

    pair = 2 * SPAN
    per = SPAN // HEAD_DIM

    def branch(i, s, which, j):
        hidden = jnp.concatenate([hid_buf[n, i] for n in range(2)], axis=1)
        at = pl.ds(pl.multiple_of(which * half + j * pair, pair), pair)
        weight = d_buf[c if s == 0 else co, :, at]
        value = jnp.dot(hidden, weight, preferred_element_type=F32).astype(BF16)
        return [(chunk(i, s, 2 * j + m), value[:, m * SPAN : (m + 1) * SPAN]) for m in range(2)]

    def down(i):
        with mark(f"hid{i}"):
            got(hid_buf.at[xo, i], hid_r.at[i])
        with mark(f"down{i}"):
            doubles = [(s, j) for s in range(2) for j in range(wide // 2)]
            for s, j in doubles:
                for k, value in branch(i, s, yo, j):
                    b_out[k] = value
                    push(b_out.at[k], b_in.at[k], branch_r.at[k], dev_y)
            for s, j in doubles:
                for m, (k, value) in enumerate(branch(i, s, y, j)):
                    stream = jnp.concatenate(
                        [
                            x_buf[y, t if s == 0 else tc, (2 * j + m) * per + q, i]
                            for q in range(per)
                        ],
                        axis=1,
                    )
                    part[k] = stream.astype(F32) + value.astype(F32)

    def blend(i, s, j):
        k = chunk(i, s, j)
        with mark(f"blend{k}"):
            got(b_in.at[k], branch_r.at[k])
            total = part[k] + b_in[k].astype(F32)
            mix[k][...] = total.astype(BF16).reshape(most, group_rows, SPAN)
        for plane, device in ((0, dev_up), (PLANES - 1, dev_dn)):

            @pl.when(z == plane)
            def _():
                push_plane(plane, mix[k], end_in[k], end_r.at[k], device)

    def pick(flag, a, b):
        mask = jnp.full(a.shape, flag.astype(jnp.int32), jnp.int32) > 0
        return jnp.where(mask, a.astype(F32), b.astype(F32)).astype(BF16)

    def give(here, way, k, d, other):
        out, arrived = (up_out, up_in) if way == 0 else (dn_out, dn_in)
        for n in range(2):
            b = 2 * d + n
            out[k, d, n] = pick(expert[b] == here, mix[k][slot[b]], other(b, n))
        push_plane(
            here,
            out.at[k, d],
            arrived.at[k, d],
            ret_r.at[d % 2, k],
            dev_up if way == 0 else dev_dn,
        )

    def turn_in(i, s, j):
        k = chunk(i, s, j)
        for here, way, targets in ((1, 0, (3, 2)), (2, 1, (0, 1))):

            @pl.when(z == here)
            def _():
                with mark(f"turn{k}"):
                    got(end_in[k], end_r.at[k])
                for d in targets:
                    give(here, way, k, d, lambda b, n: end_in[k][slot[b]])

    def carry(i, s, j):
        k = chunk(i, s, j)
        for here, way, d, out, arrived in ((2, 0, 3, up_out, up_in), (1, 1, 0, dn_out, dn_in)):

            @pl.when(z == here)
            def _():
                with mark(f"carry{k}"):
                    got(arrived.at[k, d], ret_r.at[d % 2, k])
                for n in range(2):
                    b = 2 * d + n
                    out[k, d, n] = pick(expert[b] == here, mix[k][slot[b]], arrived[k, d, n])
                    push_plane(
                        here,
                        out.at[k, d, n],
                        far_in.at[y, c, i, j],
                        far_r.at[i * wide + j],
                        (b, t if s == 0 else tc),
                    )

    def settle(i, s, j):
        k = chunk(i, s, j)
        for d in (0, PLANES - 1):

            @pl.when(z == d)
            def _():
                for n, which in enumerate((y, yo)):
                    at = slot[2 * d] + which * (slot[2 * d + 1] - slot[2 * d])
                    fin[k, n] = mix[k][at]
                there = home_in.at[y, c, i, j]
                sem = home_r.at[i * wide + j]
                push_plane(d, fin.at[k, 1], there, sem, dev_y if s == 0 else dev_yc)
                if s == 0:
                    there[...] = fin[k, 0]
                else:
                    push_plane(d, fin.at[k, 0], there, sem, dev_c)

    def final(i, j):
        for d in (0, PLANES - 1):

            @pl.when(z == d)
            def _():
                with mark(f"final{i}_{j}"):
                    wait_for(3 * size_of(fin.at[0, 0]), home_r.at[i * wide + j])
                    wait_for(4 * size_of(fin.at[0, 0]), far_r.at[i * wide + j])
                flag = jnp.where(y == 0, expert[2 * d], expert[2 * d + 1]) == d
                for half_at in range(2):
                    for side in range(2):
                        at = (half_at, side, i, j)
                        target(side, i, half_at, j)[...] = pick(flag, home_in[at], far_in[at])

    def target(side, i, which, j):
        return out_ref.at[
            pl.ds(pl.multiple_of(side * core_rows + i * group_rows, group_rows), group_rows),
            pl.ds(pl.multiple_of(which * half + j * SPAN, SPAN), SPAN),
        ]

    def arrive(i, s, j, d):
        k = chunk(i, s, j)

        @pl.when(z == d)
        def _():
            with mark(f"arrive{k}"):
                got((up_in if d > 1 else dn_in).at[k, d], ret_r.at[d % 2, k])
            for n in range(2):
                b = 2 * d + n
                lower = up_in[k, d, n] if d > 1 else end_in[k][slot[b]]
                higher = dn_in[k, d, n] if d == 1 else end_in[k][slot[b]]
                value = pick(expert[b] < d, lower, mix[k][slot[b]])
                fin[k, n] = pick(expert[b] > d, higher, value)
            mine = target(c, i, y, j)
            device = dev_y if s == 0 else dev_yc
            push_plane(d, fin.at[k, yo], mine, last_r.at[0], device)
            if s == 0:
                mine[...] = fin[k, y]
            else:
                push_plane(d, fin.at[k, y], mine, last_r.at[0], dev_c)

    def arrive_middle(i, s, j):
        arrive(i, s, j, 1)
        arrive(i, s, j, 2)

    every = [(i, s, j) for i in range(GROUPS) for s, j in pieces]
    for g in parts_last[:3]:
        hide(g)
    down(0)
    hide(parts_last[3])
    down(1)
    down(2)
    stages = (
        (0, blend),
        (4, turn_in),
        (9, carry),
        (12, arrive_middle),
        (16, settle),
    )
    for n in range(len(every) + stages[-1][0]):
        if n == len(pieces):
            down(3)
        for lag, stage in stages:
            if 0 <= n - lag < len(every):
                stage(*every[n - lag])
    with mark("lastwait"):
        for i in range(GROUPS):
            for j in range(wide):
                final(i, j)

        @pl.when((z > 0) & (z < PLANES - 1))
        def _():
            wait_for(3 * size_of(out_ref) // 4, last_r.at[0])

    def all_sent(sem, amount):
        if amount:
            ref = w_buf.at[0, pl.ds(0, amount // (2 * units))]
            remote(ref, ref, sem, hid_r.at[0], dev_y).wait_send()

    with mark("drain"):
        for lot, amount in enumerate(all_lots):
            all_sent(sent.at[lot], amount)
        all_sent(sent.at[relay_lot], 2 * size_of(x_buf.at[0, 0, 0]))
        for plane in range(PLANES):

            @pl.when(z == plane)
            def _():
                for lot, amount in enumerate(plane_lots[plane]):
                    all_sent(plane_sent.at[lot], amount)


def local(
    queries, keys, values, residual_in, norm_gain, routing, gate_weight, up_weight, down_weight
):
    seq_count = lax.axis_size("seq")
    tp_count = lax.axis_size("tp")
    rows, width = queries.shape
    units = gate_weight.shape[2]
    planes = seq_count // 2
    fits = (
        tp_count == 4
        and seq_count == 2 * PLANES
        and rows == BLOCK
        and WINDOW == 4 * rows
        and units == 128
        and width == 8 * HEAD_DIM
    )
    if not fits:
        return local_general(
            queries,
            keys,
            values,
            residual_in,
            norm_gain,
            routing,
            gate_weight,
            up_weight,
            down_weight,
        )
    half = width // 2
    heads = half // HEAD_DIM
    most = min(2 * seq_count // planes, seq_count - planes + 1)
    core_rows = rows // 2
    group_rows = core_rows // GROUPS
    wide = half // SPAN
    chunks = GROUPS * 2 * wide
    vmem = pl.BlockSpec(memory_space=pltpu.VMEM)
    anywhere = pl.BlockSpec(memory_space=pltpu.MemorySpace.HBM)
    dma = pltpu.SemaphoreType.DMA

    def room(*shape, kind=BF16):
        return pltpu.VMEM(shape, kind)

    scratch = (
        room(4, heads, 2, 2, rows, HEAD_DIM),
        room(2, heads, 2, 2, rows, HEAD_DIM),
        room(2, heads, 2, rows, HEAD_DIM),
        [room(2 * planes, 2, core_rows, HEAD_DIM) for _ in range(heads)],
        room(2, tp_count, heads, GROUPS, most * group_rows, HEAD_DIM),
        room(heads, GROUPS, most * group_rows, HEAD_DIM),
        room(4, gate_weight.shape[1], units),
        room(2, down_weight.shape[1], width),
        room(GROUPS, most * group_rows, 4 * units, kind=F32),
        room(GROUPS, most * group_rows, 1, kind=F32),
        room(2, GROUPS, most * group_rows, 2 * units),
        room(chunks, most * group_rows, SPAN),
        room(chunks, most * group_rows, SPAN),
        room(chunks, most * group_rows, SPAN, kind=F32),
        [room(most, group_rows, SPAN) for _ in range(chunks)],
        [room(most, group_rows, SPAN) for _ in range(chunks)],
        room(chunks, planes, 2, group_rows, SPAN),
        room(chunks, planes, 2, group_rows, SPAN),
        room(chunks, planes, 2, group_rows, SPAN),
        room(chunks, planes, 2, group_rows, SPAN),
        room(chunks, 2, group_rows, SPAN),
        room(2, 2, GROUPS, wide, group_rows, SPAN),
        room(2, 2, GROUPS, wide, group_rows, SPAN),
        dma((1,)),
        dma((1,)),
        dma((1,)),
        dma((2, heads)),
        dma((2 * heads + 1,)),
        dma((planes, heads)),
        dma((4, heads + GROUPS - 1)),
        dma((1,)),
        dma((GROUPS,)),
        dma((chunks,)),
        dma((chunks,)),
        dma((2, chunks)),
        dma((1,)),
        dma((GROUPS * wide,)),
        dma((GROUPS * wide,)),
        dma((8,)),
        dma((4,)),
    )
    flat, tree = jax.tree.flatten(scratch, is_leaf=lambda leaf: not isinstance(leaf, (list, tuple)))

    def kernel(*refs):
        layer_kernel(most, refs[:9], refs[9], jax.tree.unflatten(tree, refs[10:]))

    return pl.pallas_call(
        kernel,
        name="layer",
        out_shape=pltpu.VMEM((rows, width), BF16),
        in_specs=[pl.BlockSpec(memory_space=pltpu.SMEM)]
        + [anywhere] * 4
        + [vmem]
        + [anywhere] * 3,
        out_specs=vmem,
        scratch_shapes=flat,
        compiler_params=pltpu.CompilerParams(
            collective_id=0, has_side_effects=True, vmem_limit_bytes=67043328 - 2 * rows * width
        ),
    )(
        routing.reshape(-1),
        queries,
        keys,
        values,
        residual_in,
        norm_gain.reshape(1, -1),
        gate_weight,
        up_weight,
        down_weight,
    )


def solution(mesh):
    in_specs = (
        P("seq", "tp"),
        P("seq", "tp"),
        P("seq", "tp"),
        P("seq", "tp"),
        P(),
        P(),
        P("seq", None, "tp"),
        P("seq", None, "tp"),
        P("seq", None, "tp"),
    )
    out_specs = P("seq", "tp")
    return jax.shard_map(local, mesh=mesh, in_specs=in_specs, out_specs=out_specs, check_vma=False)
```

```python
import contextlib
import math

import jax
import jax.numpy as jnp
from jax import lax
from jax.experimental import pallas as pl
from jax.experimental.pallas import tpu as pltpu
from jax.sharding import PartitionSpec as P

HEAD_DIM = 128
BLOCK = 128
WINDOW = 512


epsilon = 1e-05
masked_score = -1e30


def shifted(block, axis, distance):
    devices = range(lax.axis_size(axis))
    route = [(i - distance, i) for i in devices if i - distance in devices]
    return lax.ppermute(block, axis, route)


def local_general(
    queries, keys, values, residual_in, norm_gain, routing, gate_weight, up_weight, down_weight
):
    seq_count = lax.axis_size("seq")
    seq_place = lax.axis_index("seq")
    tok_rows = queries.shape[0]
    feat_width = queries.shape[1]
    head_count = feat_width // HEAD_DIM
    prior_count = (WINDOW - 1) // tok_rows + 1
    earlier_keys = []
    earlier_values = []
    for distance in range(1, prior_count + 1):
        moved_keys, moved_values = shifted((keys, values), "seq", distance)
        earlier_keys.insert(0, moved_keys)
        earlier_values.insert(0, moved_values)
    key_all = jnp.concatenate(earlier_keys + [keys], axis=0).reshape(-1, head_count, HEAD_DIM)
    value_all = jnp.concatenate(earlier_values + [values], axis=0).reshape(-1, head_count, HEAD_DIM)
    query_heads = queries.reshape(tok_rows, head_count, HEAD_DIM)
    query_pos = seq_place * tok_rows + jnp.arange(tok_rows, dtype=jnp.int32)
    key_pos = (
        seq_place * tok_rows
        - prior_count * tok_rows
        + jnp.arange((prior_count + 1) * tok_rows, dtype=jnp.int32)
    )
    visible = (
        (key_pos[None, :] >= 0)
        & (key_pos[None, :] <= query_pos[:, None])
        & (key_pos[None, :] > query_pos[:, None] - WINDOW)
    )
    scores = jnp.einsum(
        "qhd,khd->hqk", query_heads, key_all, preferred_element_type=jnp.float32
    ) * (1.0 / math.sqrt(HEAD_DIM))
    scores = jnp.where(visible[None], scores, masked_score)
    top_score = jnp.max(scores, axis=2, keepdims=True)
    expo = jnp.exp(scores - top_score)
    weights_soft = (expo / jnp.sum(expo, axis=2, keepdims=True)).astype(jnp.bfloat16)
    attended = jnp.einsum(
        "hqk,khd->qhd", weights_soft, value_all, preferred_element_type=jnp.float32
    ).reshape(tok_rows, feat_width)
    stream = (residual_in.astype(jnp.float32) + attended).astype(jnp.bfloat16)
    send_width = stream.shape[1]
    blocks_dev = tok_rows // BLOCK
    piece_rows = BLOCK // seq_count
    spread_in = stream.reshape(blocks_dev, seq_count, piece_rows, send_width)
    spread_out = lax.all_to_all(spread_in, "seq", split_axis=1, concat_axis=0, tiled=True)
    block_count = blocks_dev * seq_count
    spread_rows = spread_out.reshape(block_count, piece_rows, send_width)
    expert_ids = routing[:, 0]
    expert_count = seq_count // 2
    most_blocks = min(2 * block_count // expert_count, block_count - expert_count + 1)
    order_index = jnp.arange(block_count, dtype=jnp.int32)
    same_expert = expert_ids[None, :] == expert_ids[:, None]
    rank_of = jnp.sum(same_expert & (order_index[None, :] < order_index[:, None]), axis=1)
    expert_range = jnp.arange(expert_count, dtype=jnp.int32)
    slot_range = jnp.arange(most_blocks, dtype=jnp.int32)
    selector = (
        (expert_ids[None, None, :] == expert_range[:, None, None])
        & (rank_of[None, None, :] == slot_range[None, :, None])
    ).astype(jnp.bfloat16)
    picked = jnp.einsum(
        "erb,bqf->erqf", selector, spread_rows, preferred_element_type=jnp.float32
    ).astype(jnp.bfloat16)
    outgoing = jnp.broadcast_to(
        picked[:, None], (expert_count, 2, most_blocks, piece_rows, send_width)
    )
    outgoing = outgoing.reshape(seq_count, most_blocks, piece_rows, send_width)
    features_full = lax.all_gather(
        lax.all_to_all(outgoing, "seq", split_axis=0, concat_axis=0, tiled=True),
        "tp",
        axis=3,
        tiled=True,
    )
    source_count = features_full.shape[0]
    slot_count = features_full.shape[1]
    stream_f32 = features_full.astype(jnp.float32)
    mean_square = jnp.mean(stream_f32 * stream_f32, axis=3, keepdims=True)
    normed = (stream_f32 * lax.rsqrt(mean_square + epsilon) * norm_gain).astype(jnp.bfloat16)
    normed = normed.reshape(-1, normed.shape[3])
    gate_val = jnp.dot(normed, gate_weight[0], preferred_element_type=jnp.float32)
    up_val = jnp.dot(normed, up_weight[0], preferred_element_type=jnp.float32)
    hidden = (jax.nn.silu(gate_val) * up_val).astype(jnp.bfloat16)
    hidden_half = lax.all_gather(hidden, "tp", axis=1, tiled=True)
    partial_value = jnp.dot(hidden_half, down_weight[0], preferred_element_type=jnp.float32).astype(
        jnp.bfloat16
    )
    partial_value = partial_value.reshape(source_count, slot_count, piece_rows, feat_width)
    returned = lax.all_to_all(partial_value, "seq", split_axis=0, concat_axis=0, tiled=True)
    returned = returned.reshape(expert_count, 2, most_blocks, piece_rows * feat_width)
    combined = jnp.einsum("erb,epry->pby", selector, returned, preferred_element_type=jnp.float32)
    residual_rows = spread_rows
    residual_rows = residual_rows.reshape(block_count, piece_rows * feat_width).astype(jnp.float32)
    finished = (residual_rows + combined[0] + combined[1]).astype(jnp.bfloat16)
    finished = finished.reshape(seq_count, blocks_dev, piece_rows, feat_width)
    restored = lax.all_to_all(finished, "seq", split_axis=0, concat_axis=2, tiled=True)
    return restored.reshape(tok_rows, feat_width)


BF16 = jnp.bfloat16
F32 = jnp.float32
PLANES = 4
GROUPS = 4
SPAN = 2 * HEAD_DIM
STAY_HEAD = 3


def mark(name):
    return contextlib.nullcontext()


def remote(src, dst, send_sem, recv_sem, device):
    return pltpu.make_async_remote_copy(
        src_ref=src,
        dst_ref=dst,
        send_sem=send_sem,
        recv_sem=recv_sem,
        device_id=device,
        device_id_type=pl.DeviceIdType.MESH,
    )


def size_of(ref):
    return math.prod(ref.shape) * ref.dtype.itemsize


def layer_kernel(most, arguments, out_ref, scratch):
    routing_ref, q_ref, k_ref, v_ref, r_ref, gain_ref, gate_ref, up_ref, down_ref = arguments
    (
        kv_buf,
        qr_buf,
        away,
        line,
        x_buf,
        x_other,
        w_buf,
        d_buf,
        acc_buf,
        square_buf,
        hid_buf,
        b_out,
        b_in,
        part,
        mix,
        end_in,
        up_out,
        up_in,
        dn_out,
        dn_in,
        fin,
        home_in,
        far_in,
        own_s,
        away_s,
        weight_s,
        swap_r,
        kv_r,
        line_r,
        feat_r,
        weight_r,
        hid_r,
        branch_r,
        end_r,
        ret_r,
        last_r,
        home_r,
        far_r,
        sent,
        plane_sent,
    ) = scratch
    rows = q_ref.shape[0]
    half = q_ref.shape[1] // 2
    heads = half // HEAD_DIM
    units = gate_ref.shape[2]
    features = gain_ref.shape[1]
    core_rows = rows // 2
    group_rows = core_rows // GROUPS
    me = lax.axis_index("seq")
    t = lax.axis_index("tp")
    z = me // 2
    y = me % 2
    x = t // 2
    c = t % 2
    yo, xo, co = 1 - y, 1 - x, 1 - c
    tc = 2 * x + co
    tx = 2 * xo + c
    txc = 2 * xo + co
    mate = 2 * z + yo
    dev_y, dev_yc = (mate, t), (mate, tc)
    dev_x, dev_xc = (me, tx), (me, txc)
    dev_c = (me, tc)
    dev_up, dev_dn = (me + 2, t), (me - 2, t)
    has_up, has_dn = z < PLANES - 1, z > 0

    limit = size_of(w_buf.at[0])
    all_lots = [0]
    plane_lots = [[0] for _ in range(PLANES)]

    def lot_for(lots, ref):
        if lots[-1] + size_of(ref) > limit:
            lots.append(0)
        lots[-1] += size_of(ref)
        return len(lots) - 1

    relay_lot = sent.shape[0] - 1

    def push(src, dst, recv_sem, device, lot=None):
        lot = lot_for(all_lots, src) if lot is None else lot
        remote(src, dst, sent.at[lot], recv_sem, device).start()

    def push_plane(plane, src, dst, recv_sem, device):
        lot = lot_for(plane_lots[plane], src)
        remote(src, dst, plane_sent.at[lot], recv_sem, device).start()

    def got(ref, recv_sem):
        remote(ref, ref, sent.at[0], recv_sem, dev_y).wait_recv()

    def wait_for(amount, recv_sem):
        got(w_buf.at[0, pl.ds(0, amount // (2 * units))], recv_sem)

    def loaded(ref, sem):
        pltpu.make_async_copy(ref, ref, sem).wait()

    barrier = pltpu.get_barrier_semaphore()

    def greet(device):
        pl.semaphore_signal(
            barrier, inc=1, device_id=device, device_id_type=pl.DeviceIdType.MESH
        )

    for device in (dev_y, dev_yc, dev_c, dev_x, dev_xc):
        greet(device)
    pl.when(has_up)(lambda: greet(dev_up))
    pl.when(has_dn)(lambda: greet(dev_dn))

    def cols(which, h):
        return pl.ds(pl.multiple_of(which * half + h * HEAD_DIM, HEAD_DIM), HEAD_DIM)

    sources = ((k_ref, v_ref), (q_ref, r_ref))

    def place(kind, h, n, block):
        buf = kv_buf if kind == 0 else qr_buf
        return buf.at[0, h, n, block]

    def load_own(kind, h):
        for n, ref in enumerate(sources[kind]):
            pltpu.make_async_copy(
                ref.at[:, cols(y, h)], place(kind, h, n, y), own_s.at[0]
            ).start()

    def load_away(kind, h):
        for n, ref in enumerate(sources[kind]):
            pltpu.make_async_copy(
                ref.at[:, cols(yo, h)], away.at[kind, h, n], away_s.at[0]
            ).start()

    def swap(kind, h):
        buf = kv_buf if kind == 0 else qr_buf
        push(away.at[kind, h], buf.at[0, h, :, y], swap_r.at[kind, h], dev_y)

    def own(kind, h):
        buf = kv_buf if kind == 0 else qr_buf
        got(buf.at[0, h, :, yo], swap_r.at[kind, h])

    for kind in range(2):
        for h in range(heads):
            load_away(kind, h)
    for kind in range(2):
        for h in range(heads):
            load_own(kind, h)

    expert = [routing_ref[b] for b in range(2 * PLANES)]
    slot = []
    for b in range(2 * PLANES):
        count = jnp.int32(0)
        for j in range(b):
            count = count + jnp.where(expert[j] == expert[b], 1, 0)
        slot.append(jnp.minimum(count, most - 1))
    chosen = []
    for r in range(most):
        index = jnp.int32(0)
        for b in range(2 * PLANES):
            index = jnp.where((expert[b] == z) & (slot[b] == r), b, index)
        chosen.append(index)

    with mark("barwait"):
        pl.semaphore_wait(barrier, 5 + jnp.where(has_up, 1, 0) + jnp.where(has_dn, 1, 0))

    low_order = ((0, 3), (0, 0), (1, 3), (1, 0), (0, 1), (1, 1), (0, 2), (1, 2))
    high_order = ((0, 0), (1, 0), (0, 3), (0, 1), (1, 1), (1, 3), (0, 2), (1, 2))

    with mark("away"):
        loaded(away, away_s.at[0])

    @pl.when(z < 2)
    def _():
        for kind, h in low_order:
            swap(kind, h)

    all_lots[:] = [0]

    @pl.when(z >= 2)
    def _():
        for kind, h in high_order:
            swap(kind, h)

    with mark("ownwait"):
        loaded(away, own_s.at[0])
    row_at = lax.broadcasted_iota(jnp.int32, (rows, rows), 0)
    col_at = lax.broadcasted_iota(jnp.int32, (rows, rows), 1)
    below, above, farther = 1, 2, 3

    def attend(here, plane, h, ways):
        side = 0 if plane == here else 1
        keep = {here: 0, here - 1: below, here + 1: above, here - 2: farther}
        reach = WINDOW // rows
        for n in range(2):
            block = 2 * plane + n
            seen = [
                (back, keep[(block - back) // 2], (block - back) % 2)
                for back in range(reach + 1)
                if block >= back
            ]
            query = qr_buf[side, h, 0, n]
            parts = []
            for back, at, odd in seen:
                score = lax.dot_general(
                    query,
                    kv_buf[at, h, 0, odd],
                    (((1,), (1,)), ((), ())),
                    preferred_element_type=F32,
                )
                if back == 0:
                    score = jnp.where(col_at <= row_at, score, masked_score)
                if back == reach:
                    score = jnp.where(col_at > row_at, score, masked_score)
                parts.append(score)
            top = parts[0]
            for score in parts[1:]:
                top = jnp.maximum(top, score)
            top = jnp.max(top, axis=1, keepdims=True)
            parts = [jnp.exp((score - top) * (1.0 / math.sqrt(HEAD_DIM))) for score in parts]
            total = parts[0]
            for score in parts[1:]:
                total = total + score
            share = 1.0 / jnp.sum(total, axis=1, keepdims=True)
            attended = jnp.dot(
                jnp.concatenate([(score * share).astype(BF16) for score in parts], axis=1),
                jnp.concatenate([kv_buf[at, h, 1, odd] for _, at, odd in seen], axis=0),
                preferred_element_type=F32,
            )
            stream = (qr_buf[side, h, 1, n].astype(F32) + attended).astype(BF16)
            line[h][block] = stream.reshape(2, core_rows, HEAD_DIM)
            for way in ways:
                ref = line[h].at[block]
                push_plane(here, ref, ref, line_r.at[plane, h], device_at(way))

    def device_at(way):
        return dev_up if way > 0 else dev_dn

    def kv_sem(at, h):
        return kv_r.at[2 * heads if at == farther else (at - 1) * heads + h]

    def send_kv(here, way, src, dst, h):
        push_plane(here, kv_buf.at[src, h], kv_buf.at[dst, h], kv_sem(dst, h), device_at(way))

    def got_kv(at, h):
        got(kv_buf.at[at, h], kv_sem(at, h))

    def send_part(here, way, kind, h, block):
        at = below if way > 0 else above
        buf, to = (kv_buf, at) if kind == 0 else (qr_buf, 1)
        push_plane(
            here, buf.at[0, h, :, block], buf.at[to, h, :, block], kv_sem(at, h), device_at(way)
        )

    def send_home(here, way, h, kinds=(0,)):
        for kind in kinds:
            send_part(here, way, kind, h, y)

    def got_above(h):
        wait_for(size_of(kv_buf.at[0, h]) + size_of(qr_buf.at[0, h]), kv_sem(above, h))

    def send_line(here, way, plane, h):
        ref = line[h].at[pl.ds(2 * plane, 2)]
        push_plane(here, ref, ref, line_r.at[plane, h], device_at(way))

    def got_line(plane, h):
        got(line[h].at[pl.ds(2 * plane, 2)], line_r.at[plane, h])

    taken = [set() for _ in range(PLANES)]

    def made(here, plane, h, hold=False):
        taken[here].add((plane, h))
        ways = []
        if here < PLANES - 1 and not hold:
            ways.append(1)
        if here > 0:
            ways.append(-1)
        with mark(f"attend{plane}_{h}"):
            attend(here, plane, h, ways)

    def pass_on(here, way, plane, h):
        with mark(f"pass{plane}_{h}"):
            taken[here].add((plane, h))
            got_line(plane, h)
            send_line(here, way, plane, h)

    def steps_0(step):
        if step == 0:
            for kind, h in low_order:
                with mark(f"own{kind}_{h}"):
                    own(kind, h)
                if kind == 0:
                    send_part(0, 1, 0, h, yo)
                else:
                    made(0, 0, h)

    def steps_1(step):
        def first(h):
            with mark(f"own0_{h}"):
                own(0, h)
            send_part(1, 1, 0, h, yo)

        def home(h):
            with mark(f"own1_{h}"):
                own(1, h)
                got_kv(below, h)
            if h == STAY_HEAD:
                send_kv(1, 1, below, farther, h)
            made(1, 1, h)

        def lower(h):
            with mark(f"lower{h}"):
                got_above(h)
            made(1, 2, h)

        if step == 0:
            first(3)
            first(0)
            home(3)
            first(1)
            home(0)
            lower(0)
            pass_on(1, 1, 0, 3)
            pass_on(1, 1, 0, 0)
            first(2)
            home(1)
            lower(1)
            pass_on(1, -1, 3, 0)
        if step == 1:
            pass_on(1, 1, 0, 1)
            home(2)
            pass_on(1, 1, 0, 2)
            pass_on(1, -1, 3, 1)
        if step == 2:
            pass_on(1, -1, 2, 3)
            pass_on(1, -1, 3, 3)
        if step == 3:
            lower(2)
        if step == 4:
            pass_on(1, -1, 3, 2)

    def steps_2(step):
        def first(h):
            with mark(f"own0_{h}"):
                own(0, h)
            send_part(2, 1 if h == STAY_HEAD else -1, 0, h, yo)

        def second(h):
            with mark(f"own1_{h}"):
                own(1, h)
            if h != STAY_HEAD:
                send_part(2, -1, 1, h, yo)

        def lower(h, hold=False):
            with mark(f"lower{h}"):
                got_above(h)
                got_kv(below, h)
            made(2, 3, h, hold)

        if step == 0:
            first(0)
            second(0)
            first(3)
            first(1)
            with mark("below3"):
                got_kv(below, 3)
            send_kv(2, 1, below, farther, 3)
            second(1)
            send_home(2, -1, 2, (0, 1))
            lower(0)
            second(3)
            with mark("farther3"):
                got_kv(farther, 3)
            made(2, 2, 3)
            pass_on(2, 1, 1, 3)
            lower(1)
            pass_on(2, -1, 3, 3)
            first(2)
            second(2)
            pass_on(2, 1, 1, 0)
            pass_on(2, 1, 0, 3)
        if step == 1:
            pass_on(2, 1, 2, 0)
            pass_on(2, 1, 0, 0)
        if step == 2:
            lower(2, True)
            pass_on(2, 1, 1, 1)
            pass_on(2, 1, 2, 1)
        if step == 3:
            pass_on(2, 1, 0, 1)
            send_line(2, 1, 3, 2)
        if step == 4:
            pass_on(2, 1, 1, 2)
            pass_on(2, 1, 0, 2)
            pass_on(2, 1, 2, 2)

    def steps_3(step):
        if step == 0:
            for kind, h in high_order:
                with mark(f"own{kind}_{h}"):
                    own(kind, h)
                if h != STAY_HEAD:
                    send_part(3, -1, kind, h, yo)
                    if (kind, h) == (1, 1):
                        send_home(3, -1, 2, (0, 1))
                elif kind == 1:
                    with mark("below3"):
                        got_kv(below, 3)
                        got_kv(farther, 3)
                    made(3, 3, 3)

    def early(plane):
        if plane < 2:
            for h in (3, 0, 1, 2):
                send_home(plane, 1, h)
        else:
            for h in (0, 1):
                send_home(plane, -1, h, (0, 1))
            if plane == 2:
                send_home(plane, 1, STAY_HEAD)

    for plane in range(PLANES):
        pl.when(z == plane)(lambda: early(plane))

    def planes(step):
        for plane, steps in enumerate((steps_0, steps_1, steps_2, steps_3)):

            @pl.when(z == plane)
            def _():
                steps(step)

    def collect(order, pos):
        h = order[pos]
        for plane in range(PLANES):
            if orders[plane // 2][pos] != h:
                continue

            @pl.when(z == plane)
            def _():
                for other in range(PLANES):
                    if (other, h) not in taken[plane]:
                        taken[plane].add((other, h))
                        got_line(other, h)

    high = jnp.where(z < 2, 0, 1)
    orders = ((0, 1, 3, 2), (3, 0, 1, 2))
    heads_at = [low + high * (up - low) for low, up in zip(*orders)]
    ends = len(heads_at) - 1

    def groups_of(pos):
        return [pl.ds(g, 1) for g in range(GROUPS)] if pos == ends else [pl.ds(0, GROUPS)]

    def feature_at(pos, g):
        return pos + g.start

    def feature(n, py, pt, pos, g, device, src=None, lot=None):
        ref = x_buf.at[py, pt, heads_at[pos], g]
        src = ref if src is None else src
        push(src, ref, feat_r.at[lot_of[n], feature_at(pos, g)], device, lot)

    lot_of = (0, 0, 1, 2, 0, 0, 0)
    arrivals = (
        (y, tc),
        (y, tx),
        (y, txc),
        (yo, t),
        (yo, tc),
        (yo, tx),
        (yo, txc),
    )

    def take(n, pos, g):
        py, pt = arrivals[n]
        got(x_buf.at[py, pt, heads_at[pos], g], feat_r.at[lot_of[n], feature_at(pos, g)])

    def choose(h, g):
        for r in range(most):
            at = pl.ds(r * group_rows, group_rows)
            for ref, side in ((x_buf.at[y, t, h], c), (x_other.at[h], co)):
                block = line[h][chosen[r], side]
                for i in range(GROUPS):
                    if g.start <= i < g.start + g.size:
                        ref[i, at] = block[i * group_rows : (i + 1) * group_rows]

    def gather(pos):
        with mark(f"collect{pos}"):
            for order in orders:
                if order is orders[0] or order[pos] != orders[0][pos]:
                    collect(order, pos)

    def first_stage(pos, lots=None):
        for g in lots or groups_of(pos):
            if orders[0][pos] == orders[1][pos]:
                choose(orders[0][pos], g)
            else:
                pl.when(z < 2)(lambda: choose(orders[0][pos], g))
                pl.when(z >= 2)(lambda: choose(orders[1][pos], g))
            other = x_other.at[heads_at[pos], g]
            feature(3, y, t, pos, g, dev_y)
            feature(2, y, t, pos, g, dev_xc, other)
            feature(1, y, t, pos, g, dev_x)
            feature(4, y, t, pos, g, dev_yc, other)
            feature(0, y, t, pos, g, dev_c, other)

    def second_stage(pos, g, lot=None):
        take(3, pos, g)
        feature(5, yo, t, pos, g, dev_x, lot=lot)
        take(2, pos, g)
        feature(6, y, txc, pos, g, dev_y, lot=lot)

    def complete(pos, g):
        wait_for(5 * size_of(x_buf.at[y, t, 0, g]), feat_r.at[0, feature_at(pos, g)])

    def expert_parts(parts, pos, g):
        depth = g.size * most * group_rows
        left, right = [], []
        square = square_buf[g].reshape(depth, 1)
        for py, pt in parts:
            start = pl.multiple_of((2 * pt + py) * half + heads_at[pos] * HEAD_DIM, HEAD_DIM)
            value = x_buf[py, pt, heads_at[pos], g].reshape(depth, HEAD_DIM).astype(F32)
            square = square + jnp.sum(value * value, axis=1, keepdims=True)
            left.append((value * gain_ref[:, pl.ds(start, HEAD_DIM)]).astype(BF16))
            right.append(
                jnp.concatenate(
                    [w_buf[i, pl.ds(start, HEAD_DIM), :] for i in range(4)], axis=1
                )
            )
        square_buf[g] = square.reshape(g.size, most * group_rows, 1)
        acc_buf[g] += jnp.dot(
            jnp.concatenate(left, axis=1),
            jnp.concatenate(right, axis=0),
            preferred_element_type=F32,
        ).reshape(g.size, most * group_rows, 4 * units)

    every_part = [(y, t)] + list(arrivals)

    parts_last = groups_of(ends)
    both = groups_of(0)[0]
    planes(0)
    weights = (
        (gate_ref.at[0], w_buf.at[c]),
        (up_ref.at[0], w_buf.at[2 + c]),
        (down_ref.at[0], d_buf.at[c]),
    )
    for src, dst in weights:
        pltpu.make_async_copy(src, dst, weight_s.at[0]).start()
        push(src, dst, weight_r.at[0], dev_c)

    gather(0)
    first_stage(0)
    planes(1)

    @pl.when(z == 0)
    def _():
        with mark("second0"):
            second_stage(0, both, relay_lot)

    gather(1)
    first_stage(1)
    planes(2)

    @pl.when(z > 0)
    def _():
        with mark("second0"):
            second_stage(0, both, relay_lot)

    planes(3)
    gather(2)
    first_stage(2)
    with mark("second1"):
        second_stage(1, both)
    planes(4)
    gather(3)
    first_stage(3, parts_last[:1])
    with mark("second2"):
        second_stage(2, both)
    first_stage(3, parts_last[1:])
    acc_buf[...] = jnp.zeros_like(acc_buf)
    square_buf[...] = jnp.zeros_like(square_buf)
    with mark("weights"):
        every = w_buf.at[pl.ds(0, len(weights))]
        loaded(every, weight_s.at[0])
        got(every, weight_r.at[0])

    def whole(pos):
        with mark(f"feat{pos}"):
            complete(pos, both)
        with mark(f"expert{pos}"):
            expert_parts(every_part, pos, both)

    def relay_last(g):
        with mark(f"secondL{g.start}"):
            second_stage(ends, g)

    def hide(g):
        i = g.start
        with mark(f"farL{i}"):
            complete(ends, g)
        with mark(f"expertL{i}"):
            expert_parts(every_part, ends, g)
            scale = lax.rsqrt(square_buf[i] * (1.0 / features) + epsilon)
            gate_val = acc_buf[i, :, pl.ds(0, 2 * units)] * scale
            up_val = acc_buf[i, :, pl.ds(2 * units, 2 * units)] * scale
            hid_buf[x, i] = (gate_val / (1.0 + jnp.exp(-gate_val)) * up_val).astype(BF16)
        push(hid_buf.at[x, i], hid_buf.at[x, i], hid_r.at[i], dev_x)

    whole(0)
    relay_last(parts_last[0])
    whole(1)
    relay_last(parts_last[1])
    whole(2)
    for g in parts_last[2:]:
        relay_last(g)

    wide = half // SPAN
    pieces = [(s, j) for s in range(2) for j in range(wide)]

    def chunk(i, s, j):
        return (i * 2 + s) * wide + j

    pair = 2 * SPAN
    per = SPAN // HEAD_DIM

    def branch(i, s, which, j):
        hidden = jnp.concatenate([hid_buf[n, i] for n in range(2)], axis=1)
        at = pl.ds(pl.multiple_of(which * half + j * pair, pair), pair)
        weight = d_buf[c if s == 0 else co, :, at]
        value = jnp.dot(hidden, weight, preferred_element_type=F32).astype(BF16)
        return [(chunk(i, s, 2 * j + m), value[:, m * SPAN : (m + 1) * SPAN]) for m in range(2)]

    def down(i):
        with mark(f"hid{i}"):
            got(hid_buf.at[xo, i], hid_r.at[i])
        with mark(f"down{i}"):
            doubles = [(s, j) for s in range(2) for j in range(wide // 2)]
            for s, j in doubles:
                for k, value in branch(i, s, yo, j):
                    b_out[k] = value
                    push(b_out.at[k], b_in.at[k], branch_r.at[k], dev_y)
            for s, j in doubles:
                for m, (k, value) in enumerate(branch(i, s, y, j)):
                    stream = jnp.concatenate(
                        [
                            x_buf[y, t if s == 0 else tc, (2 * j + m) * per + q, i]
                            for q in range(per)
                        ],
                        axis=1,
                    )
                    part[k] = stream.astype(F32) + value.astype(F32)

    def blend(i, s, j):
        k = chunk(i, s, j)
        with mark(f"blend{k}"):
            got(b_in.at[k], branch_r.at[k])
            total = part[k] + b_in[k].astype(F32)
            mix[k][...] = total.astype(BF16).reshape(most, group_rows, SPAN)
        for plane, device in ((0, dev_up), (PLANES - 1, dev_dn)):

            @pl.when(z == plane)
            def _():
                push_plane(plane, mix[k], end_in[k], end_r.at[k], device)

    def pick(flag, a, b):
        mask = jnp.full(a.shape, flag.astype(jnp.int32), jnp.int32) > 0
        return jnp.where(mask, a.astype(F32), b.astype(F32)).astype(BF16)

    def give(here, way, k, d, other):
        out, arrived = (up_out, up_in) if way == 0 else (dn_out, dn_in)
        for n in range(2):
            b = 2 * d + n
            out[k, d, n] = pick(expert[b] == here, mix[k][slot[b]], other(b, n))
        push_plane(
            here,
            out.at[k, d],
            arrived.at[k, d],
            ret_r.at[d % 2, k],
            dev_up if way == 0 else dev_dn,
        )

    def turn_in(i, s, j):
        k = chunk(i, s, j)
        for here, way, targets in ((1, 0, (3, 2)), (2, 1, (0, 1))):

            @pl.when(z == here)
            def _():
                with mark(f"turn{k}"):
                    got(end_in[k], end_r.at[k])
                for d in targets:
                    give(here, way, k, d, lambda b, n: end_in[k][slot[b]])

    def carry(i, s, j):
        k = chunk(i, s, j)
        for here, way, d, out, arrived in ((2, 0, 3, up_out, up_in), (1, 1, 0, dn_out, dn_in)):

            @pl.when(z == here)
            def _():
                with mark(f"carry{k}"):
                    got(arrived.at[k, d], ret_r.at[d % 2, k])
                for n in range(2):
                    b = 2 * d + n
                    out[k, d, n] = pick(expert[b] == here, mix[k][slot[b]], arrived[k, d, n])
                    push_plane(
                        here,
                        out.at[k, d, n],
                        far_in.at[y, c, i, j],
                        far_r.at[i * wide + j],
                        (b, t if s == 0 else tc),
                    )

    def settle(i, s, j):
        k = chunk(i, s, j)
        for d in (0, PLANES - 1):

            @pl.when(z == d)
            def _():
                for n, which in enumerate((y, yo)):
                    at = slot[2 * d] + which * (slot[2 * d + 1] - slot[2 * d])
                    fin[k, n] = mix[k][at]
                there = home_in.at[y, c, i, j]
                sem = home_r.at[0]
                push_plane(d, fin.at[k, 1], there, sem, dev_y if s == 0 else dev_yc)
                if s == 0:
                    there[...] = fin[k, 0]
                else:
                    push_plane(d, fin.at[k, 0], there, sem, dev_c)

    def final(i, j):
        for d in (0, PLANES - 1):

            @pl.when(z == d)
            def _():
                with mark(f"final{i}_{j}"):
                    if i == 0 and j == 0:
                        wait_for(3 * GROUPS * wide * size_of(fin.at[0, 0]), home_r.at[0])
                    wait_for(4 * size_of(fin.at[0, 0]), far_r.at[i * wide + j])
                flag = jnp.where(y == 0, expert[2 * d], expert[2 * d + 1]) == d
                for half_at in range(2):
                    for side in range(2):
                        at = (half_at, side, i, j)
                        target(side, i, half_at, j)[...] = pick(flag, home_in[at], far_in[at])

    def target(side, i, which, j):
        return out_ref.at[
            pl.ds(pl.multiple_of(side * core_rows + i * group_rows, group_rows), group_rows),
            pl.ds(pl.multiple_of(which * half + j * SPAN, SPAN), SPAN),
        ]

    def arrive(i, s, j, d):
        k = chunk(i, s, j)

        @pl.when(z == d)
        def _():
            with mark(f"arrive{k}"):
                got((up_in if d > 1 else dn_in).at[k, d], ret_r.at[d % 2, k])
            for n in range(2):
                b = 2 * d + n
                lower = up_in[k, d, n] if d > 1 else end_in[k][slot[b]]
                higher = dn_in[k, d, n] if d == 1 else end_in[k][slot[b]]
                value = pick(expert[b] < d, lower, mix[k][slot[b]])
                fin[k, n] = pick(expert[b] > d, higher, value)
            mine = target(c, i, y, j)
            device = dev_y if s == 0 else dev_yc
            push_plane(d, fin.at[k, yo], mine, last_r.at[0], device)
            if s == 0:
                mine[...] = fin[k, y]
            else:
                push_plane(d, fin.at[k, y], mine, last_r.at[0], dev_c)

    def arrive_middle(i, s, j):
        arrive(i, s, j, 1)
        arrive(i, s, j, 2)

    every = [(i, s, j) for i in range(GROUPS) for s, j in pieces]
    for g in parts_last[:3]:
        hide(g)
    down(0)
    hide(parts_last[3])
    down(1)
    down(2)
    stages = (
        (0, blend),
        (4, turn_in),
        (9, carry),
        (12, arrive_middle),
        (16, settle),
    )
    for n in range(len(every) + stages[-1][0]):
        if n == len(pieces):
            down(3)
        for lag, stage in stages:
            if 0 <= n - lag < len(every):
                stage(*every[n - lag])
    with mark("lastwait"):
        for i in range(GROUPS):
            for j in range(wide):
                final(i, j)

        @pl.when((z > 0) & (z < PLANES - 1))
        def _():
            wait_for(3 * size_of(out_ref) // 4, last_r.at[0])

    def all_sent(sem, amount):
        if amount:
            ref = w_buf.at[0, pl.ds(0, amount // (2 * units))]
            remote(ref, ref, sem, hid_r.at[0], dev_y).wait_send()

    with mark("drain"):
        for lot, amount in enumerate(all_lots):
            all_sent(sent.at[lot], amount)
        all_sent(sent.at[relay_lot], 2 * size_of(x_buf.at[0, 0, 0]))
        for plane in range(PLANES):

            @pl.when(z == plane)
            def _():
                for lot, amount in enumerate(plane_lots[plane]):
                    all_sent(plane_sent.at[lot], amount)


def local(
    queries, keys, values, residual_in, norm_gain, routing, gate_weight, up_weight, down_weight
):
    seq_count = lax.axis_size("seq")
    tp_count = lax.axis_size("tp")
    rows, width = queries.shape
    units = gate_weight.shape[2]
    planes = seq_count // 2
    fits = (
        tp_count == 4
        and seq_count == 2 * PLANES
        and rows == BLOCK
        and WINDOW == 4 * rows
        and units == 128
        and width == 8 * HEAD_DIM
    )
    if not fits:
        return local_general(
            queries,
            keys,
            values,
            residual_in,
            norm_gain,
            routing,
            gate_weight,
            up_weight,
            down_weight,
        )
    half = width // 2
    heads = half // HEAD_DIM
    most = min(2 * seq_count // planes, seq_count - planes + 1)
    core_rows = rows // 2
    group_rows = core_rows // GROUPS
    wide = half // SPAN
    chunks = GROUPS * 2 * wide
    vmem = pl.BlockSpec(memory_space=pltpu.VMEM)
    anywhere = pl.BlockSpec(memory_space=pltpu.MemorySpace.HBM)
    dma = pltpu.SemaphoreType.DMA

    def room(*shape, kind=BF16):
        return pltpu.VMEM(shape, kind)

    scratch = (
        room(4, heads, 2, 2, rows, HEAD_DIM),
        room(2, heads, 2, 2, rows, HEAD_DIM),
        room(2, heads, 2, rows, HEAD_DIM),
        [room(2 * planes, 2, core_rows, HEAD_DIM) for _ in range(heads)],
        room(2, tp_count, heads, GROUPS, most * group_rows, HEAD_DIM),
        room(heads, GROUPS, most * group_rows, HEAD_DIM),
        room(4, gate_weight.shape[1], units),
        room(2, down_weight.shape[1], width),
        room(GROUPS, most * group_rows, 4 * units, kind=F32),
        room(GROUPS, most * group_rows, 1, kind=F32),
        room(2, GROUPS, most * group_rows, 2 * units),
        room(chunks, most * group_rows, SPAN),
        room(chunks, most * group_rows, SPAN),
        room(chunks, most * group_rows, SPAN, kind=F32),
        [room(most, group_rows, SPAN) for _ in range(chunks)],
        [room(most, group_rows, SPAN) for _ in range(chunks)],
        room(chunks, planes, 2, group_rows, SPAN),
        room(chunks, planes, 2, group_rows, SPAN),
        room(chunks, planes, 2, group_rows, SPAN),
        room(chunks, planes, 2, group_rows, SPAN),
        room(chunks, 2, group_rows, SPAN),
        room(2, 2, GROUPS, wide, group_rows, SPAN),
        room(2, 2, GROUPS, wide, group_rows, SPAN),
        dma((1,)),
        dma((1,)),
        dma((1,)),
        dma((2, heads)),
        dma((2 * heads + 1,)),
        dma((planes, heads)),
        dma((3, heads + GROUPS - 1)),
        dma((1,)),
        dma((GROUPS,)),
        dma((chunks,)),
        dma((chunks,)),
        dma((2, chunks)),
        dma((1,)),
        dma((1,)),
        dma((GROUPS * wide,)),
        dma((8,)),
        dma((4,)),
    )
    flat, tree = jax.tree.flatten(scratch, is_leaf=lambda leaf: not isinstance(leaf, (list, tuple)))

    def kernel(*refs):
        layer_kernel(most, refs[:9], refs[9], jax.tree.unflatten(tree, refs[10:]))

    return pl.pallas_call(
        kernel,
        name="layer",
        out_shape=pltpu.VMEM((rows, width), BF16),
        in_specs=[pl.BlockSpec(memory_space=pltpu.SMEM)]
        + [anywhere] * 4
        + [vmem]
        + [anywhere] * 3,
        out_specs=vmem,
        scratch_shapes=flat,
        compiler_params=pltpu.CompilerParams(
            collective_id=0, has_side_effects=True, vmem_limit_bytes=67043328 - 2 * rows * width
        ),
    )(
        routing.reshape(-1),
        queries,
        keys,
        values,
        residual_in,
        norm_gain.reshape(1, -1),
        gate_weight,
        up_weight,
        down_weight,
    )


def solution(mesh):
    in_specs = (
        P("seq", "tp"),
        P("seq", "tp"),
        P("seq", "tp"),
        P("seq", "tp"),
        P(),
        P(),
        P("seq", None, "tp"),
        P("seq", None, "tp"),
        P("seq", None, "tp"),
    )
    out_specs = P("seq", "tp")
    return jax.shard_map(local, mesh=mesh, in_specs=in_specs, out_specs=out_specs, check_vma=False)
```

```python
import contextlib
import math

import jax
import jax.numpy as jnp
from jax import lax
from jax.experimental import pallas as pl
from jax.experimental.pallas import tpu as pltpu
from jax.sharding import PartitionSpec as P

HEAD_DIM = 128
BLOCK = 128
WINDOW = 512


epsilon = 1e-05
masked_score = -1e30


def shifted(block, axis, distance):
    devices = range(lax.axis_size(axis))
    route = [(i - distance, i) for i in devices if i - distance in devices]
    return lax.ppermute(block, axis, route)


def local_general(
    queries, keys, values, residual_in, norm_gain, routing, gate_weight, up_weight, down_weight
):
    seq_count = lax.axis_size("seq")
    seq_place = lax.axis_index("seq")
    tok_rows = queries.shape[0]
    feat_width = queries.shape[1]
    head_count = feat_width // HEAD_DIM
    prior_count = (WINDOW - 1) // tok_rows + 1
    earlier_keys = []
    earlier_values = []
    for distance in range(1, prior_count + 1):
        moved_keys, moved_values = shifted((keys, values), "seq", distance)
        earlier_keys.insert(0, moved_keys)
        earlier_values.insert(0, moved_values)
    key_all = jnp.concatenate(earlier_keys + [keys], axis=0).reshape(-1, head_count, HEAD_DIM)
    value_all = jnp.concatenate(earlier_values + [values], axis=0).reshape(-1, head_count, HEAD_DIM)
    query_heads = queries.reshape(tok_rows, head_count, HEAD_DIM)
    query_pos = seq_place * tok_rows + jnp.arange(tok_rows, dtype=jnp.int32)
    key_pos = (
        seq_place * tok_rows
        - prior_count * tok_rows
        + jnp.arange((prior_count + 1) * tok_rows, dtype=jnp.int32)
    )
    visible = (
        (key_pos[None, :] >= 0)
        & (key_pos[None, :] <= query_pos[:, None])
        & (key_pos[None, :] > query_pos[:, None] - WINDOW)
    )
    scores = jnp.einsum(
        "qhd,khd->hqk", query_heads, key_all, preferred_element_type=jnp.float32
    ) * (1.0 / math.sqrt(HEAD_DIM))
    scores = jnp.where(visible[None], scores, masked_score)
    top_score = jnp.max(scores, axis=2, keepdims=True)
    expo = jnp.exp(scores - top_score)
    weights_soft = (expo / jnp.sum(expo, axis=2, keepdims=True)).astype(jnp.bfloat16)
    attended = jnp.einsum(
        "hqk,khd->qhd", weights_soft, value_all, preferred_element_type=jnp.float32
    ).reshape(tok_rows, feat_width)
    stream = (residual_in.astype(jnp.float32) + attended).astype(jnp.bfloat16)
    send_width = stream.shape[1]
    blocks_dev = tok_rows // BLOCK
    piece_rows = BLOCK // seq_count
    spread_in = stream.reshape(blocks_dev, seq_count, piece_rows, send_width)
    spread_out = lax.all_to_all(spread_in, "seq", split_axis=1, concat_axis=0, tiled=True)
    block_count = blocks_dev * seq_count
    spread_rows = spread_out.reshape(block_count, piece_rows, send_width)
    expert_ids = routing[:, 0]
    expert_count = seq_count // 2
    most_blocks = min(2 * block_count // expert_count, block_count - expert_count + 1)
    order_index = jnp.arange(block_count, dtype=jnp.int32)
    same_expert = expert_ids[None, :] == expert_ids[:, None]
    rank_of = jnp.sum(same_expert & (order_index[None, :] < order_index[:, None]), axis=1)
    expert_range = jnp.arange(expert_count, dtype=jnp.int32)
    slot_range = jnp.arange(most_blocks, dtype=jnp.int32)
    selector = (
        (expert_ids[None, None, :] == expert_range[:, None, None])
        & (rank_of[None, None, :] == slot_range[None, :, None])
    ).astype(jnp.bfloat16)
    picked = jnp.einsum(
        "erb,bqf->erqf", selector, spread_rows, preferred_element_type=jnp.float32
    ).astype(jnp.bfloat16)
    outgoing = jnp.broadcast_to(
        picked[:, None], (expert_count, 2, most_blocks, piece_rows, send_width)
    )
    outgoing = outgoing.reshape(seq_count, most_blocks, piece_rows, send_width)
    features_full = lax.all_gather(
        lax.all_to_all(outgoing, "seq", split_axis=0, concat_axis=0, tiled=True),
        "tp",
        axis=3,
        tiled=True,
    )
    source_count = features_full.shape[0]
    slot_count = features_full.shape[1]
    stream_f32 = features_full.astype(jnp.float32)
    mean_square = jnp.mean(stream_f32 * stream_f32, axis=3, keepdims=True)
    normed = (stream_f32 * lax.rsqrt(mean_square + epsilon) * norm_gain).astype(jnp.bfloat16)
    normed = normed.reshape(-1, normed.shape[3])
    gate_val = jnp.dot(normed, gate_weight[0], preferred_element_type=jnp.float32)
    up_val = jnp.dot(normed, up_weight[0], preferred_element_type=jnp.float32)
    hidden = (jax.nn.silu(gate_val) * up_val).astype(jnp.bfloat16)
    hidden_half = lax.all_gather(hidden, "tp", axis=1, tiled=True)
    partial_value = jnp.dot(hidden_half, down_weight[0], preferred_element_type=jnp.float32).astype(
        jnp.bfloat16
    )
    partial_value = partial_value.reshape(source_count, slot_count, piece_rows, feat_width)
    returned = lax.all_to_all(partial_value, "seq", split_axis=0, concat_axis=0, tiled=True)
    returned = returned.reshape(expert_count, 2, most_blocks, piece_rows * feat_width)
    combined = jnp.einsum("erb,epry->pby", selector, returned, preferred_element_type=jnp.float32)
    residual_rows = spread_rows
    residual_rows = residual_rows.reshape(block_count, piece_rows * feat_width).astype(jnp.float32)
    finished = (residual_rows + combined[0] + combined[1]).astype(jnp.bfloat16)
    finished = finished.reshape(seq_count, blocks_dev, piece_rows, feat_width)
    restored = lax.all_to_all(finished, "seq", split_axis=0, concat_axis=2, tiled=True)
    return restored.reshape(tok_rows, feat_width)


BF16 = jnp.bfloat16
F32 = jnp.float32
PLANES = 4
GROUPS = 4
SPAN = 2 * HEAD_DIM
STAY_HEAD = 3


def mark(name):
    return contextlib.nullcontext()


def remote(src, dst, send_sem, recv_sem, device):
    return pltpu.make_async_remote_copy(
        src_ref=src,
        dst_ref=dst,
        send_sem=send_sem,
        recv_sem=recv_sem,
        device_id=device,
        device_id_type=pl.DeviceIdType.MESH,
    )


def size_of(ref):
    return math.prod(ref.shape) * ref.dtype.itemsize


def layer_kernel(most, arguments, out_ref, scratch):
    routing_ref, q_ref, k_ref, v_ref, r_ref, gain_ref, gate_ref, up_ref, down_ref = arguments
    (
        kv_buf,
        qr_buf,
        away,
        line,
        x_buf,
        x_other,
        w_buf,
        d_buf,
        acc_buf,
        square_buf,
        hid_buf,
        b_out,
        b_in,
        part,
        mix,
        end_in,
        up_out,
        up_in,
        dn_out,
        dn_in,
        fin,
        home_in,
        far_in,
        own_s,
        away_s,
        weight_s,
        swap_r,
        kv_r,
        line_r,
        feat_r,
        weight_r,
        hid_r,
        branch_r,
        end_r,
        ret_r,
        last_r,
        home_r,
        far_r,
        sent,
        plane_sent,
    ) = scratch
    rows = q_ref.shape[0]
    half = q_ref.shape[1] // 2
    heads = half // HEAD_DIM
    units = gate_ref.shape[2]
    features = gain_ref.shape[1]
    core_rows = rows // 2
    group_rows = core_rows // GROUPS
    me = lax.axis_index("seq")
    t = lax.axis_index("tp")
    z = me // 2
    y = me % 2
    x = t // 2
    c = t % 2
    yo, xo, co = 1 - y, 1 - x, 1 - c
    tc = 2 * x + co
    tx = 2 * xo + c
    txc = 2 * xo + co
    mate = 2 * z + yo
    dev_y, dev_yc = (mate, t), (mate, tc)
    dev_x, dev_xc = (me, tx), (me, txc)
    dev_c = (me, tc)
    dev_up, dev_dn = (me + 2, t), (me - 2, t)
    has_up, has_dn = z < PLANES - 1, z > 0

    limit = size_of(w_buf)
    all_lots = [0]
    plane_lots = [[0] for _ in range(PLANES)]

    def lot_for(lots, ref):
        if lots[-1] + size_of(ref) > limit:
            lots.append(0)
        lots[-1] += size_of(ref)
        return len(lots) - 1

    relay_lot = sent.shape[0] - 1

    def push(src, dst, recv_sem, device, lot=None):
        lot = lot_for(all_lots, src) if lot is None else lot
        remote(src, dst, sent.at[lot], recv_sem, device).start()

    def push_plane(plane, src, dst, recv_sem, device):
        lot = lot_for(plane_lots[plane], src)
        remote(src, dst, plane_sent.at[lot], recv_sem, device).start()

    def got(ref, recv_sem):
        remote(ref, ref, sent.at[0], recv_sem, dev_y).wait_recv()

    def wait_for(amount, recv_sem):
        got(w_buf.at[0, pl.ds(0, amount // (2 * units))], recv_sem)

    def loaded(ref, sem):
        pltpu.make_async_copy(ref, ref, sem).wait()

    barrier = pltpu.get_barrier_semaphore()

    def greet(device):
        pl.semaphore_signal(
            barrier, inc=1, device_id=device, device_id_type=pl.DeviceIdType.MESH
        )

    for device in (dev_y, dev_yc, dev_c, dev_x, dev_xc):
        greet(device)
    pl.when(has_up)(lambda: greet(dev_up))
    pl.when(has_dn)(lambda: greet(dev_dn))

    def cols(which, h):
        return pl.ds(pl.multiple_of(which * half + h * HEAD_DIM, HEAD_DIM), HEAD_DIM)

    sources = ((k_ref, v_ref), (q_ref, r_ref))

    def place(kind, h, n, block):
        buf = kv_buf if kind == 0 else qr_buf
        return buf.at[0, h, n, block]

    def load_own(kind, h):
        for n, ref in enumerate(sources[kind]):
            pltpu.make_async_copy(
                ref.at[:, cols(y, h)], place(kind, h, n, y), own_s.at[0]
            ).start()

    def load_away(kind, h):
        for n, ref in enumerate(sources[kind]):
            pltpu.make_async_copy(
                ref.at[:, cols(yo, h)], away.at[kind, h, n], away_s.at[0]
            ).start()

    def swap(kind, h):
        buf = kv_buf if kind == 0 else qr_buf
        push(away.at[kind, h], buf.at[0, h, :, y], swap_r.at[kind, h], dev_y)

    def own(kind, h):
        buf = kv_buf if kind == 0 else qr_buf
        got(buf.at[0, h, :, yo], swap_r.at[kind, h])

    for kind in range(2):
        for h in range(heads):
            load_away(kind, h)
    for kind in range(2):
        for h in range(heads):
            load_own(kind, h)

    expert = [routing_ref[b] for b in range(2 * PLANES)]
    slot = []
    for b in range(2 * PLANES):
        count = jnp.int32(0)
        for j in range(b):
            count = count + jnp.where(expert[j] == expert[b], 1, 0)
        slot.append(jnp.minimum(count, most - 1))
    chosen = []
    for r in range(most):
        index = jnp.int32(0)
        for b in range(2 * PLANES):
            index = jnp.where((expert[b] == z) & (slot[b] == r), b, index)
        chosen.append(index)

    with mark("barwait"):
        pl.semaphore_wait(barrier, 5 + jnp.where(has_up, 1, 0) + jnp.where(has_dn, 1, 0))

    low_order = ((0, 3), (0, 0), (1, 3), (1, 0), (0, 1), (1, 1), (0, 2), (1, 2))
    high_order = ((0, 0), (1, 0), (0, 3), (0, 1), (1, 1), (1, 3), (0, 2), (1, 2))

    with mark("away"):
        loaded(away, away_s.at[0])

    @pl.when(z < 2)
    def _():
        for kind, h in low_order:
            swap(kind, h)

    all_lots[:] = [0]

    @pl.when(z >= 2)
    def _():
        for kind, h in high_order:
            swap(kind, h)

    with mark("ownwait"):
        loaded(away, own_s.at[0])
    row_at = lax.broadcasted_iota(jnp.int32, (rows, rows), 0)
    col_at = lax.broadcasted_iota(jnp.int32, (rows, rows), 1)
    below, above, farther = 1, 2, 3

    def attend(here, plane, h, ways):
        side = 0 if plane == here else 1
        keep = {here: 0, here - 1: below, here + 1: above, here - 2: farther}
        reach = WINDOW // rows
        for n in range(2):
            block = 2 * plane + n
            seen = [
                (back, keep[(block - back) // 2], (block - back) % 2)
                for back in range(reach + 1)
                if block >= back
            ]
            query = qr_buf[side, h, 0, n]
            parts = []
            for back, at, odd in seen:
                score = lax.dot_general(
                    query,
                    kv_buf[at, h, 0, odd],
                    (((1,), (1,)), ((), ())),
                    preferred_element_type=F32,
                )
                if back == 0:
                    score = jnp.where(col_at <= row_at, score, masked_score)
                if back == reach:
                    score = jnp.where(col_at > row_at, score, masked_score)
                parts.append(score)
            top = parts[0]
            for score in parts[1:]:
                top = jnp.maximum(top, score)
            top = jnp.max(top, axis=1, keepdims=True)
            parts = [jnp.exp((score - top) * (1.0 / math.sqrt(HEAD_DIM))) for score in parts]
            total = parts[0]
            for score in parts[1:]:
                total = total + score
            share = 1.0 / jnp.sum(total, axis=1, keepdims=True)
            attended = jnp.dot(
                jnp.concatenate([(score * share).astype(BF16) for score in parts], axis=1),
                jnp.concatenate([kv_buf[at, h, 1, odd] for _, at, odd in seen], axis=0),
                preferred_element_type=F32,
            )
            stream = (qr_buf[side, h, 1, n].astype(F32) + attended).astype(BF16)
            line[h][block] = stream.reshape(2, core_rows, HEAD_DIM)
            for way in ways:
                ref = line[h].at[block]
                push_plane(here, ref, ref, line_r.at[plane, h], device_at(way))

    def device_at(way):
        return dev_up if way > 0 else dev_dn

    def kv_sem(at, h):
        return kv_r.at[2 * heads if at == farther else (at - 1) * heads + h]

    def send_kv(here, way, src, dst, h):
        push_plane(here, kv_buf.at[src, h], kv_buf.at[dst, h], kv_sem(dst, h), device_at(way))

    def got_kv(at, h):
        got(kv_buf.at[at, h], kv_sem(at, h))

    def send_part(here, way, kind, h, block):
        at = below if way > 0 else above
        buf, to = (kv_buf, at) if kind == 0 else (qr_buf, 1)
        push_plane(
            here, buf.at[0, h, :, block], buf.at[to, h, :, block], kv_sem(at, h), device_at(way)
        )

    def send_home(here, way, h, kinds=(0,)):
        for kind in kinds:
            send_part(here, way, kind, h, y)

    def got_above(h):
        wait_for(size_of(kv_buf.at[0, h]) + size_of(qr_buf.at[0, h]), kv_sem(above, h))

    def send_line(here, way, plane, h):
        ref = line[h].at[pl.ds(2 * plane, 2)]
        push_plane(here, ref, ref, line_r.at[plane, h], device_at(way))

    def got_line(plane, h):
        got(line[h].at[pl.ds(2 * plane, 2)], line_r.at[plane, h])

    taken = [set() for _ in range(PLANES)]

    def made(here, plane, h, hold=False):
        taken[here].add((plane, h))
        ways = []
        if here < PLANES - 1 and not hold:
            ways.append(1)
        if here > 0:
            ways.append(-1)
        with mark(f"attend{plane}_{h}"):
            attend(here, plane, h, ways)

    def pass_on(here, way, plane, h):
        with mark(f"pass{plane}_{h}"):
            taken[here].add((plane, h))
            got_line(plane, h)
            send_line(here, way, plane, h)

    def steps_0(step):
        if step == 0:
            for kind, h in low_order:
                with mark(f"own{kind}_{h}"):
                    own(kind, h)
                if kind == 0:
                    send_part(0, 1, 0, h, yo)
                else:
                    made(0, 0, h)

    def steps_1(step):
        def first(h):
            with mark(f"own0_{h}"):
                own(0, h)
            send_part(1, 1, 0, h, yo)

        def home(h):
            with mark(f"own1_{h}"):
                own(1, h)
                got_kv(below, h)
            if h == STAY_HEAD:
                send_kv(1, 1, below, farther, h)
            made(1, 1, h)

        def lower(h):
            with mark(f"lower{h}"):
                got_above(h)
            made(1, 2, h)

        if step == 0:
            first(3)
            first(0)
            home(3)
            first(1)
            home(0)
            lower(0)
            pass_on(1, 1, 0, 3)
            pass_on(1, 1, 0, 0)
            first(2)
            home(1)
            lower(1)
            pass_on(1, -1, 3, 0)
        if step == 1:
            pass_on(1, 1, 0, 1)
            home(2)
            pass_on(1, 1, 0, 2)
            pass_on(1, -1, 3, 1)
        if step == 2:
            pass_on(1, -1, 2, 3)
            pass_on(1, -1, 3, 3)
        if step == 3:
            lower(2)
        if step == 4:
            pass_on(1, -1, 3, 2)

    def steps_2(step):
        def first(h):
            with mark(f"own0_{h}"):
                own(0, h)
            send_part(2, 1 if h == STAY_HEAD else -1, 0, h, yo)

        def second(h):
            with mark(f"own1_{h}"):
                own(1, h)
            if h != STAY_HEAD:
                send_part(2, -1, 1, h, yo)

        def lower(h, hold=False):
            with mark(f"lower{h}"):
                got_above(h)
                got_kv(below, h)
            made(2, 3, h, hold)

        if step == 0:
            first(0)
            second(0)
            first(3)
            first(1)
            with mark("below3"):
                got_kv(below, 3)
            send_kv(2, 1, below, farther, 3)
            second(1)
            send_home(2, -1, 2, (0, 1))
            lower(0)
            second(3)
            with mark("farther3"):
                got_kv(farther, 3)
            made(2, 2, 3)
            pass_on(2, 1, 1, 3)
            lower(1)
            pass_on(2, -1, 3, 3)
            first(2)
            second(2)
            pass_on(2, 1, 1, 0)
            pass_on(2, 1, 0, 3)
        if step == 1:
            pass_on(2, 1, 2, 0)
            pass_on(2, 1, 0, 0)
        if step == 2:
            lower(2, True)
            pass_on(2, 1, 1, 1)
            pass_on(2, 1, 2, 1)
        if step == 3:
            pass_on(2, 1, 0, 1)
            send_line(2, 1, 3, 2)
        if step == 4:
            pass_on(2, 1, 1, 2)
            pass_on(2, 1, 0, 2)
            pass_on(2, 1, 2, 2)

    def steps_3(step):
        if step == 0:
            for kind, h in high_order:
                with mark(f"own{kind}_{h}"):
                    own(kind, h)
                if h != STAY_HEAD:
                    send_part(3, -1, kind, h, yo)
                    if (kind, h) == (1, 1):
                        send_home(3, -1, 2, (0, 1))
                elif kind == 1:
                    with mark("below3"):
                        got_kv(below, 3)
                        got_kv(farther, 3)
                    made(3, 3, 3)

    def early(plane):
        if plane < 2:
            for h in (3, 0, 1, 2):
                send_home(plane, 1, h)
        else:
            for h in (0, 1):
                send_home(plane, -1, h, (0, 1))
            if plane == 2:
                send_home(plane, 1, STAY_HEAD)

    for plane in range(PLANES):
        pl.when(z == plane)(lambda: early(plane))

    def planes(step):
        for plane, steps in enumerate((steps_0, steps_1, steps_2, steps_3)):

            @pl.when(z == plane)
            def _():
                steps(step)

    def collect(order, pos):
        h = order[pos]
        for plane in range(PLANES):
            if orders[plane // 2][pos] != h:
                continue

            @pl.when(z == plane)
            def _():
                for other in range(PLANES):
                    if (other, h) not in taken[plane]:
                        taken[plane].add((other, h))
                        got_line(other, h)

    high = jnp.where(z < 2, 0, 1)
    orders = ((0, 1, 3, 2), (3, 0, 1, 2))
    heads_at = [low + high * (up - low) for low, up in zip(*orders)]
    ends = len(heads_at) - 1

    def groups_of(pos):
        return [pl.ds(g, 1) for g in range(GROUPS)] if pos == ends else [pl.ds(0, GROUPS)]

    def feature_at(pos, g):
        return pos + g.start

    def feature(n, py, pt, pos, g, device, src=None, lot=None):
        ref = x_buf.at[py, pt, heads_at[pos], g]
        src = ref if src is None else src
        push(src, ref, feat_r.at[lot_of[n], feature_at(pos, g)], device, lot)

    lot_of = (0, 0, 1, 2, 0, 0, 0)
    arrivals = (
        (y, tc),
        (y, tx),
        (y, txc),
        (yo, t),
        (yo, tc),
        (yo, tx),
        (yo, txc),
    )

    def take(n, pos, g):
        py, pt = arrivals[n]
        got(x_buf.at[py, pt, heads_at[pos], g], feat_r.at[lot_of[n], feature_at(pos, g)])

    def choose(h, g):
        for r in range(most):
            at = pl.ds(r * group_rows, group_rows)
            for ref, side in ((x_buf.at[y, t, h], c), (x_other.at[h], co)):
                block = line[h][chosen[r], side]
                for i in range(GROUPS):
                    if g.start <= i < g.start + g.size:
                        ref[i, at] = block[i * group_rows : (i + 1) * group_rows]

    def gather(pos):
        with mark(f"collect{pos}"):
            for order in orders:
                if order is orders[0] or order[pos] != orders[0][pos]:
                    collect(order, pos)

    def first_stage(pos, lots=None):
        for g in lots or groups_of(pos):
            if orders[0][pos] == orders[1][pos]:
                choose(orders[0][pos], g)
            else:
                pl.when(z < 2)(lambda: choose(orders[0][pos], g))
                pl.when(z >= 2)(lambda: choose(orders[1][pos], g))
            other = x_other.at[heads_at[pos], g]
            feature(3, y, t, pos, g, dev_y)
            feature(2, y, t, pos, g, dev_xc, other)
            feature(1, y, t, pos, g, dev_x)
            feature(4, y, t, pos, g, dev_yc, other)
            feature(0, y, t, pos, g, dev_c, other)

    def second_stage(pos, g, lot=None):
        take(3, pos, g)
        feature(5, yo, t, pos, g, dev_x, lot=lot)
        take(2, pos, g)
        feature(6, y, txc, pos, g, dev_y, lot=lot)

    def complete(pos, g):
        wait_for(5 * size_of(x_buf.at[y, t, 0, g]), feat_r.at[0, feature_at(pos, g)])

    def expert_parts(parts, pos, g):
        depth = g.size * most * group_rows
        left, right = [], []
        square = square_buf[g].reshape(depth, 1)
        for py, pt in parts:
            start = pl.multiple_of((2 * pt + py) * half + heads_at[pos] * HEAD_DIM, HEAD_DIM)
            value = x_buf[py, pt, heads_at[pos], g].reshape(depth, HEAD_DIM).astype(F32)
            square = square + jnp.sum(value * value, axis=1, keepdims=True)
            left.append((value * gain_ref[:, pl.ds(start, HEAD_DIM)]).astype(BF16))
            right.append(
                jnp.concatenate(
                    [w_buf[i, pl.ds(start, HEAD_DIM), :] for i in range(4)], axis=1
                )
            )
        square_buf[g] = square.reshape(g.size, most * group_rows, 1)
        acc_buf[g] += jnp.dot(
            jnp.concatenate(left, axis=1),
            jnp.concatenate(right, axis=0),
            preferred_element_type=F32,
        ).reshape(g.size, most * group_rows, 4 * units)

    every_part = [(y, t)] + list(arrivals)

    parts_last = groups_of(ends)
    both = groups_of(0)[0]
    planes(0)
    weights = (
        (gate_ref.at[0], w_buf.at[c]),
        (up_ref.at[0], w_buf.at[2 + c]),
        (down_ref.at[0], d_buf.at[c]),
    )
    for src, dst in weights:
        pltpu.make_async_copy(src, dst, weight_s.at[0]).start()
        push(src, dst, weight_r.at[0], dev_c)

    gather(0)
    first_stage(0)
    planes(1)

    @pl.when(z == 0)
    def _():
        with mark("second0"):
            second_stage(0, both, relay_lot)

    gather(1)
    first_stage(1)
    planes(2)

    @pl.when(z > 0)
    def _():
        with mark("second0"):
            second_stage(0, both, relay_lot)

    planes(3)
    gather(2)
    first_stage(2)
    with mark("second1"):
        second_stage(1, both)
    planes(4)
    gather(3)
    first_stage(3, parts_last[:1])
    with mark("second2"):
        second_stage(2, both)
    first_stage(3, parts_last[1:])
    acc_buf[...] = jnp.zeros_like(acc_buf)
    square_buf[...] = jnp.zeros_like(square_buf)
    with mark("weights"):
        every = w_buf.at[pl.ds(0, len(weights))]
        loaded(every, weight_s.at[0])
        got(every, weight_r.at[0])

    def whole(pos):
        with mark(f"feat{pos}"):
            complete(pos, both)
        with mark(f"expert{pos}"):
            expert_parts(every_part, pos, both)

    def relay_last(g):
        with mark(f"secondL{g.start}"):
            second_stage(ends, g)

    def hide(g):
        i = g.start
        with mark(f"farL{i}"):
            complete(ends, g)
        with mark(f"expertL{i}"):
            expert_parts(every_part, ends, g)
            scale = lax.rsqrt(square_buf[i] * (1.0 / features) + epsilon)
            gate_val = acc_buf[i, :, pl.ds(0, 2 * units)] * scale
            up_val = acc_buf[i, :, pl.ds(2 * units, 2 * units)] * scale
            hid_buf[x, i] = (gate_val / (1.0 + jnp.exp(-gate_val)) * up_val).astype(BF16)
        push(hid_buf.at[x, i], hid_buf.at[x, i], hid_r.at[i], dev_x)

    whole(0)
    relay_last(parts_last[0])
    whole(1)
    relay_last(parts_last[1])
    whole(2)
    for g in parts_last[2:]:
        relay_last(g)

    wide = half // SPAN
    pieces = [(s, j) for s in range(2) for j in range(wide)]

    def chunk(i, s, j):
        return (i * 2 + s) * wide + j

    pair = 2 * SPAN
    per = SPAN // HEAD_DIM

    def branch(i, s, which, j):
        hidden = jnp.concatenate([hid_buf[n, i] for n in range(2)], axis=1)
        at = pl.ds(pl.multiple_of(which * half + j * pair, pair), pair)
        weight = d_buf[c if s == 0 else co, :, at]
        value = jnp.dot(hidden, weight, preferred_element_type=F32).astype(BF16)
        return [(chunk(i, s, 2 * j + m), value[:, m * SPAN : (m + 1) * SPAN]) for m in range(2)]

    def down(i):
        with mark(f"hid{i}"):
            got(hid_buf.at[xo, i], hid_r.at[i])
        with mark(f"down{i}"):
            doubles = [(s, j) for s in range(2) for j in range(wide // 2)]
            for s, j in doubles:
                for k, value in branch(i, s, yo, j):
                    b_out[k] = value
                    push(b_out.at[k], b_in.at[k], branch_r.at[k], dev_y)
            for s, j in doubles:
                for m, (k, value) in enumerate(branch(i, s, y, j)):
                    stream = jnp.concatenate(
                        [
                            x_buf[y, t if s == 0 else tc, (2 * j + m) * per + q, i]
                            for q in range(per)
                        ],
                        axis=1,
                    )
                    part[k] = stream.astype(F32) + value.astype(F32)

    def blend(i, s, j):
        k = chunk(i, s, j)
        with mark(f"blend{k}"):
            got(b_in.at[k], branch_r.at[k])
            total = part[k] + b_in[k].astype(F32)
            mix[k][...] = total.astype(BF16).reshape(most, group_rows, SPAN)
        for plane, device in ((0, dev_up), (PLANES - 1, dev_dn)):

            @pl.when(z == plane)
            def _():
                push_plane(plane, mix[k], end_in[k], end_r.at[k], device)

    def pick(flag, a, b):
        mask = jnp.full(a.shape, flag.astype(jnp.int32), jnp.int32) > 0
        return jnp.where(mask, a.astype(F32), b.astype(F32)).astype(BF16)

    def give(here, way, k, d, other):
        out, arrived = (up_out, up_in) if way == 0 else (dn_out, dn_in)
        for n in range(2):
            b = 2 * d + n
            out[k, d, n] = pick(expert[b] == here, mix[k][slot[b]], other(b, n))
        push_plane(
            here,
            out.at[k, d],
            arrived.at[k, d],
            ret_r.at[d % 2, k],
            dev_up if way == 0 else dev_dn,
        )

    def turn_in(i, s, j):
        k = chunk(i, s, j)
        for here, way, targets in ((1, 0, (3, 2)), (2, 1, (0, 1))):

            @pl.when(z == here)
            def _():
                with mark(f"turn{k}"):
                    got(end_in[k], end_r.at[k])
                for d in targets:
                    give(here, way, k, d, lambda b, n: end_in[k][slot[b]])

    def carry(i, s, j):
        k = chunk(i, s, j)
        for here, way, d, out, arrived in ((2, 0, 3, up_out, up_in), (1, 1, 0, dn_out, dn_in)):

            @pl.when(z == here)
            def _():
                with mark(f"carry{k}"):
                    got(arrived.at[k, d], ret_r.at[d % 2, k])
                for n in range(2):
                    b = 2 * d + n
                    out[k, d, n] = pick(expert[b] == here, mix[k][slot[b]], arrived[k, d, n])
                    push_plane(
                        here,
                        out.at[k, d, n],
                        far_in.at[y, c, i, j],
                        far_r.at[i * wide + j],
                        (b, t if s == 0 else tc),
                    )

    def settle(i, s, j):
        k = chunk(i, s, j)
        for d in (0, PLANES - 1):

            @pl.when(z == d)
            def _():
                for n, which in enumerate((y, yo)):
                    at = slot[2 * d] + which * (slot[2 * d + 1] - slot[2 * d])
                    fin[k, n] = mix[k][at]
                there = home_in.at[y, c, i, j]
                sem = home_r.at[0]
                push_plane(d, fin.at[k, 1], there, sem, dev_y if s == 0 else dev_yc)
                if s == 0:
                    there[...] = fin[k, 0]
                else:
                    push_plane(d, fin.at[k, 0], there, sem, dev_c)

    def final(i, j):
        for d in (0, PLANES - 1):

            @pl.when(z == d)
            def _():
                with mark(f"final{i}_{j}"):
                    if i == 0 and j == 0:
                        wait_for(3 * GROUPS * wide * size_of(fin.at[0, 0]), home_r.at[0])
                    wait_for(4 * size_of(fin.at[0, 0]), far_r.at[i * wide + j])
                flag = jnp.where(y == 0, expert[2 * d], expert[2 * d + 1]) == d
                for half_at in range(2):
                    for side in range(2):
                        at = (half_at, side, i, j)
                        target(side, i, half_at, j)[...] = pick(flag, home_in[at], far_in[at])

    def target(side, i, which, j):
        return out_ref.at[
            pl.ds(pl.multiple_of(side * core_rows + i * group_rows, group_rows), group_rows),
            pl.ds(pl.multiple_of(which * half + j * SPAN, SPAN), SPAN),
        ]

    def arrive(i, s, j, d):
        k = chunk(i, s, j)

        @pl.when(z == d)
        def _():
            with mark(f"arrive{k}"):
                got((up_in if d > 1 else dn_in).at[k, d], ret_r.at[d % 2, k])
            for n in range(2):
                b = 2 * d + n
                lower = up_in[k, d, n] if d > 1 else end_in[k][slot[b]]
                higher = dn_in[k, d, n] if d == 1 else end_in[k][slot[b]]
                value = pick(expert[b] < d, lower, mix[k][slot[b]])
                fin[k, n] = pick(expert[b] > d, higher, value)
            mine = target(c, i, y, j)
            device = dev_y if s == 0 else dev_yc
            push_plane(d, fin.at[k, yo], mine, last_r.at[0], device)
            if s == 0:
                mine[...] = fin[k, y]
            else:
                push_plane(d, fin.at[k, y], mine, last_r.at[0], dev_c)

    def arrive_middle(i, s, j):
        arrive(i, s, j, 1)
        arrive(i, s, j, 2)

    every = [(i, s, j) for i in range(GROUPS) for s, j in pieces]
    for g in parts_last[:3]:
        hide(g)
    down(0)
    hide(parts_last[3])
    down(1)
    down(2)
    stages = (
        (0, blend),
        (4, turn_in),
        (9, carry),
        (12, arrive_middle),
        (16, settle),
    )
    for n in range(len(every) + stages[-1][0]):
        if n == len(pieces):
            down(3)
        for lag, stage in stages:
            if 0 <= n - lag < len(every):
                stage(*every[n - lag])
    with mark("lastwait"):
        for i in range(GROUPS):
            for j in range(wide):
                final(i, j)

        @pl.when((z > 0) & (z < PLANES - 1))
        def _():
            wait_for(3 * size_of(out_ref) // 4, last_r.at[0])

    def all_sent(sem, amount):
        if amount:
            ref = w_buf.at[:, pl.ds(0, amount // (8 * units))]
            remote(ref, ref, sem, hid_r.at[0], dev_y).wait_send()

    with mark("drain"):
        for lot, amount in enumerate(all_lots):
            all_sent(sent.at[lot], amount)
        all_sent(sent.at[relay_lot], 2 * size_of(x_buf.at[0, 0, 0]))
        for plane in range(PLANES):

            @pl.when(z == plane)
            def _():
                for lot, amount in enumerate(plane_lots[plane]):
                    all_sent(plane_sent.at[lot], amount)


def local(
    queries, keys, values, residual_in, norm_gain, routing, gate_weight, up_weight, down_weight
):
    seq_count = lax.axis_size("seq")
    tp_count = lax.axis_size("tp")
    rows, width = queries.shape
    units = gate_weight.shape[2]
    planes = seq_count // 2
    fits = (
        tp_count == 4
        and seq_count == 2 * PLANES
        and rows == BLOCK
        and WINDOW == 4 * rows
        and units == 128
        and width == 8 * HEAD_DIM
    )
    if not fits:
        return local_general(
            queries,
            keys,
            values,
            residual_in,
            norm_gain,
            routing,
            gate_weight,
            up_weight,
            down_weight,
        )
    half = width // 2
    heads = half // HEAD_DIM
    most = min(2 * seq_count // planes, seq_count - planes + 1)
    core_rows = rows // 2
    group_rows = core_rows // GROUPS
    wide = half // SPAN
    chunks = GROUPS * 2 * wide
    vmem = pl.BlockSpec(memory_space=pltpu.VMEM)
    anywhere = pl.BlockSpec(memory_space=pltpu.MemorySpace.HBM)
    dma = pltpu.SemaphoreType.DMA

    def room(*shape, kind=BF16):
        return pltpu.VMEM(shape, kind)

    scratch = (
        room(4, heads, 2, 2, rows, HEAD_DIM),
        room(2, heads, 2, 2, rows, HEAD_DIM),
        room(2, heads, 2, rows, HEAD_DIM),
        [room(2 * planes, 2, core_rows, HEAD_DIM) for _ in range(heads)],
        room(2, tp_count, heads, GROUPS, most * group_rows, HEAD_DIM),
        room(heads, GROUPS, most * group_rows, HEAD_DIM),
        room(4, gate_weight.shape[1], units),
        room(2, down_weight.shape[1], width),
        room(GROUPS, most * group_rows, 4 * units, kind=F32),
        room(GROUPS, most * group_rows, 1, kind=F32),
        room(2, GROUPS, most * group_rows, 2 * units),
        room(chunks, most * group_rows, SPAN),
        room(chunks, most * group_rows, SPAN),
        room(chunks, most * group_rows, SPAN, kind=F32),
        [room(most, group_rows, SPAN) for _ in range(chunks)],
        [room(most, group_rows, SPAN) for _ in range(chunks)],
        room(chunks, planes, 2, group_rows, SPAN),
        room(chunks, planes, 2, group_rows, SPAN),
        room(chunks, planes, 2, group_rows, SPAN),
        room(chunks, planes, 2, group_rows, SPAN),
        room(chunks, 2, group_rows, SPAN),
        room(2, 2, GROUPS, wide, group_rows, SPAN),
        room(2, 2, GROUPS, wide, group_rows, SPAN),
        dma((1,)),
        dma((1,)),
        dma((1,)),
        dma((2, heads)),
        dma((2 * heads + 1,)),
        dma((planes, heads)),
        dma((3, heads + GROUPS - 1)),
        dma((1,)),
        dma((GROUPS,)),
        dma((chunks,)),
        dma((chunks,)),
        dma((2, chunks)),
        dma((1,)),
        dma((1,)),
        dma((GROUPS * wide,)),
        dma((3,)),
        dma((1,)),
    )
    flat, tree = jax.tree.flatten(scratch, is_leaf=lambda leaf: not isinstance(leaf, (list, tuple)))

    def kernel(*refs):
        layer_kernel(most, refs[:9], refs[9], jax.tree.unflatten(tree, refs[10:]))

    return pl.pallas_call(
        kernel,
        name="layer",
        out_shape=pltpu.VMEM((rows, width), BF16),
        in_specs=[pl.BlockSpec(memory_space=pltpu.SMEM)]
        + [anywhere] * 4
        + [vmem]
        + [anywhere] * 3,
        out_specs=vmem,
        scratch_shapes=flat,
        compiler_params=pltpu.CompilerParams(
            collective_id=0, has_side_effects=True, vmem_limit_bytes=67043328 - 2 * rows * width
        ),
    )(
        routing.reshape(-1),
        queries,
        keys,
        values,
        residual_in,
        norm_gain.reshape(1, -1),
        gate_weight,
        up_weight,
        down_weight,
    )


def solution(mesh):
    in_specs = (
        P("seq", "tp"),
        P("seq", "tp"),
        P("seq", "tp"),
        P("seq", "tp"),
        P(),
        P(),
        P("seq", None, "tp"),
        P("seq", None, "tp"),
        P("seq", None, "tp"),
    )
    out_specs = P("seq", "tp")
    return jax.shard_map(local, mesh=mesh, in_specs=in_specs, out_specs=out_specs, check_vma=False)
```
